128 devices in a mesh: scan: 16 (over x, z_hi, core), grp: 8 (over z_lo, y).
Axes of the slice: x: 4, y: 4, z: 4 (z_hi: 2, z_lo: 2; z = z_hi * 2 + z_lo), core: 2. Of those that a mesh axis runs over, the one named last changes fastest.
Arguments:
- frames: bfloat16 [256, 1024, 1024], P('scan', 'grp'), may hold values from -6 to 6
- dark_frame: int32 [36864], replicated, may hold values from 0 to 15
- gain_frame: int32 [36864], replicated, may hold values from 3072 to 5120
- bf_index: int32 [1024], replicated, may hold values from 0 to 36863
- row_level: float32 [256], P('scan'), may hold values from 0.5 to 2
- shift_num: int32 [2, 1024], P(None, ('scan', 'grp')), may hold values from -32 to 32
Outputs:
- upsampled: float32 [512, 2048], P(('scan', 'grp'))
- correlation: float32 [1024, 256], P(('scan', 'grp'))
The draws below stay inside these ranges and needn't reach their ends.
All inputs are finite; a program needn't handle non-finite values.
Results may differ from the reference program's by a relative error of at most 0.0085.
Values may be sent and summed in bfloat16 or wider, within the bound.
No kernel may reach another device: no remote copies, remote signals or barrier semaphores. Data moves between devices by JAX's collectives and lax.ppermute only.
A program may use at most 64 MiB of HBM per device.

```python
import math
import jax
import jax.numpy as jnp
from jax import lax

SY = 256
SX = 1024
BF = 1024
DET = 36864
LAGS = 16
DEN = 4


def set_ends(entries, own_key, least, top_value):
    shape = entries.shape
    spot = [jax.random.randint(jax.random.fold_in(own_key, axis), (), 0, shape[axis]) for axis in range(len(shape))]
    entries = entries.at[tuple(spot)].set(least)
    longest = shape.index(max(shape))
    spot[longest] = (spot[longest] + 1) % shape[longest]
    return entries.at[tuple(spot)].set(top_value)


def steps_of(rng, extent, split, low, top_value):
    loudness, own = 1.0, jax.random.fold_in(rng, 6)
    for position, blocks in split:
        draws = jnp.exp(jax.random.uniform(jax.random.fold_in(own, position), (blocks,), jnp.float32, low / len(split), top_value / len(split)))
        loudness = loudness * jnp.repeat(draws, extent[position] // blocks).reshape([-1 if axis == position else 1 for axis in range(len(extent))])
    return loudness


def bell_draw(own_key, extent, deviation, reach, pieces=(), kind=jnp.bfloat16):
    array = jax.random.normal(own_key, extent, jnp.float32) * deviation
    if len(pieces) > 0:
        array = steps_of(own_key, extent, pieces, -0.22, 0.18) * array
    return jnp.clip(array, min=-reach, max=reach).astype(kind)


def setup_inputs(seed: int = 0) -> dict:
    key_list = jax.random.split(jax.random.key(seed), 7)
    return {
        "frames": bell_draw(key_list[0], (SY, SX, BF), 1.0, 6.0, ((0, 16), (1, 8))),
        "dark_frame": set_ends(jax.random.randint(key_list[1], (DET,), 0, 16), jax.random.fold_in(key_list[1], 1), 0, 15).astype(jnp.int32),
        "gain_frame": set_ends(jax.random.randint(key_list[2], (DET,), 3072, 5121), jax.random.fold_in(key_list[2], 1), 3072, 5120).astype(jnp.int32),
        "bf_index": set_ends(jax.random.randint(key_list[3], (BF,), 0, DET), jax.random.fold_in(key_list[3], 1), 0, DET - 1).astype(jnp.int32),
        "row_level": jnp.clip(jnp.exp(math.log(2.0) - 1.3862944 * jax.random.uniform(key_list[4], (SY,), jnp.float32) ** steps_of(key_list[4], (SY,), ((0, 16),), -0.2, 0.2)), 0.5, 2.0),
        "shift_num": set_ends(jax.random.randint(key_list[5], (2, BF), -32, 33), jax.random.fold_in(key_list[5], 1), -32, 32).astype(jnp.int32),
    }


def signed_freq(length):
    indices = jnp.arange(length, dtype=jnp.int32)
    return jnp.where(indices < length // 2, indices, indices - length)

def phase_pair(leading, trailing, period):
    product = jnp.mod(leading[:, None] * trailing[None, :], period)
    angles = product.astype(jnp.float32) * (2.0 * math.pi / period)
    return (jnp.cos(angles), jnp.sin(angles))

def matmul(left, right):
    return jnp.dot(left.astype(jnp.float32), right.astype(jnp.float32), precision=lax.Precision.HIGHEST, preferred_element_type=jnp.float32)

def forward_pair(picture, cosine_cols, sine_cols, cosine_rows, sine_rows):
    real_rows = matmul(picture, cosine_cols).astype(jnp.bfloat16)
    imag_rows = (-matmul(picture, sine_cols)).astype(jnp.bfloat16)
    real_part = matmul(cosine_rows, real_rows) + matmul(sine_rows, imag_rows)
    imag_part = matmul(cosine_rows, imag_rows) - matmul(sine_rows, real_rows)
    anchor = (jnp.arange(real_part.shape[0])[:, None] == 0) & (jnp.arange(real_part.shape[1])[None, :] == 0)
    return (jnp.where(anchor, 0.0, real_part), jnp.where(anchor, 0.0, imag_part))

def axis_phase(length, amount):
    product = jnp.mod(signed_freq(length) * amount, DEN * length)
    angles = product.astype(jnp.float32) * (2.0 * math.pi / (DEN * length))
    return (jnp.cos(angles), jnp.sin(angles))

def shift_apply(real_part, imag_part, amounts):
    cosine_y, sine_y = axis_phase(real_part.shape[0], amounts[0])
    cosine_x, sine_x = axis_phase(real_part.shape[1], amounts[1])
    cos_phi = cosine_y[:, None] * cosine_x[None, :] - sine_y[:, None] * sine_x[None, :]
    sin_phi = sine_y[:, None] * cosine_x[None, :] + cosine_y[:, None] * sine_x[None, :]
    real_shift = (real_part * cos_phi + imag_part * sin_phi).astype(jnp.bfloat16)
    imag_shift = (imag_part * cos_phi - real_part * sin_phi).astype(jnp.bfloat16)
    return (real_shift, imag_shift)

def correlate(real_part, imag_part, ref_real, ref_imag, lag_tables, scale):
    lag_rows_cos, lag_rows_sin, lag_cols_cos, lag_cols_sin = lag_tables
    cross_real = (real_part * ref_real + imag_part * ref_imag).astype(jnp.bfloat16)
    cross_imag = (imag_part * ref_real - real_part * ref_imag).astype(jnp.bfloat16)
    half_real = matmul(lag_rows_cos, cross_real) - matmul(lag_rows_sin, cross_imag)
    half_imag = matmul(lag_rows_cos, cross_imag) + matmul(lag_rows_sin, cross_real)
    return ((matmul(half_real, lag_cols_cos) - matmul(half_imag, lag_cols_sin)) * scale).reshape(-1)

def reference(frames, dark_frame, gain_frame, bf_index, row_level, shift_num):
    rows, cols = (SY, SX)
    dark_pixel = dark_frame[bf_index].astype(jnp.float32) / 256.0
    gain_pixel = gain_frame[bf_index].astype(jnp.float32) / 4096.0
    corrected = (frames.astype(jnp.float32) - row_level[:, None, None] * dark_pixel) * gain_pixel
    ref_image = lax.optimization_barrier(jnp.sum(corrected, axis=2)).astype(jnp.bfloat16)
    pictures = jnp.transpose(corrected.astype(jnp.bfloat16), (2, 0, 1))
    del_rows = jnp.arange(rows, dtype=jnp.int32)
    col_range = jnp.arange(cols, dtype=jnp.int32)
    cosine_cols, sine_cols = phase_pair(col_range, col_range, cols)
    cosine_rows, sine_rows = phase_pair(del_rows, del_rows, rows)
    tables = tuple((t.astype(jnp.bfloat16) for t in (cosine_cols, sine_cols, cosine_rows, sine_rows)))
    up_rows_cos, up_rows_sin = phase_pair(jnp.arange(2 * rows, dtype=jnp.int32), signed_freq(rows), 2 * rows)
    up_rows_cos, up_rows_sin = (up_rows_cos.astype(jnp.bfloat16), up_rows_sin.astype(jnp.bfloat16))
    up_cols_cos, up_cols_sin = phase_pair(signed_freq(cols), jnp.arange(2 * cols, dtype=jnp.int32), 2 * cols)
    up_cols_cos, up_cols_sin = (up_cols_cos.astype(jnp.bfloat16), up_cols_sin.astype(jnp.bfloat16))
    lag_values = jnp.arange(LAGS, dtype=jnp.int32) - LAGS // 2
    lag_rows_cos, lag_rows_sin = phase_pair(lag_values, del_rows, rows)
    lag_rows_cos, lag_rows_sin = (lag_rows_cos.astype(jnp.bfloat16), lag_rows_sin.astype(jnp.bfloat16))
    lag_cols_cos, lag_cols_sin = phase_pair(col_range, lag_values, cols)
    lag_tables = (lag_rows_cos, lag_rows_sin, lag_cols_cos, lag_cols_sin)
    corr_scale = 1.0 / (rows * cols * math.sqrt(BF * rows * cols))
    ref_real, ref_imag = forward_pair(ref_image, *tables)

    def visit(totals, element):
        picture, amounts = element
        real_part, imag_part = forward_pair(picture, *tables)
        correl = correlate(real_part, imag_part, ref_real, ref_imag, lag_tables, corr_scale)
        real_shift, imag_shift = shift_apply(real_part, imag_part, amounts)
        total_real = totals[0] + matmul(up_rows_cos, real_shift) - matmul(up_rows_sin, imag_shift)
        total_imag = totals[1] + matmul(up_rows_cos, imag_shift) + matmul(up_rows_sin, real_shift)
        return ((total_real, total_imag), correl)
    start_totals = (jnp.zeros((2 * rows, cols), jnp.float32), jnp.zeros((2 * rows, cols), jnp.float32))
    totals, correls = lax.scan(visit, start_totals, (pictures, shift_num.T))
    rows_real = totals[0].astype(jnp.bfloat16)
    rows_imag = totals[1].astype(jnp.bfloat16)
    upsampled = (matmul(rows_real, up_cols_cos) - matmul(rows_imag, up_cols_sin)) * (1.0 / (rows * cols * math.sqrt(BF)))
    return (upsampled, correls)
```

```python
import math

import jax
import jax.numpy as jnp
import ml_dtypes
import numpy as np
from jax import lax
from jax.experimental import pallas as pl
from jax.experimental.pallas import tpu as pltpu
from jax.sharding import PartitionSpec as P

SY = 256
SX = 1024
BF = 1024
DET = 36864
AXES = ("scan", "grp")
S = 16
G = 8
N = S * G
YS = SY // S
XS = SX // G
ROWS = DET // 128
BX = 17
F32 = jnp.float32
BF16 = jnp.bfloat16
NT = (((1,), (1,)), ((), ()))
TN = (((0,), (0,)), ((), ()))
VMEM_LIMIT = 56 * 1024 * 1024


def row_kernel():
    k = np.arange(-128, 128)
    q = np.arange(1024)
    d = np.cos(2 * np.pi * k[None, :] * q[:, None] / 1024).sum(1) / 256
    yp = np.arange(1024) % 512
    yy = np.repeat(np.arange(32), 4)
    fy = np.tile(np.arange(4), 32)
    return d[(2 * yp[:, None] - fy[None, :] - 4 * (yy[None, :] - 8)) % 1024].astype(ml_dtypes.bfloat16)


def col_tables():
    x = np.arange(512) - 8
    out = []
    for par in (0, 1):
        k = 2 * np.arange(256) + par
        ang = 2 * np.pi * ((x[:, None] * k[None, :]) % 1024) / 1024
        c, s = np.cos(ang), np.sin(ang)
        if par == 0:
            s[:, 0] = np.where(x % 2 == 0, 1.0, -1.0)
        out.append(np.concatenate([c, s], 1).astype(ml_dtypes.bfloat16))
    xp = np.arange(1024)
    for par in (0, 1):
        k = 2 * np.arange(256) + par
        w = np.where(k == 0, 1.0, 2.0)[:, None]
        ang = 2 * np.pi * ((k[:, None] * xp[None, :]) % 2048) / 2048
        out.append(np.concatenate([w * np.cos(ang), -w * np.sin(ang)], 0).astype(ml_dtypes.bfloat16))
    phase = np.zeros((16, 256), np.float32)
    for par in (0, 1):
        k = 2 * np.arange(256) + par
        for fx in range(4):
            phase[par * 8 + fx] = np.cos(2 * np.pi * k * fx / 4096)
            phase[par * 8 + 4 + fx] = np.sin(2 * np.pi * k * fx / 4096)
    return (*out, phase)


def nyquist_tables():
    w = np.zeros((16, 128), np.float32)
    for yp in range(4):
        for fx in range(4):
            for fy in range(4):
                sy = math.sin(math.pi * (2 * yp - fy) / 4) / 256
                for base in (64, 80):
                    w[yp, base + fx * 4 + fy] = sy * math.sin(math.pi * fx / 4)
                    w[8 + yp, base + fx * 4 + fy] = -sy * math.cos(math.pi * fx / 4)
    return w


def correct_kernel(level, frames, dark, gain, index, v_out, r_out, dark_px, gain_px):
    y = pl.program_id(0)

    @pl.when(y == 0)
    def _():
        g = gain[...]
        table = jnp.concatenate(
            [dark[...].astype(F32), (g >> 5).astype(F32), (g & 31).astype(F32)], axis=1
        ).astype(BF16)
        idx = index[...]
        hot = (lax.broadcasted_iota(jnp.int32, (ROWS, BF), 0) == (idx >> 7)).astype(F32).astype(BF16)
        picked = lax.dot_general(table, hot, TN, preferred_element_type=F32)
        mine = lax.broadcasted_iota(jnp.int32, (128, BF), 0) == (idx & 127)

        def pick(i):
            return jnp.sum(jnp.where(mine, picked[128 * i : 128 * (i + 1)], 0.0), axis=0, keepdims=True)

        dark_px[...] = pick(0) * (1.0 / 256.0)
        gain_px[...] = (pick(1) * 32.0 + pick(2)) * (1.0 / 4096.0)

    value = (frames[0].astype(F32) - level[y] * dark_px[...]) * gain_px[...]
    value = value.astype(BF16)
    v_out[0] = value
    total = lax.dot_general(jnp.ones((8, BF), BF16), value, NT, preferred_element_type=F32)
    r_out[pl.ds(y, 1), :] = total[0:1]


def shift_kernel(strip, shifts, v, rows, z_out, moved, hot, main, over):
    for t in range(8):
        lanes = slice(128 * t, 128 * (t + 1))
        sy = shifts[t, 0:1, :]
        sx = shifts[t, 1:2, :]
        by = (sy >> 2) + 8
        code = ((sx >> 2) + 8) * 16 + (sx & 3) * 4 + (sy & 3)
        hot[:, lanes] = (
            (lax.broadcasted_iota(jnp.int32, (BX * 16, 128), 0) == code).astype(F32).astype(BF16)
        )
        masks = [
            jnp.broadcast_to(((by >> b) & 1).astype(F32), (16, 128)).astype(BF16) > 0.5 for b in range(5)
        ]

        def barrel(i, _, lanes=lanes, masks=masks):
            x0 = pl.multiple_of(i * 16, 16)
            rows_in = [v[y, pl.ds(x0, 16), lanes] for y in range(YS)]
            zero = jnp.zeros((16, 128), BF16)
            for b in range(5):
                step = 1 << b
                size = min(len(rows_in) + step, 32)
                old = rows_in
                rows_in = [
                    jnp.where(
                        masks[b],
                        old[j - step] if 0 <= j - step < len(old) else zero,
                        old[j] if j < len(old) else zero,
                    )
                    for j in range(size)
                ]
            for j in range(32):
                moved[j, pl.ds(x0, 16), lanes] = rows_in[j]
            return 0

        lax.fori_loop(0, 8, barrel, 0)

    lane = lax.broadcasted_iota(jnp.int32, (16, 128), 1)

    def group(j, _):
        block = moved[pl.ds(2 * j, 2)].reshape(256, BF)
        sums = lax.dot_general(hot[...], block, NT, preferred_element_type=F32)
        for h in range(2):
            acc_main = sums[0:16, 128 * h : 128 * (h + 1)]
            acc_over = jnp.zeros((16, 128), F32)
            for b in range(1, BX):
                piece = pltpu.roll(sums[16 * b : 16 * (b + 1), 128 * h : 128 * (h + 1)], b, 1)
                acc_main = acc_main + jnp.where(lane >= b, piece, 0.0)
                acc_over = acc_over + jnp.where(lane < b, piece, 0.0)
            main[2 * j + h] = acc_main
            over[2 * j + h] = acc_over
        return 0

    lax.fori_loop(0, 16, group, 0)

    sign_y = 1.0 - 2.0 * (lax.broadcasted_iota(jnp.int32, (32, 16, 128), 0) & 1).astype(F32)
    sign_x = 1.0 - 2.0 * (lax.broadcasted_iota(jnp.int32, (8, 128), 1) & 1).astype(F32)
    folded = jnp.sum((main[...] + over[...]) * sign_y, axis=0)
    folded = jnp.concatenate([jnp.zeros((64, 128), F32), folded, jnp.zeros((48, 128), F32)], axis=0)
    q_row = lax.dot_general(sign_x, folded, NT, precision=lax.Precision.HIGHEST, preferred_element_type=F32)[0:1]
    q_high = q_row.astype(BF16).astype(F32)
    q_row = q_high + pltpu.roll(q_row - q_high, 16, 1)

    spread = (
        (lax.broadcasted_iota(jnp.int32, (128, 512), 0) >> 2)
        == (lax.broadcasted_iota(jnp.int32, (128, 512), 1) >> 4)
    ) & (
        (lax.broadcasted_iota(jnp.int32, (128, 512), 0) & 3)
        == (lax.broadcasted_iota(jnp.int32, (128, 512), 1) & 3)
    )
    start = pl.multiple_of(512 - 32 * strip[0], 32)
    left = jnp.dot(
        rows[pl.ds(start, 512), :], spread.astype(F32).astype(BF16), preferred_element_type=F32
    ).astype(BF16)
    kind = (lax.broadcasted_iota(jnp.int32, (512, 128), 0) >> 2) & 3
    u_main = main[...].reshape(512, 128)
    u_over = over[...].reshape(512, 128)
    tail = jnp.zeros((512, 128), F32)
    for fx in range(4):
        part = jnp.where(kind == fx, u_main, 0.0).astype(BF16)
        z_out[:, 128 * fx : 128 * (fx + 1)] = jnp.dot(left, part, preferred_element_type=F32).astype(BF16)
        piece = jnp.where(kind == fx, u_over, 0.0)
        tail = tail + (pltpu.roll(piece, 16 * fx, 1) if fx else piece)
    z_out[:, 512:640] = (jnp.dot(left, tail.astype(BF16), preferred_element_type=F32) + q_row).astype(BF16)


def correlate_kernel(place, v, r_all, c_out, total_out, window, table):
    s = place[0]
    g = place[1]
    whole = r_all[...].astype(F32)
    total = jnp.sum(jnp.sum(whole, axis=0), keepdims=True)
    mean = total * (1.0 / (SY * SX))
    rest = jnp.sum(jnp.sum((whole - mean).astype(BF16).astype(F32), axis=0), keepdims=True) * (1.0 / (SY * SX))
    total_out[...] = jnp.broadcast_to(total, (8, 128))
    for dg in range(3):
        gg = lax.rem(g + (dg + G - 1), G)
        above = r_all[lax.rem(s + (S - 1), S) * G + gg].astype(F32)
        here = r_all[s * G + gg].astype(F32)
        below = r_all[lax.rem(s + 1, S) * G + gg].astype(F32)
        window[0:8, 128 * dg : 128 * (dg + 1)] = above[8:16] - mean
        window[8:24, 128 * dg : 128 * (dg + 1)] = here - mean
        window[24:32, 128 * dg : 128 * (dg + 1)] = below[0:8] - mean
    for b in range(16):
        moved = pltpu.roll(window[...], (b - 8) % 384, 1)[:, 128:256]
        for yy in range(32):
            table[31 - yy, b : b + 1, :] = moved[yy : yy + 1]
    acc = jnp.zeros((256, BF), F32)
    sums = jnp.zeros((8, BF), F32)
    for j in range(0, YS, 2):
        left = jnp.concatenate(
            [table[15 - i : 31 - i].reshape(256, 128).astype(BF16) for i in (j, j + 1)], axis=1
        )
        right = v[j : j + 2].reshape(256, BF)
        acc = acc + jnp.dot(left, right, preferred_element_type=F32)
        sums = sums + jnp.dot(jnp.ones((8, 256), BF16), right, preferred_element_type=F32)
    acc = acc - rest * sums[0:1]
    c_out[...] = acc.T.astype(BF16)


def finish_kernel(zs, total, t1e, t1o, t2e, t2o, phase, nyquist, out, full):
    full[...] = jnp.zeros((32, SX), F32)
    for g in range(G):
        for fx in range(4):
            full[8 * fx : 8 * fx + 4, 128 * g : 128 * (g + 1)] = zs[g, :, 128 * fx : 128 * (fx + 1)]
    lane = lax.broadcasted_iota(jnp.int32, (4, 128), 1)
    q_rows = jnp.zeros((4, 128), F32)
    for g in range(G):
        nxt = (g + 1) % G
        tail = zs[g, :, 512:640]
        q_rows = q_rows + tail
        for fx in range(4):
            piece = pltpu.roll(tail, (128 - 16 * fx) % 128, 1) if fx else tail
            full[8 * fx : 8 * fx + 4, 128 * nxt : 128 * (nxt + 1)] += jnp.where(lane < 16, piece, 0.0)
    low = full[:, 0:512]
    high = full[:, 512:1024]
    lane_e = lax.broadcasted_iota(jnp.int32, (8, 256), 1)
    results = []
    for par, (t1, t2, part) in enumerate(((t1e, t2e, low + high), (t1o, t2o, low - high))):
        spec = jnp.dot(part.astype(BF16), t1[...], preferred_element_type=F32)
        re = jnp.zeros((8, 256), F32)
        im = jnp.zeros((8, 256), F32)
        for fx in range(4):
            c = spec[8 * fx : 8 * fx + 8, 0:256]
            s = spec[8 * fx : 8 * fx + 8, 256:512]
            if par == 0:
                ny = s[:, 0:1]
                if fx == 0:
                    ny_cos = ny
                    ny_sin = jnp.zeros_like(ny)
                else:
                    ny_cos = ny_cos + ny * math.cos(math.pi * fx / 4)
                    ny_sin = ny_sin + ny * math.sin(math.pi * fx / 4)
                s = jnp.where(lane_e == 0, 0.0, s)
            pc = phase[8 * par + fx : 8 * par + fx + 1, :]
            ps = phase[8 * par + 4 + fx : 8 * par + 5 + fx, :]
            re = re + c * pc - s * ps
            im = im - (s * pc + c * ps)
        if par == 0:
            re = jnp.where(lane_e == 0, re - total[0:1, 0:1] * (1.0 / SY), re)
        coef = jnp.concatenate([re, im], axis=1).astype(BF16)
        results.append(jnp.dot(coef, t2[...], preferred_element_type=F32))
    q_cos = jnp.sum(q_rows * nyquist[0:4, :], axis=1, keepdims=True)
    q_sin = jnp.sum(q_rows * nyquist[8:12, :], axis=1, keepdims=True)
    place = lax.broadcasted_iota(jnp.int32, (4, 1024), 1) & 3
    wave_cos = jnp.where(place == 0, 1.0, jnp.where(place == 2, -1.0, 0.0))
    wave_sin = jnp.where(place == 1, 1.0, jnp.where(place == 3, -1.0, 0.0))
    wave = (ny_cos[0:4] + q_cos) * wave_cos + (ny_sin[0:4] + q_sin) * wave_sin
    scale = 1.0 / (SX * math.sqrt(BF))
    even = results[0][0:4] + wave
    odd = results[1][0:4]
    out[:, 0:1024] = (even + odd) * scale
    out[:, 1024:2048] = (even - odd) * scale


def exchange(value):
    return lax.all_to_all(value, AXES, split_axis=0, concat_axis=0, tiled=True)


def local(frames, dark_frame, gain_frame, bf_index, row_level, shift_num):
    s = lax.axis_index("scan")
    g = lax.axis_index("grp")
    place = jnp.stack([s, g]).astype(jnp.int32)
    smem = pl.BlockSpec(memory_space=pltpu.SMEM)
    vmem = pl.BlockSpec(memory_space=pltpu.VMEM)
    params = pltpu.CompilerParams(vmem_limit_bytes=VMEM_LIMIT)

    slot = (s * G + g) % 16
    spread = jnp.tile(shift_num, (1, 16))
    spread = jnp.where(jnp.arange(128) // 8 == slot, spread, 0)
    shifts = exchange(jnp.broadcast_to(spread[None], (N, 2, 128)))
    shifts = shifts.reshape(8, 16, 2, 128).sum(axis=1)

    v, r = pl.pallas_call(
        correct_kernel,
        grid=(YS,),
        in_specs=[
            smem,
            pl.BlockSpec((1, XS, BF), lambda i: (i, 0, 0)),
            pl.BlockSpec((ROWS, 128), lambda i: (0, 0)),
            pl.BlockSpec((ROWS, 128), lambda i: (0, 0)),
            pl.BlockSpec((1, BF), lambda i: (0, 0)),
        ],
        out_specs=[
            pl.BlockSpec((1, XS, BF), lambda i: (i, 0, 0)),
            pl.BlockSpec((YS, XS), lambda i: (0, 0)),
        ],
        out_shape=[
            jax.ShapeDtypeStruct((YS, XS, BF), BF16),
            jax.ShapeDtypeStruct((YS, XS), F32),
        ],
        scratch_shapes=[pltpu.VMEM((1, BF), F32), pltpu.VMEM((1, BF), F32)],
        compiler_params=params,
        name="correct",
    )(
        row_level,
        frames,
        dark_frame.reshape(ROWS, 128),
        gain_frame.reshape(ROWS, 128),
        bf_index.reshape(1, BF),
    )
    r_all = exchange(jnp.broadcast_to(r.astype(BF16)[None], (N, YS, XS)))

    z = pl.pallas_call(
        shift_kernel,
        in_specs=[smem, vmem, vmem, vmem],
        out_specs=vmem,
        out_shape=jax.ShapeDtypeStruct((2 * SY, 640), BF16),
        scratch_shapes=[
            pltpu.VMEM((32, XS, BF), BF16),
            pltpu.VMEM((BX * 16, BF), BF16),
            pltpu.VMEM((32, 16, 128), F32),
            pltpu.VMEM((32, 16, 128), F32),
        ],
        compiler_params=params,
        name="shift",
    )(place, shifts, v, jnp.asarray(row_kernel()))
    z_all = exchange(z.reshape(N, 4, 640))

    c, total = pl.pallas_call(
        correlate_kernel,
        in_specs=[smem, vmem, vmem],
        out_specs=[vmem, vmem],
        out_shape=[
            jax.ShapeDtypeStruct((BF, 256), BF16),
            jax.ShapeDtypeStruct((8, 128), F32),
        ],
        scratch_shapes=[pltpu.VMEM((32, 384), F32), pltpu.VMEM((32, 16, 128), F32)],
        compiler_params=params,
        name="correlate",
    )(place, v, r_all)
    c_all = exchange(c.reshape(N, 8, 256))

    z_sum = z_all.reshape(S, G, 4, 640).astype(F32).sum(axis=0)
    tables = tuple(jnp.asarray(t) for t in col_tables())
    upsampled = pl.pallas_call(
        finish_kernel,
        in_specs=[vmem] * 8,
        out_specs=vmem,
        out_shape=jax.ShapeDtypeStruct((4, 2 * SX), F32),
        scratch_shapes=[pltpu.VMEM((32, SX), F32)],
        compiler_params=params,
        name="finish",
    )(z_sum, total, *tables, jnp.asarray(nyquist_tables()))
    correlation = c_all.astype(F32).sum(axis=0) * (1.0 / math.sqrt(BF * SY * SX))
    return (upsampled, correlation)


def solution(mesh):
    return jax.shard_map(
        local,
        mesh=mesh,
        in_specs=(P("scan", "grp", None), P(), P(), P(), P("scan"), P(None, AXES)),
        out_specs=(P(AXES, None), P(AXES, None)),
        check_vma=False,
    )
```

```python
import math

import jax
import jax.numpy as jnp
import ml_dtypes
import numpy as np
from jax import lax
from jax.experimental import pallas as pl
from jax.experimental.pallas import tpu as pltpu
from jax.sharding import PartitionSpec as P

SY = 256
SX = 1024
BF = 1024
DET = 36864
AXES = ("scan", "grp")
S = 16
G = 8
N = S * G
YS = SY // S
XS = SX // G
ROWS = DET // 128
BX = 17
PARTS = 4
F32 = jnp.float32
BF16 = jnp.bfloat16
NT = (((1,), (1,)), ((), ()))
TN = (((0,), (0,)), ((), ()))
MIB = 1024 * 1024


def iota(shape, dim):
    return lax.broadcasted_iota(jnp.int32, shape, dim)


def row_kernel():
    k = np.arange(-128, 128)
    q = np.arange(1024)
    d = np.cos(2 * np.pi * k[None, :] * q[:, None] / 1024).sum(1) / 256
    r = np.arange(2048) % 1024
    yp = 4 * (r // 8) + r % 4
    yy = np.repeat(np.arange(32), 4)
    fy = np.tile(np.arange(4), 32)
    return d[(2 * yp[:, None] - fy[None, :] - 4 * (yy[None, :] - 8)) % 1024].astype(ml_dtypes.bfloat16)


def col_tables():
    x = np.arange(512) - 8
    out = []
    for par in (0, 1):
        k = 2 * np.arange(256) + par
        ang = 2 * np.pi * ((x[:, None] * k[None, :]) % 1024) / 1024
        c, s = np.cos(ang), np.sin(ang)
        if par == 0:
            s[:, 0] = np.where(x % 2 == 0, 1.0, -1.0)
        out.append(np.concatenate([c, s], 1).astype(ml_dtypes.bfloat16))
    xp = np.arange(1024)
    for par in (0, 1):
        k = 2 * np.arange(256) + par
        w = np.where(k == 0, 1.0, 2.0)[:, None]
        ang = 2 * np.pi * ((k[:, None] * xp[None, :]) % 2048) / 2048
        out.append(np.concatenate([w * np.cos(ang), -w * np.sin(ang)], 0).astype(ml_dtypes.bfloat16))
    return out


def phase_tables():
    out = np.zeros((2, 2, 2, 8, 256), np.float32)
    for par in (0, 1):
        k = 2 * np.arange(256) + par
        for fx in range(4):
            rows = slice(4 * (fx >> 1), 4 * (fx >> 1) + 4)
            out[par, 0, fx & 1, rows] = np.cos(2 * np.pi * k * fx / 4096)
            out[par, 1, fx & 1, rows] = np.sin(2 * np.pi * k * fx / 4096)
    return out.reshape(64, 256)


def nyquist_tables():
    w = np.zeros((2, 8, 128), np.float32)
    for i in range(8):
        for fx in range(4):
            for fy in range(4):
                sy = math.sin(math.pi * (2 * (i % 4) - fy) / 4) / 256
                for base in (64, 80):
                    w[0, i, base + fx * 4 + fy] = sy * math.sin(math.pi * fx / 4)
                    w[1, i, base + fx * 4 + fy] = -sy * math.cos(math.pi * fx / 4)
    v = np.zeros((2, 2, 8, 128), np.float32)
    for fx in range(4):
        rows = slice(4 * (fx >> 1), 4 * (fx >> 1) + 4)
        v[fx & 1, 0, rows] = math.cos(math.pi * fx / 4)
        v[fx & 1, 1, rows] = math.sin(math.pi * fx / 4)
    return np.concatenate([w.reshape(16, 128), v.reshape(32, 128)], 0)


def three_parts(value):
    high = value.astype(BF16).astype(F32)
    mid = (value - high).astype(BF16).astype(F32)
    return high, mid, value - high - mid


def reference_kernel(place, level, amounts, frames, dark, gain, index, send, r_out, pixel_out, held, sems):
    def part(i):
        span = pl.ds(i * (YS // PARTS), YS // PARTS)
        return pltpu.make_async_copy(frames.at[span], held.at[span], sems.at[i])

    for i in range(PARTS):
        part(i).start()
    g = gain[...]
    table = jnp.concatenate(
        [dark[...].astype(F32), (g >> 5).astype(F32), (g & 31).astype(F32)], axis=1
    ).astype(BF16)
    idx = index[...]
    hot = (iota((ROWS, BF), 0) == (idx >> 7)).astype(F32).astype(BF16)
    picked = lax.dot_general(table, hot, TN, preferred_element_type=F32)
    mine = iota((128, BF), 0) == (idx & 127)

    def pick(i):
        return jnp.sum(jnp.where(mine, picked[128 * i : 128 * (i + 1)], 0.0), axis=0, keepdims=True)

    dark_px = pick(0) * (1.0 / 256.0)
    gain_px = (pick(1) * 32.0 + pick(2)) * (1.0 / 4096.0)
    pixel_out[0:1, :] = dark_px
    pixel_out[1:2, :] = gain_px
    offset = jnp.sum(dark_px * gain_px)
    for i in range(PARTS):
        part(i).wait()
        for y in range(i * (YS // PARTS), (i + 1) * (YS // PARTS)):
            acc = None
            for t in range(8):
                lanes = slice(128 * t, 128 * (t + 1))
                term = held[y, :, lanes].astype(F32) * gain_px[:, lanes]
                acc = term if acc is None else acc + term
            high = acc.astype(BF16)
            low = (acc - high.astype(F32)).astype(BF16)
            total = lax.dot_general(
                jnp.ones((8, 256), BF16), jnp.concatenate([high, low], 1), NT, preferred_element_type=F32
            )
            r_out[y : y + 1, :] = total[0:1] - level[y] * offset
    s = place[0]
    g = place[1]
    r = r_out[...]
    center = jnp.sum(r) * (1.0 / (YS * XS))
    rest = r - center
    lane = iota((1, 128), 1)
    base = 8 * lax.rem(s * G + g, 16)
    row_sy = jnp.zeros((1, 128), F32)
    row_sx = jnp.zeros((1, 128), F32)
    for i in range(8):
        row_sy = jnp.where(lane == base + i, amounts[0, i].astype(F32), row_sy)
        row_sx = jnp.where(lane == base + i, amounts[1, i].astype(F32), row_sx)
    row_center = jnp.zeros((1, 128), F32)
    for i, piece in enumerate(three_parts(jnp.full((1, 128), center))):
        row_center = jnp.where(lane == i, piece, row_center)
    foot = jnp.concatenate([row_sy, row_sx, row_center, jnp.zeros((5, 128), F32)], axis=0)

    def chunk(top):
        return jnp.concatenate([top, foot], axis=0).astype(BF16)

    plain = chunk(jnp.zeros((8, 128), F32))
    for d in range(N):
        send[d] = plain
    lanes = iota((8, 128), 1)
    sides = jnp.where((lanes >= 32) & (lanes < 96), pltpu.roll(rest[8:16], 64, 1), rest[0:8])
    for ds, top in ((S - 1, rest[0:8]), (0, sides), (1, rest[8:16])):
        for dg in (G - 1, 0, 1):
            if ds or dg:
                send[lax.rem(s + ds, S) * G + lax.rem(g + dg, G)] = chunk(top)


def correct_kernel(level, frames, pixel, v_out):
    y = pl.program_id(0) * (YS // PARTS)
    for i in range(YS // PARTS):
        value = (frames[i].astype(F32) - level[y + i] * pixel[0:1, :]) * pixel[1:2, :]
        v_out[i] = value.astype(BF16)


def strip_kernel(
    place, recv, r_own, v_hbm, rows, out, total_out, v, moved, hot, main, over, window, table, sems
):
    s = place[0]
    g = place[1]

    def part(i):
        span = pl.ds(i * (YS // PARTS), YS // PARTS)
        return pltpu.make_async_copy(v_hbm.at[span], v.at[span], sems.at[i])

    for i in range(PARTS):
        part(i).start()

    centers = jnp.zeros((8, 128), F32)
    feet = []
    for t in range(8):
        foot = jnp.zeros((8, 128), F32)
        for i in range(16):
            foot = foot + recv[16 * t + i].astype(F32)[8:16]
        feet.append(foot)
        centers = centers + foot
    mean = jnp.sum(jnp.where(iota((1, 128), 1) < 3, centers[2:3], 0.0), axis=1, keepdims=True) * (1.0 / N)
    total_out[...] = jnp.broadcast_to(mean * (SY * SX), (8, 128))

    def neighbour(ds, dg):
        got = recv[lax.rem(s + ds, S) * G + lax.rem(g + dg, G)].astype(F32)
        center = jnp.sum(jnp.where(iota((1, 128), 1) < 3, got[10:11], 0.0), axis=1, keepdims=True)
        return got[0:8] + (center - mean)

    for j, dg in enumerate((G - 1, 0, 1)):
        lanes = slice(128 * j, 128 * (j + 1))
        window[0:8, lanes] = neighbour(S - 1, dg)
        window[24:32, lanes] = neighbour(1, dg)
        if dg:
            side = neighbour(0, dg)
            window[8:16, lanes] = side
            window[16:24, lanes] = pltpu.roll(side, 64, 1)
        else:
            window[8:24, lanes] = r_own[...] - mean
    for b in range(16):
        table[b] = pltpu.roll(window[...], (b - 8) % 384, 1)[:, 128:256]

    row = iota((BX * 16, 128), 0)
    for t in range(8):
        sy = feet[t][0:1].astype(jnp.int32)
        sx = feet[t][1:2].astype(jnp.int32)
        code = ((sx >> 2) + 8) * 16 + (sx & 3) * 4 + (sy & 3)
        hot[:, 128 * t : 128 * (t + 1)] = (row == code).astype(F32).astype(BF16)

    for i in range(PARTS):
        part(i).wait()

    acc = jnp.zeros((256, BF), F32)
    for j in range(0, YS, 2):
        left = jnp.concatenate(
            [
                jnp.concatenate([table[b, i + 1 : i + 17, :] for b in range(16)], axis=0).astype(BF16)
                for i in (j, j + 1)
            ],
            axis=1,
        )
        acc = acc + jnp.dot(left, v[j : j + 2].reshape(256, BF), preferred_element_type=F32)
    out[:, 384:640] = acc.T.astype(BF16)

    for t in range(8):
        lanes = slice(128 * t, 128 * (t + 1))
        by = (feet[t][0:1].astype(jnp.int32) >> 2) + 8
        masks = [
            jnp.broadcast_to(((by >> b) & 1).astype(F32), (16, 128)).astype(BF16) > 0.5 for b in range(5)
        ]

        def barrel(i, _, lanes=lanes, masks=masks):
            x0 = pl.multiple_of(i * 16, 16)
            rows_in = [v[y, pl.ds(x0, 16), lanes] for y in range(YS)]
            zero = jnp.zeros((16, 128), BF16)
            for b in range(5):
                step = 1 << b
                size = min(len(rows_in) + step, 32)
                old = rows_in
                rows_in = [
                    jnp.where(
                        masks[b],
                        old[j - step] if 0 <= j - step < len(old) else zero,
                        old[j] if j < len(old) else zero,
                    )
                    for j in range(size)
                ]
            for j in range(32):
                moved[j, pl.ds(x0, 16), lanes] = rows_in[j]
            return 0

        lax.fori_loop(0, 8, barrel, 0)

    lane = iota((16, 128), 1)

    def group(j, _):
        block = moved[pl.ds(2 * j, 2)].reshape(256, BF)
        sums = lax.dot_general(hot[...], block, NT, preferred_element_type=F32)
        for h in range(2):
            acc_main = sums[0:16, 128 * h : 128 * (h + 1)]
            acc_over = jnp.zeros((16, 128), F32)
            for b in range(1, BX):
                piece = pltpu.roll(sums[16 * b : 16 * (b + 1), 128 * h : 128 * (h + 1)], b, 1)
                acc_main = acc_main + jnp.where(lane >= b, piece, 0.0)
                acc_over = acc_over + jnp.where(lane < b, piece, 0.0)
            main[2 * j + h] = acc_main
            over[2 * j + h] = acc_over
        return 0

    lax.fori_loop(0, 16, group, 0)

    sign_y = 1.0 - 2.0 * (iota((32, 16, 128), 0) & 1).astype(F32)
    sign_x = 1.0 - 2.0 * (iota((8, 128), 1) & 1).astype(F32)
    folded = jnp.sum((main[...] + over[...]) * sign_y, axis=0)
    folded = jnp.concatenate([jnp.zeros((64, 128), F32), folded, jnp.zeros((48, 128), F32)], axis=0)
    q_row = lax.dot_general(sign_x, folded, NT, precision=lax.Precision.HIGHEST, preferred_element_type=F32)[0:1]
    q_high = q_row.astype(BF16).astype(F32)
    q_row = q_high + pltpu.roll(q_row - q_high, 16, 1)

    col = iota((128, 512), 1)
    spread = ((iota((128, 512), 0) >> 2) == (col >> 4)) & ((iota((128, 512), 0) & 3) == (col & 3))
    start = pl.multiple_of(1024 - 64 * s, 64)
    left = jnp.dot(rows[pl.ds(start, 1024), :], spread.astype(F32).astype(BF16), preferred_element_type=F32)
    left = jnp.where(
        ((iota((1024, 512), 0) >> 2) & 1) == ((iota((1024, 512), 1) >> 3) & 1), left, 0.0
    ).astype(BF16)
    kind = (iota((512, 128), 0) >> 2) & 1
    u_main = main[...].reshape(512, 128)
    u_over = over[...].reshape(512, 128)
    first = jnp.where(kind == 0, u_over, 0.0)
    second = jnp.where(kind == 1, u_over, 0.0)
    right = jnp.concatenate(
        [
            jnp.where(kind == 0, u_main, 0.0),
            jnp.where(kind == 1, u_main, 0.0),
            first + pltpu.roll(second, 16, 1),
        ],
        axis=1,
    ).astype(BF16)
    z = jnp.dot(left, right, preferred_element_type=F32)
    out[:, 0:256] = z[:, 0:256].astype(BF16)
    out[:, 256:384] = (z[:, 256:384] + q_row).astype(BF16)


def finish_kernel(recv, total, t1e, t1o, t2e, t2o, phase, nyquist, out, corr_out, full):
    corr = jnp.zeros((8, 256), F32)
    sums = []
    for g in range(G):
        acc = jnp.zeros((8, 384), F32)
        for s in range(S):
            got = recv[s * G + g].astype(F32)
            acc = acc + got[:, 0:384]
            corr = corr + got[:, 384:640]
        sums.append(acc)
    n = iota((256, 256), 0)
    m = iota((256, 256), 1)
    order = ((n >> 4) == (m & 15)) & ((15 - (n & 15)) == (m >> 4))
    corr_out[...] = jnp.dot(
        corr * (1.0 / math.sqrt(BF * SY * SX)),
        order.astype(F32),
        precision=lax.Precision.HIGHEST,
        preferred_element_type=F32,
    )
    lane = iota((8, 128), 1)
    q_rows = jnp.zeros((8, 128), F32)
    for g in range(G):
        tail = sums[(g - 1) % G][:, 256:384]
        q_rows = q_rows + tail
        lanes = slice(128 * g, 128 * (g + 1))
        full[0:8, lanes] = sums[g][:, 0:128] + jnp.where(lane < 16, tail, 0.0)
        full[8:16, lanes] = sums[g][:, 128:256] + jnp.where(lane < 16, pltpu.roll(tail, 112, 1), 0.0)
    low = full[:, 0:512]
    high = full[:, 512:1024]
    lane_e = iota((8, 256), 1)
    results = []
    wave_cos = jnp.sum(q_rows * nyquist[0:8, :], axis=1, keepdims=True)
    wave_sin = jnp.sum(q_rows * nyquist[8:16, :], axis=1, keepdims=True)

    def both(value):
        return value + pltpu.roll(value, 4, 0)

    real_cos = jnp.zeros((8, 128), F32)
    real_sin = jnp.zeros((8, 128), F32)
    for par, (t1, t2, part) in enumerate(((t1e, t2e, low + high), (t1o, t2o, low - high))):
        spec = jnp.dot(part.astype(BF16), t1[...], preferred_element_type=F32)
        re = jnp.zeros((8, 256), F32)
        im = jnp.zeros((8, 256), F32)
        for fxl in range(2):
            c = spec[8 * fxl : 8 * fxl + 8, 0:256]
            s = spec[8 * fxl : 8 * fxl + 8, 256:512]
            if par == 0:
                ny = s[:, 0:1]
                real_cos = real_cos + ny * nyquist[16 + 16 * fxl : 24 + 16 * fxl, :]
                real_sin = real_sin + ny * nyquist[24 + 16 * fxl : 32 + 16 * fxl, :]
                s = jnp.where(lane_e == 0, 0.0, s)
            pc = phase[32 * par + 8 * fxl : 32 * par + 8 * fxl + 8, :]
            ps = phase[32 * par + 16 + 8 * fxl : 32 * par + 24 + 8 * fxl, :]
            re = re + c * pc - s * ps
            im = im - (s * pc + c * ps)
        re = both(re)
        im = both(im)
        if par == 0:
            re = jnp.where(lane_e == 0, re - total[0:1, 0:1] * (1.0 / SY), re)
        coef = jnp.concatenate([re, im], axis=1).astype(BF16)
        results.append(jnp.dot(coef, t2[...], preferred_element_type=F32))
    wave_cos = wave_cos + both(real_cos)[:, 0:1]
    wave_sin = wave_sin + both(real_sin)[:, 0:1]
    turn = iota((8, 1024), 1) & 3
    wave = wave_cos * jnp.where(turn == 0, 1.0, jnp.where(turn == 2, -1.0, 0.0))
    wave = wave + wave_sin * jnp.where(turn == 1, 1.0, jnp.where(turn == 3, -1.0, 0.0))
    scale = 1.0 / (SX * math.sqrt(BF))
    even = results[0] + wave
    odd = results[1]
    out[:, 0:1024] = ((even + odd) * scale)[0:4]
    out[:, 1024:2048] = ((even - odd) * scale)[0:4]


def exchange(value):
    return lax.all_to_all(value, AXES, split_axis=0, concat_axis=0, tiled=True)


def limit(mib):
    return pltpu.CompilerParams(vmem_limit_bytes=mib * MIB)


def local(frames, dark_frame, gain_frame, bf_index, row_level, shift_num):
    place = jnp.stack([lax.axis_index("scan"), lax.axis_index("grp")]).astype(jnp.int32)
    smem = pl.BlockSpec(memory_space=pltpu.SMEM)
    vmem = pl.BlockSpec(memory_space=pltpu.VMEM)
    hbm = pl.BlockSpec(memory_space=pl.ANY)

    send, r_own, pixel = pl.pallas_call(
        reference_kernel,
        in_specs=[smem, smem, smem, hbm, vmem, vmem, vmem],
        out_specs=[vmem, vmem, vmem],
        out_shape=[
            jax.ShapeDtypeStruct((N, 16, 128), BF16),
            jax.ShapeDtypeStruct((YS, XS), F32),
            jax.ShapeDtypeStruct((8, BF), F32),
        ],
        scratch_shapes=[pltpu.VMEM((YS, XS, BF), BF16), pltpu.SemaphoreType.DMA((PARTS,))],
        compiler_params=limit(60),
        name="reference_image",
    )(
        place,
        row_level,
        shift_num,
        frames,
        dark_frame.reshape(ROWS, 128),
        gain_frame.reshape(ROWS, 128),
        bf_index.reshape(1, BF),
    )
    recv = exchange(send)
    v = pl.pallas_call(
        correct_kernel,
        grid=(PARTS,),
        in_specs=[
            smem,
            pl.BlockSpec((YS // PARTS, XS, BF), lambda i: (i, 0, 0)),
            pl.BlockSpec((8, BF), lambda i: (0, 0)),
        ],
        out_specs=pl.BlockSpec((YS // PARTS, XS, BF), lambda i: (i, 0, 0)),
        out_shape=jax.ShapeDtypeStruct((YS, XS, BF), BF16),
        compiler_params=limit(24),
        cost_estimate=pl.CostEstimate(flops=8 * YS * XS * BF, bytes_accessed=4 * YS * XS * BF, transcendentals=0),
        name="correct",
    )(row_level, frames, pixel)
    sums, total = pl.pallas_call(
        strip_kernel,
        in_specs=[smem, vmem, vmem, hbm, vmem],
        out_specs=[vmem, vmem],
        out_shape=[
            jax.ShapeDtypeStruct((BF, 640), BF16),
            jax.ShapeDtypeStruct((8, 128), F32),
        ],
        scratch_shapes=[
            pltpu.VMEM((YS, XS, BF), BF16),
            pltpu.VMEM((32, XS, BF), BF16),
            pltpu.VMEM((BX * 16, BF), BF16),
            pltpu.VMEM((32, 16, 128), F32),
            pltpu.VMEM((32, 16, 128), F32),
            pltpu.VMEM((32, 384), F32),
            pltpu.VMEM((16, 32, 128), F32),
            pltpu.SemaphoreType.DMA((PARTS,)),
        ],
        compiler_params=limit(30),
        name="strip",
    )(place, recv, r_own, v, jnp.asarray(row_kernel()))
    parts = exchange(sums.reshape(N, 8, 640))
    tables = [jnp.asarray(t) for t in (*col_tables(), phase_tables(), nyquist_tables())]
    return pl.pallas_call(
        finish_kernel,
        in_specs=[vmem] * 8,
        out_specs=[vmem, vmem],
        out_shape=[
            jax.ShapeDtypeStruct((4, 2 * SX), F32),
            jax.ShapeDtypeStruct((8, 256), F32),
        ],
        scratch_shapes=[pltpu.VMEM((16, SX), F32)],
        compiler_params=limit(24),
        name="finish",
    )(parts, total, *tables)


def solution(mesh):
    return jax.shard_map(
        local,
        mesh=mesh,
        in_specs=(P("scan", "grp", None), P(), P(), P(), P("scan"), P(None, AXES)),
        out_specs=(P(AXES, None), P(AXES, None)),
        check_vma=False,
    )
```

```python
import math

import jax
import jax.numpy as jnp
import ml_dtypes
import numpy as np
from jax import lax
from jax.experimental import pallas as pl
from jax.experimental.pallas import tpu as pltpu
from jax.sharding import PartitionSpec as P

SY = 256
SX = 1024
BF = 1024
DET = 36864
AXES = ("scan", "grp")
S = 16
G = 8
N = S * G
YS = SY // S
XS = SX // G
ROWS = DET // 128
BX = 17
PARTS = 4
F32 = jnp.float32
BF16 = jnp.bfloat16
NT = (((1,), (1,)), ((), ()))
TN = (((0,), (0,)), ((), ()))
MIB = 1024 * 1024
YP = YS // PARTS


def iota(shape, dim):
    return lax.broadcasted_iota(jnp.int32, shape, dim)


def row_kernel():
    k = np.arange(-128, 128)
    q = np.arange(1024)
    d = np.cos(2 * np.pi * k[None, :] * q[:, None] / 1024).sum(1) / 256
    r = np.arange(1024)
    yp = 4 * (r // 8) + r % 4
    yy = np.repeat(np.arange(32), 4)
    fy = np.tile(np.arange(4), 32)
    return d[(2 * yp[:, None] - fy[None, :] - 4 * (yy[None, :] - 8)) % 1024].astype(ml_dtypes.bfloat16)


def col_tables():
    x = np.arange(256) - 8
    xp = np.arange(512)
    forward, inverse = [], []
    for par in range(4):
        k = 4 * np.arange(128) + par
        ang = 2 * np.pi * ((x[:, None] * k[None, :]) % 1024) / 1024
        c, s = np.cos(ang), np.sin(ang)
        if par == 0:
            s[:, 0] = np.where(x % 2 == 0, 1.0, -1.0)
        forward.append(np.concatenate([c, s], 1))
        w = np.where(k == 0, 1.0, 2.0)[:, None]
        ang = 2 * np.pi * ((k[:, None] * xp[None, :]) % 2048) / 2048
        inverse.append(np.concatenate([w * np.cos(ang), -w * np.sin(ang)], 0))
    return [np.stack(t).astype(ml_dtypes.bfloat16) for t in (forward, inverse)]


def phase_tables():
    out = np.zeros((4, 2, 2, 8, 128), np.float32)
    for par in range(4):
        k = 4 * np.arange(128) + par
        for fx in range(4):
            rows = slice(4 * (fx >> 1), 4 * (fx >> 1) + 4)
            out[par, 0, fx & 1, rows] = np.cos(2 * np.pi * k * fx / 4096)
            out[par, 1, fx & 1, rows] = np.sin(2 * np.pi * k * fx / 4096)
    return out.reshape(128, 128)


def nyquist_tables():
    w = np.zeros((2, 8, 128), np.float32)
    for i in range(8):
        for fx in range(4):
            for fy in range(4):
                sy = math.sin(math.pi * (2 * (i % 4) - fy) / 4) / 256
                for base in (64, 80):
                    w[0, i, base + fx * 4 + fy] = sy * math.sin(math.pi * fx / 4)
                    w[1, i, base + fx * 4 + fy] = -sy * math.cos(math.pi * fx / 4)
    v = np.zeros((2, 2, 8, 128), np.float32)
    for fx in range(4):
        rows = slice(4 * (fx >> 1), 4 * (fx >> 1) + 4)
        v[fx & 1, 0, rows] = math.cos(math.pi * fx / 4)
        v[fx & 1, 1, rows] = math.sin(math.pi * fx / 4)
    return np.concatenate([w.reshape(16, 128), v.reshape(32, 128)], 0)


def three_parts(value):
    high = value.astype(BF16).astype(F32)
    mid = (value - high).astype(BF16).astype(F32)
    return high, mid, value - high - mid


def reference_kernel(level, amounts, frames, dark, gain, index, send, r_out, pixel_out, held, sems):
    def part(i):
        span = pl.ds(i * (YS // PARTS), YS // PARTS)
        return pltpu.make_async_copy(frames.at[span], held.at[span], sems.at[i])

    for i in range(PARTS):
        part(i).start()
    g = gain[...]
    table = jnp.concatenate(
        [dark[...].astype(F32), (g >> 5).astype(F32), (g & 31).astype(F32)], axis=1
    ).astype(BF16)
    idx = index[...]
    hot = (iota((ROWS, BF), 0) == (idx >> 7)).astype(F32).astype(BF16)
    picked = lax.dot_general(table, hot, TN, preferred_element_type=F32)
    mine = iota((128, BF), 0) == (idx & 127)

    def pick(i):
        return jnp.sum(jnp.where(mine, picked[128 * i : 128 * (i + 1)], 0.0), axis=0, keepdims=True)

    dark_px = pick(0) * (1.0 / 256.0)
    gain_px = (pick(1) * 32.0 + pick(2)) * (1.0 / 4096.0)
    pixel_out[0:1, :] = dark_px
    pixel_out[1:2, :] = gain_px
    offset = jnp.sum(dark_px * gain_px)
    for i in range(PARTS):
        part(i).wait()
        for y in range(i * (YS // PARTS), (i + 1) * (YS // PARTS)):
            acc = None
            for t in range(8):
                lanes = slice(128 * t, 128 * (t + 1))
                term = held[y, :, lanes].astype(F32) * gain_px[:, lanes]
                acc = term if acc is None else acc + term
            high = acc.astype(BF16)
            low = (acc - high.astype(F32)).astype(BF16)
            total = lax.dot_general(
                jnp.ones((8, 256), BF16), jnp.concatenate([high, low], 1), NT, preferred_element_type=F32
            )
            r_out[y : y + 1, :] = total[0:1] - level[y] * offset
    s = lax.axis_index("scan")
    g = lax.axis_index("grp")
    r = r_out[...]
    center = jnp.sum(r) * (1.0 / (YS * XS))
    rest = r - center
    lane = iota((1, 128), 1)
    base = 8 * lax.rem(s * G + g, 16)
    row_sy = jnp.zeros((1, 128), F32)
    row_sx = jnp.zeros((1, 128), F32)
    for i in range(8):
        row_sy = jnp.where(lane == base + i, amounts[0, i].astype(F32), row_sy)
        row_sx = jnp.where(lane == base + i, amounts[1, i].astype(F32), row_sx)
    row_center = jnp.zeros((1, 128), F32)
    for i, piece in enumerate(three_parts(jnp.full((1, 128), center))):
        row_center = jnp.where(lane == i, piece, row_center)
    foot = jnp.concatenate([row_sy, row_sx, row_center, jnp.zeros((5, 128), F32)], axis=0)

    def chunk(top):
        return jnp.concatenate([top, foot], axis=0).astype(BF16)

    plain = chunk(jnp.zeros((8, 128), F32))
    for d in range(N):
        send[d] = plain
    lanes = iota((8, 128), 1)
    sides = jnp.where((lanes >= 32) & (lanes < 96), pltpu.roll(rest[8:16], 64, 1), rest[0:8])
    for ds, top in ((S - 1, rest[0:8]), (0, sides), (1, rest[8:16])):
        for dg in (G - 1, 0, 1):
            if ds or dg:
                send[lax.rem(s + ds, S) * G + lax.rem(g + dg, G)] = chunk(top)


def correct_kernel(level, frames, pixel, rows, v_out, left_out, held, ready, in_sems, out_sems):
    def part(i):
        return pltpu.make_async_copy(frames.at[pl.ds(i * YP, YP)], held.at[pl.ds(i * YP, YP)], in_sems.at[i])

    def back(i):
        return pltpu.make_async_copy(ready.at[pl.ds(i * YP, YP)], v_out.at[pl.ds(i * YP, YP)], out_sems.at[i])

    for i in range(PARTS):
        part(i).start()
    col = iota((128, 512), 1)
    spread = ((iota((128, 512), 0) >> 2) == (col >> 4)) & ((iota((128, 512), 0) & 3) == (col & 3))
    left = jnp.dot(rows[...], spread.astype(F32).astype(BF16), preferred_element_type=F32)
    left_out[...] = jnp.where(
        ((iota((BF, 512), 0) >> 2) & 1) == ((iota((BF, 512), 1) >> 3) & 1), left, 0.0
    ).astype(BF16)
    for i in range(PARTS):
        part(i).wait()
        for y in range(i * YP, (i + 1) * YP):
            value = (held[y].astype(F32) - level[y] * pixel[0:1, :]) * pixel[1:2, :]
            ready[y] = value.astype(BF16)
        back(i).start()
    for i in range(PARTS):
        back(i).wait()


def strip_kernel(
    recv, r_own, v_hbm, left, out, total_out, v, moved, hot, main, over, window, table, around, sums, sems
):
    s = lax.axis_index("scan")
    g = lax.axis_index("grp")

    def part(i):
        return pltpu.make_async_copy(v_hbm.at[pl.ds(i * YP, YP)], v.at[pl.ds(i * YP, YP)], sems.at[i])

    for i in range(PARTS):
        part(i).start()

    centers = jnp.zeros((8, 128), F32)
    feet = []
    for t in range(8):
        foot = jnp.zeros((8, 128), F32)
        for i in range(16):
            foot = foot + recv[16 * t + i].astype(F32)[8:16]
        feet.append(foot)
        centers = centers + foot
    mean = jnp.sum(jnp.where(iota((1, 128), 1) < 3, centers[2:3], 0.0), axis=1, keepdims=True) * (1.0 / N)
    total_out[...] = jnp.broadcast_to(mean * (SY * SX), (8, 128))

    def neighbour(ds, dg):
        got = recv[lax.rem(s + ds, S) * G + lax.rem(g + dg, G)].astype(F32)
        center = jnp.sum(jnp.where(iota((1, 128), 1) < 3, got[10:11], 0.0), axis=1, keepdims=True)
        return got[0:8] + (center - mean)

    for j, dg in enumerate((G - 1, 0, 1)):
        lanes = slice(128 * j, 128 * (j + 1))
        window[0:8, lanes] = neighbour(S - 1, dg)
        window[24:32, lanes] = neighbour(1, dg)
        if dg:
            side = neighbour(0, dg)
            window[8:16, lanes] = side
            window[16:24, lanes] = pltpu.roll(side, 64, 1)
        else:
            window[8:24, lanes] = r_own[...] - mean
    for b in range(16):
        table[b] = pltpu.roll(window[...], (b - 8) % 384, 1)[:, 128:256]

    row = iota((BX * 16, 128), 0)
    for t in range(8):
        sy = feet[t][0:1].astype(jnp.int32)
        sx = feet[t][1:2].astype(jnp.int32)
        code = ((sx >> 2) + 8) * 16 + (sx & 3) * 4 + (sy & 3)
        hot[:, 128 * t : 128 * (t + 1)] = (row == code).astype(F32).astype(BF16)

    for y in range(YS):
        for b in range(16):
            around[16 * b : 16 * (b + 1), 128 * y : 128 * (y + 1)] = table[b, y + 1 : y + 17, :].astype(BF16)
    span = YP * XS
    corr = jnp.zeros((BF, 256), F32)
    for i in range(PARTS):
        part(i).wait()
        corr = corr + lax.dot_general(
            v[i * YP : (i + 1) * YP].reshape(span, BF),
            around[:, span * i : span * (i + 1)],
            (((0,), (1,)), ((), ())),
            preferred_element_type=F32,
        )
    out[:, 384:640] = corr.astype(BF16)

    for t in range(8):
        lanes = slice(128 * t, 128 * (t + 1))
        by = (feet[t][0:1].astype(jnp.int32) >> 2) + 8
        masks = [
            jnp.broadcast_to(((by >> b) & 1).astype(F32), (16, 128)).astype(BF16) > 0.5 for b in range(5)
        ]

        def barrel(i, _, lanes=lanes, masks=masks):
            x0 = pl.multiple_of(i * 16, 16)
            rows_in = [v[y, pl.ds(x0, 16), lanes] for y in range(YS)]
            zero = jnp.zeros((16, 128), BF16)
            for b in range(5):
                step = 1 << b
                size = min(len(rows_in) + step, 32)
                old = rows_in
                rows_in = [
                    jnp.where(
                        masks[b],
                        old[j - step] if 0 <= j - step < len(old) else zero,
                        old[j] if j < len(old) else zero,
                    )
                    for j in range(size)
                ]
            for j in range(32):
                moved[j, pl.ds(x0, 16), lanes] = rows_in[j]
            return 0

        lax.fori_loop(0, 8, barrel, 0)

    lane = iota((16, 128), 1)

    for j in range(4):
        block = moved[8 * j : 8 * j + 8].reshape(8 * XS, BF)
        sums[j & 1] = lax.dot_general(hot[...], block, NT, preferred_element_type=F32)
        for h in range(8):
            lanes = slice(128 * h, 128 * (h + 1))
            acc_main = sums[j & 1, 0:16, lanes]
            acc_over = jnp.zeros((16, 128), F32)
            for b in range(1, BX):
                piece = pltpu.roll(sums[j & 1, 16 * b : 16 * (b + 1), lanes], b, 1)
                acc_main = acc_main + jnp.where(lane >= b, piece, 0.0)
                acc_over = acc_over + jnp.where(lane < b, piece, 0.0)
            main[8 * j + h] = acc_main
            over[8 * j + h] = acc_over

    sign_y = 1.0 - 2.0 * (iota((32, 16, 128), 0) & 1).astype(F32)
    sign_x = 1.0 - 2.0 * (iota((8, 128), 1) & 1).astype(F32)
    folded = jnp.sum((main[...] + over[...]) * sign_y, axis=0)
    folded = jnp.concatenate([jnp.zeros((64, 128), F32), folded, jnp.zeros((48, 128), F32)], axis=0)
    q_row = lax.dot_general(sign_x, folded, NT, precision=lax.Precision.HIGHEST, preferred_element_type=F32)[0:1]
    q_high = q_row.astype(BF16).astype(F32)
    q_row = q_high + pltpu.roll(q_row - q_high, 16, 1)

    kind = (iota((512, 128), 0) >> 2) & 1
    u_main = main[...].reshape(512, 128)
    u_over = over[...].reshape(512, 128)
    first = jnp.where(kind == 0, u_over, 0.0)
    second = jnp.where(kind == 1, u_over, 0.0)
    right = jnp.concatenate(
        [
            jnp.where(kind == 0, u_main, 0.0),
            jnp.where(kind == 1, u_main, 0.0),
            first + pltpu.roll(second, 16, 1),
        ],
        axis=1,
    ).astype(BF16)
    z = jnp.dot(left[...], right, preferred_element_type=F32)
    z = jnp.concatenate([z[:, 0:256], z[:, 256:384] + q_row], axis=1).astype(BF16)
    for b in range(S):
        place = pl.multiple_of(64 * lax.rem(s + b, S), 64)
        out[pl.ds(place, 64), 0:384] = z[64 * b : 64 * (b + 1)]


def finish_kernel(recv, total, forward, inverse, phase, nyquist, out, corr_out, full):
    corr = jnp.zeros((8, 256), F32)
    sums = []
    for g in range(G):
        acc = jnp.zeros((8, 384), F32)
        for s in range(S):
            got = recv[s * G + g].astype(F32)
            acc = acc + got[:, 0:384]
            corr = corr + got[:, 384:640]
        sums.append(acc)
    n = iota((256, 256), 0)
    m = iota((256, 256), 1)
    order = ((n >> 4) == (m & 15)) & ((15 - (n & 15)) == (m >> 4))
    corr_out[...] = jnp.dot(
        corr * (1.0 / math.sqrt(BF * SY * SX)),
        order.astype(F32),
        precision=lax.Precision.HIGHEST,
        preferred_element_type=F32,
    )
    lane = iota((8, 128), 1)
    q_rows = jnp.zeros((8, 128), F32)
    for g in range(G):
        tail = sums[(g - 1) % G][:, 256:384]
        q_rows = q_rows + tail
        lanes = slice(128 * g, 128 * (g + 1))
        full[0:8, lanes] = sums[g][:, 0:128] + jnp.where(lane < 16, tail, 0.0)
        full[8:16, lanes] = sums[g][:, 128:256] + jnp.where(lane < 16, pltpu.roll(tail, 112, 1), 0.0)
    z0, z1, z2, z3 = (full[:, 256 * j : 256 * (j + 1)] for j in range(4))
    inputs = (
        (z0 + z1 + z2 + z3, None),
        (z0 - z2, z3 - z1),
        (z0 - z1 + z2 - z3, None),
        (z0 - z2, z1 - z3),
    )
    lane_e = iota((8, 128), 1)
    wave_cos = jnp.sum(q_rows * nyquist[0:8, :], axis=1, keepdims=True)
    wave_sin = jnp.sum(q_rows * nyquist[8:16, :], axis=1, keepdims=True)

    def both(value):
        return value + pltpu.roll(value, 4, 0)

    real_cos = jnp.zeros((8, 128), F32)
    real_sin = jnp.zeros((8, 128), F32)
    results = []
    for par, (real, imag) in enumerate(inputs):
        if imag is None:
            spec = jnp.dot(real.astype(BF16), forward[par], preferred_element_type=F32)
            cos_part, sin_part = spec[:, 0:128], spec[:, 128:256]
        else:
            stacked = jnp.concatenate([real, imag], axis=0).astype(BF16)
            spec = jnp.dot(stacked, forward[par], preferred_element_type=F32)
            cos_part = spec[0:16, 0:128] + spec[16:32, 128:256]
            sin_part = spec[0:16, 128:256] - spec[16:32, 0:128]
        re = jnp.zeros((8, 128), F32)
        im = jnp.zeros((8, 128), F32)
        for fxl in range(2):
            c = cos_part[8 * fxl : 8 * fxl + 8]
            s = sin_part[8 * fxl : 8 * fxl + 8]
            if par == 0:
                ny = s[:, 0:1]
                real_cos = real_cos + ny * nyquist[16 + 16 * fxl : 24 + 16 * fxl, :]
                real_sin = real_sin + ny * nyquist[24 + 16 * fxl : 32 + 16 * fxl, :]
                s = jnp.where(lane_e == 0, 0.0, s)
            pc = phase[32 * par + 8 * fxl : 32 * par + 8 * fxl + 8, :]
            ps = phase[32 * par + 16 + 8 * fxl : 32 * par + 24 + 8 * fxl, :]
            re = re + c * pc - s * ps
            im = im - (s * pc + c * ps)
        re = both(re)
        im = both(im)
        if par == 0:
            re = jnp.where(lane_e == 0, re - total[0:1, 0:1] * (1.0 / SY), re)
        coef = jnp.concatenate([re, im], axis=1)
        if imag is not None:
            coef = jnp.concatenate([coef, jnp.concatenate([im, -re], axis=1)], axis=0)
        results.append(jnp.dot(coef.astype(BF16), inverse[par], preferred_element_type=F32))
    wave_cos = wave_cos + both(real_cos)[:, 0:1]
    wave_sin = wave_sin + both(real_sin)[:, 0:1]
    turn = iota((8, 512), 1) & 3
    wave = wave_cos * jnp.where(turn == 0, 1.0, jnp.where(turn == 2, -1.0, 0.0))
    wave = wave + wave_sin * jnp.where(turn == 1, 1.0, jnp.where(turn == 3, -1.0, 0.0))
    scale = 1.0 / (SX * math.sqrt(BF))
    first = results[0] + wave
    e1, f1 = results[1][0:8], results[1][8:16]
    e3, f3 = results[3][0:8], results[3][8:16]
    quarters = (
        first + results[2] + e1 + e3,
        first - results[2] - f1 + f3,
        first + results[2] - e1 - e3,
        first - results[2] + f1 - f3,
    )
    for j, quarter in enumerate(quarters):
        out[:, 512 * j : 512 * (j + 1)] = (quarter * scale)[0:4]


def exchange(value):
    return lax.all_to_all(value, AXES, split_axis=0, concat_axis=0, tiled=True)


def limit(mib):
    return pltpu.CompilerParams(vmem_limit_bytes=mib * MIB)


def local(frames, dark_frame, gain_frame, bf_index, row_level, shift_num):
    smem = pl.BlockSpec(memory_space=pltpu.SMEM)
    vmem = pl.BlockSpec(memory_space=pltpu.VMEM)
    hbm = pl.BlockSpec(memory_space=pltpu.HBM)

    send, r_own, pixel = pl.pallas_call(
        reference_kernel,
        in_specs=[smem, smem, hbm, vmem, vmem, vmem],
        out_specs=[vmem, vmem, vmem],
        out_shape=[
            jax.ShapeDtypeStruct((N, 16, 128), BF16),
            jax.ShapeDtypeStruct((YS, XS), F32),
            jax.ShapeDtypeStruct((8, BF), F32),
        ],
        scratch_shapes=[pltpu.VMEM((YS, XS, BF), BF16), pltpu.SemaphoreType.DMA((PARTS,))],
        compiler_params=limit(60),
        name="reference_image",
    )(
        row_level,
        shift_num,
        frames,
        dark_frame.reshape(ROWS, 128),
        gain_frame.reshape(ROWS, 128),
        bf_index.reshape(1, BF),
    )
    recv = exchange(send)
    v, left = pl.pallas_call(
        correct_kernel,
        in_specs=[smem, hbm, vmem, vmem],
        out_specs=[hbm, vmem],
        out_shape=[
            jax.ShapeDtypeStruct((YS, XS, BF), BF16),
            jax.ShapeDtypeStruct((BF, 512), BF16),
        ],
        scratch_shapes=[
            pltpu.VMEM((YS, XS, BF), BF16),
            pltpu.VMEM((YS, XS, BF), BF16),
            pltpu.SemaphoreType.DMA((PARTS,)),
            pltpu.SemaphoreType.DMA((PARTS,)),
        ],
        compiler_params=limit(60),
        cost_estimate=pl.CostEstimate(flops=8 * YS * XS * BF, bytes_accessed=4 * YS * XS * BF, transcendentals=0),
        name="correct",
    )(row_level, frames, pixel, jnp.asarray(row_kernel()))
    sums, total = pl.pallas_call(
        strip_kernel,
        in_specs=[vmem, vmem, hbm, vmem],
        out_specs=[vmem, vmem],
        out_shape=[
            jax.ShapeDtypeStruct((BF, 640), BF16),
            jax.ShapeDtypeStruct((8, 128), F32),
        ],
        scratch_shapes=[
            pltpu.VMEM((YS, XS, BF), BF16),
            pltpu.VMEM((32, XS, BF), BF16),
            pltpu.VMEM((BX * 16, BF), BF16),
            pltpu.VMEM((32, 16, 128), F32),
            pltpu.VMEM((32, 16, 128), F32),
            pltpu.VMEM((32, 384), F32),
            pltpu.VMEM((16, 32, 128), F32),
            pltpu.VMEM((256, YS * XS), BF16),
            pltpu.VMEM((2, BX * 16, BF), F32),
            pltpu.SemaphoreType.DMA((PARTS,)),
        ],
        compiler_params=limit(60),
        name="strip",
    )(recv, r_own, v, left)
    parts = exchange(sums.reshape(N, 8, 640))
    tables = [jnp.asarray(t) for t in (*col_tables(), phase_tables(), nyquist_tables())]
    return pl.pallas_call(
        finish_kernel,
        in_specs=[vmem] * 6,
        out_specs=[vmem, vmem],
        out_shape=[
            jax.ShapeDtypeStruct((4, 2 * SX), F32),
            jax.ShapeDtypeStruct((8, 256), F32),
        ],
        scratch_shapes=[pltpu.VMEM((16, SX), F32)],
        compiler_params=limit(24),
        name="finish",
    )(parts, total, *tables)


def solution(mesh):
    return jax.shard_map(
        local,
        mesh=mesh,
        in_specs=(P("scan", "grp", None), P(), P(), P(), P("scan"), P(None, AXES)),
        out_specs=(P(AXES, None), P(AXES, None)),
        check_vma=False,
    )
```

```python
import math

import jax
import jax.numpy as jnp
import ml_dtypes
import numpy as np
from jax import lax
from jax.experimental import pallas as pl
from jax.experimental.pallas import tpu as pltpu
from jax.sharding import PartitionSpec as P

SY = 256
SX = 1024
BF = 1024
DET = 36864
AXES = ("scan", "grp")
S = 16
G = 8
N = S * G
YS = SY // S
XS = SX // G
ROWS = DET // 128
BX = 17
PARTS = 4
F32 = jnp.float32
BF16 = jnp.bfloat16
NT = (((1,), (1,)), ((), ()))
TN = (((0,), (0,)), ((), ()))
MIB = 1024 * 1024
YP = YS // PARTS


def iota(shape, dim):
    return lax.broadcasted_iota(jnp.int32, shape, dim)


def row_kernel():
    k = np.arange(-128, 128)
    q = np.arange(1024)
    d = np.cos(2 * np.pi * k[None, :] * q[:, None] / 1024).sum(1) / 256
    r = np.arange(1024)
    yp = 4 * (r // 8) + r % 4
    yy = np.repeat(np.arange(32), 4)
    fy = np.tile(np.arange(4), 32)
    return d[(2 * yp[:, None] - fy[None, :] - 4 * (yy[None, :] - 8)) % 1024].astype(ml_dtypes.bfloat16)


def col_tables():
    x = np.arange(256) - 8
    xp = np.arange(512)
    forward, inverse = [], []
    for par in range(4):
        k = 4 * np.arange(128) + par
        ang = 2 * np.pi * ((x[:, None] * k[None, :]) % 1024) / 1024
        c, s = np.cos(ang), np.sin(ang)
        if par == 0:
            s[:, 0] = np.where(x % 2 == 0, 1.0, -1.0)
        forward.append(np.concatenate([c, s], 1))
        w = np.where(k == 0, 1.0, 2.0)[:, None]
        ang = 2 * np.pi * ((k[:, None] * xp[None, :]) % 2048) / 2048
        inverse.append(np.concatenate([w * np.cos(ang), -w * np.sin(ang)], 0))
    return [np.stack(t).astype(ml_dtypes.bfloat16) for t in (forward, inverse)]


def phase_tables():
    out = np.zeros((4, 2, 2, 8, 128), np.float32)
    for par in range(4):
        k = 4 * np.arange(128) + par
        for fx in range(4):
            rows = slice(4 * (fx >> 1), 4 * (fx >> 1) + 4)
            out[par, 0, fx & 1, rows] = np.cos(2 * np.pi * k * fx / 4096)
            out[par, 1, fx & 1, rows] = np.sin(2 * np.pi * k * fx / 4096)
    return out.reshape(128, 128)


def nyquist_tables():
    w = np.zeros((2, 8, 128), np.float32)
    for i in range(8):
        for fx in range(4):
            for fy in range(4):
                sy = math.sin(math.pi * (2 * (i % 4) - fy) / 4) / 256
                for base in (64, 80):
                    w[0, i, base + fx * 4 + fy] = sy * math.sin(math.pi * fx / 4)
                    w[1, i, base + fx * 4 + fy] = -sy * math.cos(math.pi * fx / 4)
    v = np.zeros((2, 2, 8, 128), np.float32)
    for fx in range(4):
        rows = slice(4 * (fx >> 1), 4 * (fx >> 1) + 4)
        v[fx & 1, 0, rows] = math.cos(math.pi * fx / 4)
        v[fx & 1, 1, rows] = math.sin(math.pi * fx / 4)
    return np.concatenate([w.reshape(16, 128), v.reshape(32, 128)], 0)


def three_parts(value):
    high = value.astype(BF16).astype(F32)
    mid = (value - high).astype(BF16).astype(F32)
    return high, mid, value - high - mid


def reference_kernel(level, amounts, frames, dark, gain, index, send, r_out, pixel_out, held, sems):
    def part(i):
        span = pl.ds(i * (YS // PARTS), YS // PARTS)
        return pltpu.make_async_copy(frames.at[span], held.at[span], sems.at[i])

    for i in range(PARTS):
        part(i).start()
    g = gain[...]
    table = jnp.concatenate(
        [dark[...].astype(F32), (g >> 5).astype(F32), (g & 31).astype(F32)], axis=1
    ).astype(BF16)
    idx = index[...]
    hot = (iota((ROWS, BF), 0) == (idx >> 7)).astype(F32).astype(BF16)
    picked = lax.dot_general(table, hot, TN, preferred_element_type=F32)
    mine = iota((128, BF), 0) == (idx & 127)

    def pick(i):
        return jnp.sum(jnp.where(mine, picked[128 * i : 128 * (i + 1)], 0.0), axis=0, keepdims=True)

    dark_px = pick(0) * (1.0 / 256.0)
    gain_px = (pick(1) * 32.0 + pick(2)) * (1.0 / 4096.0)
    pixel_out[0:1, :] = dark_px
    pixel_out[1:2, :] = gain_px
    offset = jnp.sum(dark_px * gain_px)
    for i in range(PARTS):
        part(i).wait()
        for y in range(i * (YS // PARTS), (i + 1) * (YS // PARTS)):
            acc = None
            for t in range(8):
                lanes = slice(128 * t, 128 * (t + 1))
                term = held[y, :, lanes].astype(F32) * gain_px[:, lanes]
                acc = term if acc is None else acc + term
            high = acc.astype(BF16)
            low = (acc - high.astype(F32)).astype(BF16)
            total = lax.dot_general(
                jnp.ones((8, 256), BF16), jnp.concatenate([high, low], 1), NT, preferred_element_type=F32
            )
            r_out[y : y + 1, :] = total[0:1] - level[y] * offset
    s = lax.axis_index("scan")
    g = lax.axis_index("grp")
    r = r_out[...]
    center = jnp.sum(r) * (1.0 / (YS * XS))
    rest = r - center
    lane = iota((1, 128), 1)
    base = 8 * lax.rem(s * G + g, 16)
    row_sy = jnp.zeros((1, 128), F32)
    row_sx = jnp.zeros((1, 128), F32)
    for i in range(8):
        row_sy = jnp.where(lane == base + i, amounts[0, i].astype(F32), row_sy)
        row_sx = jnp.where(lane == base + i, amounts[1, i].astype(F32), row_sx)
    row_center = jnp.zeros((1, 128), F32)
    for i, piece in enumerate(three_parts(jnp.full((1, 128), center))):
        row_center = jnp.where(lane == i, piece, row_center)
    foot = jnp.concatenate([row_sy, row_sx, row_center, jnp.zeros((5, 128), F32)], axis=0)

    def chunk(top):
        return jnp.concatenate([top, foot], axis=0).astype(BF16)

    plain = chunk(jnp.zeros((8, 128), F32))
    for d in range(N):
        send[d] = plain
    lanes = iota((8, 128), 1)
    sides = jnp.where((lanes >= 32) & (lanes < 96), pltpu.roll(rest[8:16], 64, 1), rest[0:8])
    for ds, top in ((S - 1, rest[0:8]), (0, sides), (1, rest[8:16])):
        for dg in (G - 1, 0, 1):
            if ds or dg:
                send[lax.rem(s + ds, S) * G + lax.rem(g + dg, G)] = chunk(top)


def strip_kernel(
    level, recv, r_own, pixel, frames, rows, out, held, v, moved, hot, main, over, window, table, around, sums, sems
):
    s = lax.axis_index("scan")
    g = lax.axis_index("grp")

    def part(i):
        return pltpu.make_async_copy(frames.at[pl.ds(i * YP, YP)], held.at[pl.ds(i * YP, YP)], sems.at[i])

    for i in range(PARTS):
        part(i).start()

    centers = jnp.zeros((8, 128), F32)
    feet = []
    for t in range(8):
        foot = jnp.zeros((8, 128), F32)
        for i in range(16):
            foot = foot + recv[16 * t + i].astype(F32)[8:16]
        feet.append(foot)
        centers = centers + foot
    mean = jnp.sum(jnp.where(iota((1, 128), 1) < 3, centers[2:3], 0.0), axis=1, keepdims=True) * (1.0 / N)
    total_row = jnp.zeros((1, 128), F32)
    for i, piece in enumerate(three_parts(mean * (SY * SX))):
        total_row = jnp.where(iota((1, 128), 1) == 96 + i, piece, total_row)

    def neighbour(ds, dg):
        got = recv[lax.rem(s + ds, S) * G + lax.rem(g + dg, G)].astype(F32)
        center = jnp.sum(jnp.where(iota((1, 128), 1) < 3, got[10:11], 0.0), axis=1, keepdims=True)
        return got[0:8] + (center - mean)

    for j, dg in enumerate((G - 1, 0, 1)):
        lanes = slice(128 * j, 128 * (j + 1))
        window[0:8, lanes] = neighbour(S - 1, dg)
        window[24:32, lanes] = neighbour(1, dg)
        if dg:
            side = neighbour(0, dg)
            window[8:16, lanes] = side
            window[16:24, lanes] = pltpu.roll(side, 64, 1)
        else:
            window[8:24, lanes] = r_own[...] - mean
    for b in range(16):
        table[b] = pltpu.roll(window[...], (b - 8) % 384, 1)[:, 128:256]

    row = iota((BX * 16, 128), 0)
    for t in range(8):
        sy = feet[t][0:1].astype(jnp.int32)
        sx = feet[t][1:2].astype(jnp.int32)
        code = ((sx >> 2) + 8) * 16 + (sx & 3) * 4 + (sy & 3)
        hot[:, 128 * t : 128 * (t + 1)] = (row == code).astype(F32).astype(BF16)

    for y in range(YS):
        for b in range(16):
            around[16 * b : 16 * (b + 1), 128 * y : 128 * (y + 1)] = table[b, y + 1 : y + 17, :].astype(BF16)
    span = YP * XS
    corr = jnp.zeros((BF, 256), F32)
    for i in range(PARTS):
        part(i).wait()
        for y in range(i * YP, (i + 1) * YP):
            value = (held[y].astype(F32) - level[y] * pixel[0:1, :]) * pixel[1:2, :]
            v[y] = value.astype(BF16)
        corr = corr + lax.dot_general(
            v[i * YP : (i + 1) * YP].reshape(span, BF),
            around[:, span * i : span * (i + 1)],
            (((0,), (1,)), ((), ())),
            preferred_element_type=F32,
        )
    out[:, 384:640] = corr.astype(BF16)

    for t in range(8):
        lanes = slice(128 * t, 128 * (t + 1))
        by = (feet[t][0:1].astype(jnp.int32) >> 2) + 8
        masks = [
            jnp.broadcast_to(((by >> b) & 1).astype(F32), (16, 128)).astype(BF16) > 0.5 for b in range(5)
        ]

        def barrel(i, _, lanes=lanes, masks=masks):
            x0 = pl.multiple_of(i * 16, 16)
            rows_in = [v[y, pl.ds(x0, 16), lanes] for y in range(YS)]
            zero = jnp.zeros((16, 128), BF16)
            for b in range(5):
                step = 1 << b
                size = min(len(rows_in) + step, 32)
                old = rows_in
                rows_in = [
                    jnp.where(
                        masks[b],
                        old[j - step] if 0 <= j - step < len(old) else zero,
                        old[j] if j < len(old) else zero,
                    )
                    for j in range(size)
                ]
            for j in range(32):
                moved[j, pl.ds(x0, 16), lanes] = rows_in[j]
            return 0

        lax.fori_loop(0, 8, barrel, 0)

    lane = iota((16, 128), 1)

    for j in range(4):
        block = moved[8 * j : 8 * j + 8].reshape(8 * XS, BF)
        sums[j & 1] = lax.dot_general(hot[...], block, NT, preferred_element_type=F32)
        for h in range(8):
            lanes = slice(128 * h, 128 * (h + 1))
            acc_main = sums[j & 1, 0:16, lanes]
            acc_over = jnp.zeros((16, 128), F32)
            for b in range(1, BX):
                piece = pltpu.roll(sums[j & 1, 16 * b : 16 * (b + 1), lanes], b, 1)
                acc_main = acc_main + jnp.where(lane >= b, piece, 0.0)
                acc_over = acc_over + jnp.where(lane < b, piece, 0.0)
            main[8 * j + h] = acc_main
            over[8 * j + h] = acc_over

    sign_y = 1.0 - 2.0 * (iota((32, 16, 128), 0) & 1).astype(F32)
    sign_x = 1.0 - 2.0 * (iota((8, 128), 1) & 1).astype(F32)
    folded = jnp.sum((main[...] + over[...]) * sign_y, axis=0)
    folded = jnp.concatenate([jnp.zeros((64, 128), F32), folded, jnp.zeros((48, 128), F32)], axis=0)
    q_row = lax.dot_general(sign_x, folded, NT, precision=lax.Precision.HIGHEST, preferred_element_type=F32)[0:1]
    q_high = q_row.astype(BF16).astype(F32)
    q_row = q_high + pltpu.roll(q_row - q_high, 16, 1)

    col = iota((128, 512), 1)
    spread = ((iota((128, 512), 0) >> 2) == (col >> 4)) & ((iota((128, 512), 0) & 3) == (col & 3))
    left = jnp.dot(rows[...], spread.astype(F32).astype(BF16), preferred_element_type=F32)
    left = jnp.where(((iota((BF, 512), 0) >> 2) & 1) == ((iota((BF, 512), 1) >> 3) & 1), left, 0.0).astype(BF16)
    kind = (iota((512, 128), 0) >> 2) & 1
    u_main = main[...].reshape(512, 128)
    u_over = over[...].reshape(512, 128)
    first = jnp.where(kind == 0, u_over, 0.0)
    second = jnp.where(kind == 1, u_over, 0.0)
    right = jnp.concatenate(
        [
            jnp.where(kind == 0, u_main, 0.0),
            jnp.where(kind == 1, u_main, 0.0),
            first + pltpu.roll(second, 16, 1),
        ],
        axis=1,
    ).astype(BF16)
    z = jnp.dot(left, right, preferred_element_type=F32)
    z = jnp.concatenate([z[:, 0:256], z[:, 256:384] + (q_row + total_row)], axis=1).astype(BF16)
    for b in range(S):
        place = pl.multiple_of(64 * lax.rem(s + b, S), 64)
        out[pl.ds(place, 64), 0:384] = z[64 * b : 64 * (b + 1)]


def finish_kernel(recv, forward, inverse, phase, nyquist, out, corr_out, full):
    corr = jnp.zeros((8, 256), F32)
    sums = []
    for g in range(G):
        acc = jnp.zeros((8, 384), F32)
        for s in range(S):
            got = recv[s * G + g].astype(F32)
            acc = acc + got[:, 0:384]
            corr = corr + got[:, 384:640]
        sums.append(acc)
    n = iota((256, 256), 0)
    m = iota((256, 256), 1)
    order = ((n >> 4) == (m & 15)) & ((15 - (n & 15)) == (m >> 4))
    corr_out[...] = jnp.dot(
        corr * (1.0 / math.sqrt(BF * SY * SX)),
        order.astype(F32),
        precision=lax.Precision.HIGHEST,
        preferred_element_type=F32,
    )
    lane = iota((8, 128), 1)
    foot = recv[0].astype(F32)[:, 256:384]
    total = jnp.sum(jnp.where((lane >= 96) & (lane < 99), foot, 0.0), axis=1, keepdims=True)
    q_rows = jnp.zeros((8, 128), F32)
    for g in range(G):
        tail = sums[(g - 1) % G][:, 256:384]
        q_rows = q_rows + tail
        lanes = slice(128 * g, 128 * (g + 1))
        full[0:8, lanes] = sums[g][:, 0:128] + jnp.where(lane < 16, tail, 0.0)
        full[8:16, lanes] = sums[g][:, 128:256] + jnp.where(lane < 16, pltpu.roll(tail, 112, 1), 0.0)
    z0, z1, z2, z3 = (full[:, 256 * j : 256 * (j + 1)] for j in range(4))
    inputs = (
        (z0 + z1 + z2 + z3, None),
        (z0 - z2, z3 - z1),
        (z0 - z1 + z2 - z3, None),
        (z0 - z2, z1 - z3),
    )
    lane_e = iota((8, 128), 1)
    wave_cos = jnp.sum(q_rows * nyquist[0:8, :], axis=1, keepdims=True)
    wave_sin = jnp.sum(q_rows * nyquist[8:16, :], axis=1, keepdims=True)

    def both(value):
        return value + pltpu.roll(value, 4, 0)

    real_cos = jnp.zeros((8, 128), F32)
    real_sin = jnp.zeros((8, 128), F32)
    results = []
    for par, (real, imag) in enumerate(inputs):
        if imag is None:
            spec = jnp.dot(real.astype(BF16), forward[par], preferred_element_type=F32)
            cos_part, sin_part = spec[:, 0:128], spec[:, 128:256]
        else:
            stacked = jnp.concatenate([real, imag], axis=0).astype(BF16)
            spec = jnp.dot(stacked, forward[par], preferred_element_type=F32)
            cos_part = spec[0:16, 0:128] + spec[16:32, 128:256]
            sin_part = spec[0:16, 128:256] - spec[16:32, 0:128]
        re = jnp.zeros((8, 128), F32)
        im = jnp.zeros((8, 128), F32)
        for fxl in range(2):
            c = cos_part[8 * fxl : 8 * fxl + 8]
            s = sin_part[8 * fxl : 8 * fxl + 8]
            if par == 0:
                ny = s[:, 0:1]
                real_cos = real_cos + ny * nyquist[16 + 16 * fxl : 24 + 16 * fxl, :]
                real_sin = real_sin + ny * nyquist[24 + 16 * fxl : 32 + 16 * fxl, :]
                s = jnp.where(lane_e == 0, 0.0, s)
            pc = phase[32 * par + 8 * fxl : 32 * par + 8 * fxl + 8, :]
            ps = phase[32 * par + 16 + 8 * fxl : 32 * par + 24 + 8 * fxl, :]
            re = re + c * pc - s * ps
            im = im - (s * pc + c * ps)
        re = both(re)
        im = both(im)
        if par == 0:
            re = jnp.where(lane_e == 0, re - total * (1.0 / SY), re)
        coef = jnp.concatenate([re, im], axis=1)
        if imag is not None:
            coef = jnp.concatenate([coef, jnp.concatenate([im, -re], axis=1)], axis=0)
        results.append(jnp.dot(coef.astype(BF16), inverse[par], preferred_element_type=F32))
    wave_cos = wave_cos + both(real_cos)[:, 0:1]
    wave_sin = wave_sin + both(real_sin)[:, 0:1]
    turn = iota((8, 512), 1) & 3
    wave = wave_cos * jnp.where(turn == 0, 1.0, jnp.where(turn == 2, -1.0, 0.0))
    wave = wave + wave_sin * jnp.where(turn == 1, 1.0, jnp.where(turn == 3, -1.0, 0.0))
    scale = 1.0 / (SX * math.sqrt(BF))
    first = results[0] + wave
    e1, f1 = results[1][0:8], results[1][8:16]
    e3, f3 = results[3][0:8], results[3][8:16]
    quarters = (
        first + results[2] + e1 + e3,
        first - results[2] - f1 + f3,
        first + results[2] - e1 - e3,
        first - results[2] + f1 - f3,
    )
    for j, quarter in enumerate(quarters):
        out[:, 512 * j : 512 * (j + 1)] = (quarter * scale)[0:4]


def exchange(value):
    return lax.all_to_all(value, AXES, split_axis=0, concat_axis=0, tiled=True)


def limit(mib):
    return pltpu.CompilerParams(vmem_limit_bytes=mib * MIB)


def local(frames, dark_frame, gain_frame, bf_index, row_level, shift_num):
    smem = pl.BlockSpec(memory_space=pltpu.SMEM)
    vmem = pl.BlockSpec(memory_space=pltpu.VMEM)
    hbm = pl.BlockSpec(memory_space=pltpu.HBM)

    send, r_own, pixel = pl.pallas_call(
        reference_kernel,
        in_specs=[smem, smem, hbm, vmem, vmem, vmem],
        out_specs=[vmem, vmem, vmem],
        out_shape=[
            jax.ShapeDtypeStruct((N, 16, 128), BF16),
            jax.ShapeDtypeStruct((YS, XS), F32),
            jax.ShapeDtypeStruct((8, BF), F32),
        ],
        scratch_shapes=[pltpu.VMEM((YS, XS, BF), BF16), pltpu.SemaphoreType.DMA((PARTS,))],
        compiler_params=limit(60),
        name="reference_image",
    )(
        row_level,
        shift_num,
        frames,
        dark_frame.reshape(ROWS, 128),
        gain_frame.reshape(ROWS, 128),
        bf_index.reshape(1, BF),
    )
    recv = exchange(send)
    sums = pl.pallas_call(
        strip_kernel,
        in_specs=[smem, vmem, vmem, vmem, hbm, vmem],
        out_specs=vmem,
        out_shape=jax.ShapeDtypeStruct((BF, 640), BF16),
        scratch_shapes=[
            pltpu.VMEM((YS, XS, BF), BF16),
            pltpu.VMEM((YS, XS, BF), BF16),
            pltpu.VMEM((32, XS, BF), BF16),
            pltpu.VMEM((BX * 16, BF), BF16),
            pltpu.VMEM((32, 16, 128), F32),
            pltpu.VMEM((32, 16, 128), F32),
            pltpu.VMEM((32, 384), F32),
            pltpu.VMEM((16, 32, 128), F32),
            pltpu.VMEM((256, YS * XS), BF16),
            pltpu.VMEM((2, BX * 16, BF), F32),
            pltpu.SemaphoreType.DMA((PARTS,)),
        ],
        compiler_params=limit(50),
        name="strip",
    )(row_level, recv, r_own, pixel, frames, jnp.asarray(row_kernel()))
    parts = exchange(sums.reshape(N, 8, 640))
    tables = [jnp.asarray(t) for t in (*col_tables(), phase_tables(), nyquist_tables())]
    return pl.pallas_call(
        finish_kernel,
        in_specs=[vmem] * 5,
        out_specs=[vmem, vmem],
        out_shape=[
            jax.ShapeDtypeStruct((4, 2 * SX), F32),
            jax.ShapeDtypeStruct((8, 256), F32),
        ],
        scratch_shapes=[pltpu.VMEM((16, SX), F32)],
        compiler_params=limit(24),
        name="finish",
    )(parts, *tables)


def solution(mesh):
    return jax.shard_map(
        local,
        mesh=mesh,
        in_specs=(P("scan", "grp", None), P(), P(), P(), P("scan"), P(None, AXES)),
        out_specs=(P(AXES, None), P(AXES, None)),
        check_vma=False,
    )
```

```python
import math

import jax
import jax.numpy as jnp
import ml_dtypes
import numpy as np
from jax import lax
from jax.experimental import pallas as pl
from jax.experimental.pallas import tpu as pltpu
from jax.sharding import PartitionSpec as P

SY = 256
SX = 1024
BF = 1024
DET = 36864
AXES = ("scan", "grp")
S = 16
G = 8
N = S * G
YS = SY // S
XS = SX // G
ROWS = DET // 128
BX = 17
PARTS = 4
F32 = jnp.float32
BF16 = jnp.bfloat16
NT = (((1,), (1,)), ((), ()))
TN = (((0,), (0,)), ((), ()))
MIB = 1024 * 1024
YP = YS // PARTS


def iota(shape, dim):
    return lax.broadcasted_iota(jnp.int32, shape, dim)


def row_kernel():
    k = np.arange(-128, 128)
    q = np.arange(1024)
    d = np.cos(2 * np.pi * k[None, :] * q[:, None] / 1024).sum(1) / 256
    r = np.arange(1024)
    yp = 4 * (r // 8) + r % 4
    yy = np.repeat(np.arange(32), 4)
    fy = np.tile(np.arange(4), 32)
    return d[(2 * yp[:, None] - fy[None, :] - 4 * (yy[None, :] - 8)) % 1024].astype(ml_dtypes.bfloat16)


def col_tables():
    x = np.arange(256) - 8
    xp = np.arange(512)
    forward, inverse = [], []
    for par in range(4):
        k = 4 * np.arange(128) + par
        ang = 2 * np.pi * ((x[:, None] * k[None, :]) % 1024) / 1024
        c, s = np.cos(ang), np.sin(ang)
        if par == 0:
            s[:, 0] = np.where(x % 2 == 0, 1.0, -1.0)
        forward.append(np.concatenate([c, s], 1))
        w = np.where(k == 0, 1.0, 2.0)[:, None]
        ang = 2 * np.pi * ((k[:, None] * xp[None, :]) % 2048) / 2048
        inverse.append(np.concatenate([w * np.cos(ang), -w * np.sin(ang)], 0))
    return [np.stack(t).astype(ml_dtypes.bfloat16) for t in (forward, inverse)]


def phase_tables():
    out = np.zeros((4, 2, 2, 8, 128), np.float32)
    for par in range(4):
        k = 4 * np.arange(128) + par
        for fx in range(4):
            rows = slice(4 * (fx >> 1), 4 * (fx >> 1) + 4)
            out[par, 0, fx & 1, rows] = np.cos(2 * np.pi * k * fx / 4096)
            out[par, 1, fx & 1, rows] = np.sin(2 * np.pi * k * fx / 4096)
    return out.reshape(128, 128)


def nyquist_tables():
    w = np.zeros((2, 8, 128), np.float32)
    for i in range(8):
        for fx in range(4):
            for fy in range(4):
                sy = math.sin(math.pi * (2 * (i % 4) - fy) / 4) / 256
                for base in (64, 80):
                    w[0, i, base + fx * 4 + fy] = sy * math.sin(math.pi * fx / 4)
                    w[1, i, base + fx * 4 + fy] = -sy * math.cos(math.pi * fx / 4)
    v = np.zeros((2, 2, 8, 128), np.float32)
    for fx in range(4):
        rows = slice(4 * (fx >> 1), 4 * (fx >> 1) + 4)
        v[fx & 1, 0, rows] = math.cos(math.pi * fx / 4)
        v[fx & 1, 1, rows] = math.sin(math.pi * fx / 4)
    return np.concatenate([w.reshape(16, 128), v.reshape(32, 128)], 0)


def three_parts(value):
    high = value.astype(BF16).astype(F32)
    mid = (value - high).astype(BF16).astype(F32)
    return high, mid, value - high - mid


def reference_kernel(level, amounts, frames, dark, gain, index, send, keep, held, sems):
    def part(i):
        span = pl.ds(i * (YS // PARTS), YS // PARTS)
        return pltpu.make_async_copy(frames.at[span], held.at[span], sems.at[i])

    for i in range(PARTS):
        part(i).start()
    g = gain[...]
    table = jnp.concatenate(
        [dark[...].astype(F32), (g >> 5).astype(F32), (g & 31).astype(F32)], axis=1
    ).astype(BF16)
    idx = index[...]
    hot = (iota((ROWS, BF), 0) == (idx >> 7)).astype(F32).astype(BF16)
    picked = lax.dot_general(table, hot, TN, preferred_element_type=F32)
    mine = iota((128, BF), 0) == (idx & 127)

    def pick(i):
        return jnp.sum(jnp.where(mine, picked[128 * i : 128 * (i + 1)], 0.0), axis=0, keepdims=True)

    dark_px = pick(0) * (1.0 / 256.0)
    gain_px = (pick(1) * 32.0 + pick(2)) * (1.0 / 4096.0)
    keep[0:1, :] = dark_px
    keep[1:2, :] = gain_px
    offset = jnp.sum(dark_px * gain_px)
    for i in range(PARTS):
        part(i).wait()
        for y in range(i * (YS // PARTS), (i + 1) * (YS // PARTS)):
            acc = None
            for t in range(8):
                lanes = slice(128 * t, 128 * (t + 1))
                term = held[y, :, lanes].astype(F32) * gain_px[:, lanes]
                acc = term if acc is None else acc + term
            high = acc.astype(BF16)
            low = (acc - high.astype(F32)).astype(BF16)
            total = lax.dot_general(
                jnp.ones((8, 256), BF16), jnp.concatenate([high, low], 1), NT, preferred_element_type=F32
            )
            keep[8 + y : 9 + y, 0:128] = total[0:1] - level[y] * offset
    s = lax.axis_index("scan")
    g = lax.axis_index("grp")
    r = keep[8:24, 0:128]
    center = jnp.sum(r) * (1.0 / (YS * XS))
    rest = r - center
    lane = iota((1, 128), 1)
    base = 8 * lax.rem(s * G + g, 16)
    row_sy = jnp.zeros((1, 128), F32)
    row_sx = jnp.zeros((1, 128), F32)
    for i in range(8):
        row_sy = jnp.where(lane == base + i, amounts[0, i].astype(F32), row_sy)
        row_sx = jnp.where(lane == base + i, amounts[1, i].astype(F32), row_sx)
    row_center = jnp.zeros((1, 128), F32)
    for i, piece in enumerate(three_parts(jnp.full((1, 128), center))):
        row_center = jnp.where(lane == i, piece, row_center)
    foot = jnp.concatenate([row_sy, row_sx, row_center, jnp.zeros((5, 128), F32)], axis=0)

    def chunk(top):
        return jnp.concatenate([top, foot], axis=0).astype(BF16)

    plain = chunk(jnp.zeros((8, 128), F32))
    for d in range(N):
        send[d] = plain
    lanes = iota((8, 128), 1)
    sides = jnp.where((lanes >= 32) & (lanes < 96), pltpu.roll(rest[8:16], 64, 1), rest[0:8])
    for ds, top in ((S - 1, rest[0:8]), (0, sides), (1, rest[8:16])):
        for dg in (G - 1, 0, 1):
            if ds or dg:
                send[lax.rem(s + ds, S) * G + lax.rem(g + dg, G)] = chunk(top)


def strip_kernel(
    level, recv, keep, frames, rows, out, held, v, moved, hot, main, over, window, table, around, sums, sems
):
    s = lax.axis_index("scan")
    g = lax.axis_index("grp")

    def part(i):
        return pltpu.make_async_copy(frames.at[pl.ds(i * YP, YP)], held.at[pl.ds(i * YP, YP)], sems.at[i])

    for i in range(PARTS):
        part(i).start()

    centers = jnp.zeros((8, 128), F32)
    feet = []
    for t in range(8):
        foot = jnp.zeros((8, 128), F32)
        for i in range(16):
            foot = foot + recv[16 * t + i].astype(F32)[8:16]
        feet.append(foot)
        centers = centers + foot
    mean = jnp.sum(jnp.where(iota((1, 128), 1) < 3, centers[2:3], 0.0), axis=1, keepdims=True) * (1.0 / N)
    total_row = jnp.zeros((1, 128), F32)
    for i, piece in enumerate(three_parts(mean * (SY * SX))):
        total_row = jnp.where(iota((1, 128), 1) == 96 + i, piece, total_row)

    def neighbour(ds, dg):
        got = recv[lax.rem(s + ds, S) * G + lax.rem(g + dg, G)].astype(F32)
        center = jnp.sum(jnp.where(iota((1, 128), 1) < 3, got[10:11], 0.0), axis=1, keepdims=True)
        return got[0:8] + (center - mean)

    for j, dg in enumerate((G - 1, 0, 1)):
        lanes = slice(128 * j, 128 * (j + 1))
        window[0:8, lanes] = neighbour(S - 1, dg)
        window[24:32, lanes] = neighbour(1, dg)
        if dg:
            side = neighbour(0, dg)
            window[8:16, lanes] = side
            window[16:24, lanes] = pltpu.roll(side, 64, 1)
        else:
            window[8:24, lanes] = keep[8:24, 0:128] - mean
    for b in range(16):
        table[b] = pltpu.roll(window[...], (b - 8) % 384, 1)[:, 128:256]

    row = iota((BX * 16, 128), 0)
    for t in range(8):
        sy = feet[t][0:1].astype(jnp.int32)
        sx = feet[t][1:2].astype(jnp.int32)
        code = ((sx >> 2) + 8) * 16 + (sx & 3) * 4 + (sy & 3)
        hot[:, 128 * t : 128 * (t + 1)] = (row == code).astype(F32).astype(BF16)

    for y in range(YS):
        for b in range(16):
            around[16 * b : 16 * (b + 1), 128 * y : 128 * (y + 1)] = table[b, y + 1 : y + 17, :].astype(BF16)
    for i in range(PARTS):
        part(i).wait()
        for y in range(i * YP, (i + 1) * YP):
            value = (held[y].astype(F32) - level[y] * keep[0:1, :]) * keep[1:2, :]
            v[y] = value.astype(BF16)
    out[:, 384:640] = lax.dot_general(
        v[...].reshape(YS * XS, BF), around[...], (((0,), (1,)), ((), ())), preferred_element_type=F32
    ).astype(BF16)

    for t in range(8):
        lanes = slice(128 * t, 128 * (t + 1))
        by = (feet[t][0:1].astype(jnp.int32) >> 2) + 8
        masks = [
            jnp.broadcast_to(((by >> b) & 1).astype(F32), (16, 128)).astype(BF16) > 0.5 for b in range(5)
        ]

        zero = jnp.zeros((16, 128), BF16)
        for x0 in range(0, XS, 16):
            rows_in = [v[y, x0 : x0 + 16, lanes] for y in range(YS)]
            for b in range(5):
                step = 1 << b
                size = min(len(rows_in) + step, 32)
                old = rows_in
                rows_in = [
                    jnp.where(
                        masks[b],
                        old[j - step] if 0 <= j - step < len(old) else zero,
                        old[j] if j < len(old) else zero,
                    )
                    for j in range(size)
                ]
            for j in range(32):
                moved[j, x0 : x0 + 16, lanes] = rows_in[j]

    lane = iota((16, 128), 1)

    for j in range(4):
        block = moved[8 * j : 8 * j + 8].reshape(8 * XS, BF)
        sums[j & 1] = lax.dot_general(hot[...], block, NT, preferred_element_type=F32)
        for h in range(8):
            lanes = slice(128 * h, 128 * (h + 1))
            acc_main = sums[j & 1, 0:16, lanes]
            acc_over = jnp.zeros((16, 128), F32)
            for b in range(1, BX):
                piece = pltpu.roll(sums[j & 1, 16 * b : 16 * (b + 1), lanes], b, 1)
                acc_main = acc_main + jnp.where(lane >= b, piece, 0.0)
                acc_over = acc_over + jnp.where(lane < b, piece, 0.0)
            main[8 * j + h] = acc_main
            over[8 * j + h] = acc_over

    sign_y = 1.0 - 2.0 * (iota((32, 16, 128), 0) & 1).astype(F32)
    sign_x = 1.0 - 2.0 * (iota((8, 128), 1) & 1).astype(F32)
    folded = jnp.sum((main[...] + over[...]) * sign_y, axis=0)
    folded = jnp.concatenate([jnp.zeros((64, 128), F32), folded, jnp.zeros((48, 128), F32)], axis=0)
    q_row = lax.dot_general(sign_x, folded, NT, precision=lax.Precision.HIGHEST, preferred_element_type=F32)[0:1]
    q_high = q_row.astype(BF16).astype(F32)
    q_row = q_high + pltpu.roll(q_row - q_high, 16, 1)

    col = iota((128, 512), 1)
    spread = ((iota((128, 512), 0) >> 2) == (col >> 4)) & ((iota((128, 512), 0) & 3) == (col & 3))
    left = jnp.dot(rows[...], spread.astype(F32).astype(BF16), preferred_element_type=F32)
    left = jnp.where(((iota((BF, 512), 0) >> 2) & 1) == ((iota((BF, 512), 1) >> 3) & 1), left, 0.0).astype(BF16)
    kind = (iota((512, 128), 0) >> 2) & 1
    u_main = main[...].reshape(512, 128)
    u_over = over[...].reshape(512, 128)
    first = jnp.where(kind == 0, u_over, 0.0)
    second = jnp.where(kind == 1, u_over, 0.0)
    right = jnp.concatenate(
        [
            jnp.where(kind == 0, u_main, 0.0),
            jnp.where(kind == 1, u_main, 0.0),
            first + pltpu.roll(second, 16, 1),
        ],
        axis=1,
    ).astype(BF16)
    z = jnp.dot(left, right, preferred_element_type=F32)
    z = jnp.concatenate([z[:, 0:256], z[:, 256:384] + (q_row + total_row)], axis=1).astype(BF16)
    for b in range(S):
        place = pl.multiple_of(64 * lax.rem(s + b, S), 64)
        out[pl.ds(place, 64), 0:384] = z[64 * b : 64 * (b + 1)]


def finish_kernel(recv, forward, inverse, phase, nyquist, out, corr_out, full):
    corr = jnp.zeros((8, 256), F32)
    sums = []
    for g in range(G):
        acc = jnp.zeros((8, 384), F32)
        for s in range(S):
            got = recv[s * G + g].astype(F32)
            acc = acc + got[:, 0:384]
            corr = corr + got[:, 384:640]
        sums.append(acc)
    n = iota((256, 256), 0)
    m = iota((256, 256), 1)
    order = ((n >> 4) == (m & 15)) & ((15 - (n & 15)) == (m >> 4))
    corr_out[...] = jnp.dot(
        corr * (1.0 / math.sqrt(BF * SY * SX)),
        order.astype(F32),
        precision=lax.Precision.HIGHEST,
        preferred_element_type=F32,
    )
    lane = iota((8, 128), 1)
    foot = recv[0].astype(F32)[:, 256:384]
    total = jnp.sum(jnp.where((lane >= 96) & (lane < 99), foot, 0.0), axis=1, keepdims=True)
    q_rows = jnp.zeros((8, 128), F32)
    for g in range(G):
        tail = sums[(g - 1) % G][:, 256:384]
        q_rows = q_rows + tail
        lanes = slice(128 * g, 128 * (g + 1))
        full[0:8, lanes] = sums[g][:, 0:128] + jnp.where(lane < 16, tail, 0.0)
        full[8:16, lanes] = sums[g][:, 128:256] + jnp.where(lane < 16, pltpu.roll(tail, 112, 1), 0.0)
    z0, z1, z2, z3 = (full[:, 256 * j : 256 * (j + 1)] for j in range(4))
    inputs = (
        (z0 + z1 + z2 + z3, None),
        (z0 - z2, z3 - z1),
        (z0 - z1 + z2 - z3, None),
        (z0 - z2, z1 - z3),
    )
    lane_e = iota((8, 128), 1)
    wave_cos = jnp.sum(q_rows * nyquist[0:8, :], axis=1, keepdims=True)
    wave_sin = jnp.sum(q_rows * nyquist[8:16, :], axis=1, keepdims=True)

    def both(value):
        return value + pltpu.roll(value, 4, 0)

    real_cos = jnp.zeros((8, 128), F32)
    real_sin = jnp.zeros((8, 128), F32)
    results = []
    for par, (real, imag) in enumerate(inputs):
        if imag is None:
            spec = jnp.dot(real.astype(BF16), forward[par], preferred_element_type=F32)
            cos_part, sin_part = spec[:, 0:128], spec[:, 128:256]
        else:
            stacked = jnp.concatenate([real, imag], axis=0).astype(BF16)
            spec = jnp.dot(stacked, forward[par], preferred_element_type=F32)
            cos_part = spec[0:16, 0:128] + spec[16:32, 128:256]
            sin_part = spec[0:16, 128:256] - spec[16:32, 0:128]
        re = jnp.zeros((8, 128), F32)
        im = jnp.zeros((8, 128), F32)
        for fxl in range(2):
            c = cos_part[8 * fxl : 8 * fxl + 8]
            s = sin_part[8 * fxl : 8 * fxl + 8]
            if par == 0:
                ny = s[:, 0:1]
                real_cos = real_cos + ny * nyquist[16 + 16 * fxl : 24 + 16 * fxl, :]
                real_sin = real_sin + ny * nyquist[24 + 16 * fxl : 32 + 16 * fxl, :]
                s = jnp.where(lane_e == 0, 0.0, s)
            pc = phase[32 * par + 8 * fxl : 32 * par + 8 * fxl + 8, :]
            ps = phase[32 * par + 16 + 8 * fxl : 32 * par + 24 + 8 * fxl, :]
            re = re + c * pc - s * ps
            im = im - (s * pc + c * ps)
        re = both(re)
        im = both(im)
        if par == 0:
            re = jnp.where(lane_e == 0, re - total * (1.0 / SY), re)
        coef = jnp.concatenate([re, im], axis=1)
        if imag is not None:
            coef = jnp.concatenate([coef, jnp.concatenate([im, -re], axis=1)], axis=0)
        results.append(jnp.dot(coef.astype(BF16), inverse[par], preferred_element_type=F32))
    wave_cos = wave_cos + both(real_cos)[:, 0:1]
    wave_sin = wave_sin + both(real_sin)[:, 0:1]
    turn = iota((8, 512), 1) & 3
    wave = wave_cos * jnp.where(turn == 0, 1.0, jnp.where(turn == 2, -1.0, 0.0))
    wave = wave + wave_sin * jnp.where(turn == 1, 1.0, jnp.where(turn == 3, -1.0, 0.0))
    scale = 1.0 / (SX * math.sqrt(BF))
    first = results[0] + wave
    e1, f1 = results[1][0:8], results[1][8:16]
    e3, f3 = results[3][0:8], results[3][8:16]
    quarters = (
        first + results[2] + e1 + e3,
        first - results[2] - f1 + f3,
        first + results[2] - e1 - e3,
        first - results[2] + f1 - f3,
    )
    for j, quarter in enumerate(quarters):
        out[:, 512 * j : 512 * (j + 1)] = (quarter * scale)[0:4]


def exchange(value):
    return lax.all_to_all(value, AXES, split_axis=0, concat_axis=0, tiled=True)


def limit(mib):
    return pltpu.CompilerParams(vmem_limit_bytes=mib * MIB)


def local(frames, dark_frame, gain_frame, bf_index, row_level, shift_num):
    smem = pl.BlockSpec(memory_space=pltpu.SMEM)
    vmem = pl.BlockSpec(memory_space=pltpu.VMEM)
    hbm = pl.BlockSpec(memory_space=pltpu.HBM)

    send, keep = pl.pallas_call(
        reference_kernel,
        in_specs=[smem, smem, hbm, vmem, vmem, vmem],
        out_specs=[vmem, vmem],
        out_shape=[
            jax.ShapeDtypeStruct((N, 16, 128), BF16),
            jax.ShapeDtypeStruct((24, BF), F32),
        ],
        scratch_shapes=[pltpu.VMEM((YS, XS, BF), BF16), pltpu.SemaphoreType.DMA((PARTS,))],
        compiler_params=limit(60),
        name="reference_image",
    )(
        row_level,
        shift_num,
        frames,
        dark_frame.reshape(ROWS, 128),
        gain_frame.reshape(ROWS, 128),
        bf_index.reshape(1, BF),
    )
    recv = exchange(send)
    sums = pl.pallas_call(
        strip_kernel,
        in_specs=[smem, vmem, vmem, hbm, vmem],
        out_specs=vmem,
        out_shape=jax.ShapeDtypeStruct((BF, 640), BF16),
        scratch_shapes=[
            pltpu.VMEM((YS, XS, BF), BF16),
            pltpu.VMEM((YS, XS, BF), BF16),
            pltpu.VMEM((32, XS, BF), BF16),
            pltpu.VMEM((BX * 16, BF), BF16),
            pltpu.VMEM((32, 16, 128), F32),
            pltpu.VMEM((32, 16, 128), F32),
            pltpu.VMEM((32, 384), F32),
            pltpu.VMEM((16, 32, 128), F32),
            pltpu.VMEM((256, YS * XS), BF16),
            pltpu.VMEM((2, BX * 16, BF), F32),
            pltpu.SemaphoreType.DMA((PARTS,)),
        ],
        compiler_params=limit(50),
        name="strip",
    )(row_level, recv, keep, frames, jnp.asarray(row_kernel()))
    parts = exchange(sums.reshape(N, 8, 640))
    tables = [jnp.asarray(t) for t in (*col_tables(), phase_tables(), nyquist_tables())]
    return pl.pallas_call(
        finish_kernel,
        in_specs=[vmem] * 5,
        out_specs=[vmem, vmem],
        out_shape=[
            jax.ShapeDtypeStruct((4, 2 * SX), F32),
            jax.ShapeDtypeStruct((8, 256), F32),
        ],
        scratch_shapes=[pltpu.VMEM((16, SX), F32)],
        compiler_params=limit(24),
        name="finish",
    )(parts, *tables)


def solution(mesh):
    return jax.shard_map(
        local,
        mesh=mesh,
        in_specs=(P("scan", "grp", None), P(), P(), P(), P("scan"), P(None, AXES)),
        out_specs=(P(AXES, None), P(AXES, None)),
        check_vma=False,
    )
```

```python
import math

import jax
import jax.numpy as jnp
import ml_dtypes
import numpy as np
from jax import lax
from jax.experimental import pallas as pl
from jax.experimental.pallas import tpu as pltpu
from jax.sharding import Mesh
from jax.sharding import PartitionSpec as P

SY = 256
SX = 1024
BF = 1024
DET = 36864
AXES = ("pair", "core", "grp")
S = 16
G = 8
N = S * G
YS = SY // S
XS = SX // G
ROWS = DET // 128
BX = 17
PARTS = 4
F32 = jnp.float32
BF16 = jnp.bfloat16
NT = (((1,), (1,)), ((), ()))
TN = (((0,), (0,)), ((), ()))
MIB = 1024 * 1024
YP = YS // PARTS


def iota(shape, dim):
    return lax.broadcasted_iota(jnp.int32, shape, dim)


def row_kernel():
    k = np.arange(-128, 128)
    q = np.arange(1024)
    d = np.cos(2 * np.pi * k[None, :] * q[:, None] / 1024).sum(1) / 256
    r = np.arange(1024)
    yp = 4 * (r // 8) + r % 4
    yy = np.repeat(np.arange(32), 4)
    fy = np.tile(np.arange(4), 32)
    return d[(2 * yp[:, None] - fy[None, :] - 4 * (yy[None, :] - 8)) % 1024].astype(ml_dtypes.bfloat16)


def col_tables():
    x = np.arange(256) - 8
    xp = np.arange(512)
    forward, inverse = [], []
    for par in range(4):
        k = 4 * np.arange(128) + par
        ang = 2 * np.pi * ((x[:, None] * k[None, :]) % 1024) / 1024
        c, s = np.cos(ang), np.sin(ang)
        if par == 0:
            s[:, 0] = np.where(x % 2 == 0, 1.0, -1.0)
        forward.append(np.concatenate([c, s], 1))
        w = np.where(k == 0, 1.0, 2.0)[:, None]
        ang = 2 * np.pi * ((k[:, None] * xp[None, :]) % 2048) / 2048
        inverse.append(np.concatenate([w * np.cos(ang), -w * np.sin(ang)], 0))
    return [np.stack(t).astype(ml_dtypes.bfloat16) for t in (forward, inverse)]


def phase_tables():
    out = np.zeros((4, 2, 2, 8, 128), np.float32)
    for par in range(4):
        k = 4 * np.arange(128) + par
        for fx in range(4):
            rows = slice(4 * (fx >> 1), 4 * (fx >> 1) + 4)
            out[par, 0, fx & 1, rows] = np.cos(2 * np.pi * k * fx / 4096)
            out[par, 1, fx & 1, rows] = np.sin(2 * np.pi * k * fx / 4096)
    return out.reshape(128, 128)


def nyquist_tables():
    w = np.zeros((2, 8, 128), np.float32)
    for i in range(8):
        for fx in range(4):
            for fy in range(4):
                sy = math.sin(math.pi * (2 * (i % 4) - fy) / 4) / 256
                for base in (64, 80):
                    w[0, i, base + fx * 4 + fy] = sy * math.sin(math.pi * fx / 4)
                    w[1, i, base + fx * 4 + fy] = -sy * math.cos(math.pi * fx / 4)
    v = np.zeros((2, 2, 8, 128), np.float32)
    for fx in range(4):
        rows = slice(4 * (fx >> 1), 4 * (fx >> 1) + 4)
        v[fx & 1, 0, rows] = math.cos(math.pi * fx / 4)
        v[fx & 1, 1, rows] = math.sin(math.pi * fx / 4)
    return np.concatenate([w.reshape(16, 128), v.reshape(32, 128)], 0)


def three_parts(value):
    high = value.astype(BF16).astype(F32)
    mid = (value - high).astype(BF16).astype(F32)
    return high, mid, value - high - mid


def reference_kernel(level, amounts, frames, dark, gain, index, send, keep, held, sems):
    def part(i):
        span = pl.ds(i * (YS // PARTS), YS // PARTS)
        return pltpu.make_async_copy(frames.at[span], held.at[span], sems.at[i])

    for i in range(PARTS):
        part(i).start()
    g = gain[...]
    table = jnp.concatenate(
        [dark[...].astype(F32), (g >> 5).astype(F32), (g & 31).astype(F32)], axis=1
    ).astype(BF16)
    idx = index[...]
    hot = (iota((ROWS, BF), 0) == (idx >> 7)).astype(F32).astype(BF16)
    picked = lax.dot_general(table, hot, TN, preferred_element_type=F32)
    mine = iota((128, BF), 0) == (idx & 127)

    def pick(i):
        return jnp.sum(jnp.where(mine, picked[128 * i : 128 * (i + 1)], 0.0), axis=0, keepdims=True)

    dark_px = pick(0) * (1.0 / 256.0)
    gain_px = (pick(1) * 32.0 + pick(2)) * (1.0 / 4096.0)
    keep[0:1, :] = dark_px
    keep[1:2, :] = gain_px
    offset = jnp.sum(dark_px * gain_px)
    for i in range(PARTS):
        part(i).wait()
        for y in range(i * (YS // PARTS), (i + 1) * (YS // PARTS)):
            acc = None
            for t in range(8):
                lanes = slice(128 * t, 128 * (t + 1))
                term = held[y, :, lanes].astype(F32) * gain_px[:, lanes]
                acc = term if acc is None else acc + term
            high = acc.astype(BF16)
            low = (acc - high.astype(F32)).astype(BF16)
            total = lax.dot_general(
                jnp.ones((8, 256), BF16), jnp.concatenate([high, low], 1), NT, preferred_element_type=F32
            )
            keep[8 + y : 9 + y, 0:128] = total[0:1] - level[y] * offset
    s = lax.axis_index("pair") * 2 + lax.axis_index("core")
    g = lax.axis_index("grp")
    r = keep[8:24, 0:128]
    center = jnp.sum(r) * (1.0 / (YS * XS))
    rest = r - center
    lane = iota((1, 128), 1)
    base = 8 * lax.rem(s * G + g, 16)
    row_sy = jnp.zeros((1, 128), F32)
    row_sx = jnp.zeros((1, 128), F32)
    for i in range(8):
        row_sy = jnp.where(lane == base + i, amounts[0, i].astype(F32), row_sy)
        row_sx = jnp.where(lane == base + i, amounts[1, i].astype(F32), row_sx)
    row_center = jnp.zeros((1, 128), F32)
    for i, piece in enumerate(three_parts(jnp.full((1, 128), center))):
        row_center = jnp.where(lane == i, piece, row_center)
    foot = jnp.concatenate([row_sy, row_sx, row_center, jnp.zeros((5, 128), F32)], axis=0)

    def chunk(top):
        return jnp.concatenate([top, foot], axis=0).astype(BF16)

    plain = chunk(jnp.zeros((8, 128), F32))
    for d in range(N):
        send[d] = plain
    lanes = iota((8, 128), 1)
    sides = jnp.where((lanes >= 32) & (lanes < 96), pltpu.roll(rest[8:16], 64, 1), rest[0:8])
    for ds, top in ((S - 1, rest[0:8]), (0, sides), (1, rest[8:16])):
        for dg in (G - 1, 0, 1):
            if ds or dg:
                send[lax.rem(s + ds, S) * G + lax.rem(g + dg, G)] = chunk(top)


def strip_kernel(
    level, recv, keep, frames, rows, mine, theirs, corr, held, v, moved, hot, main, over, window, table, around, sums, sems
):
    s = lax.axis_index("pair") * 2 + lax.axis_index("core")
    g = lax.axis_index("grp")

    def part(i):
        return pltpu.make_async_copy(frames.at[pl.ds(i * YP, YP)], held.at[pl.ds(i * YP, YP)], sems.at[i])

    for i in range(PARTS):
        part(i).start()

    centers = jnp.zeros((8, 128), F32)
    feet = []
    for t in range(8):
        foot = jnp.zeros((8, 128), F32)
        for i in range(16):
            foot = foot + recv[16 * t + i].astype(F32)[8:16]
        feet.append(foot)
        centers = centers + foot
    mean = jnp.sum(jnp.where(iota((1, 128), 1) < 3, centers[2:3], 0.0), axis=1, keepdims=True) * (1.0 / N)
    total_row = jnp.zeros((1, 128), F32)
    for i, piece in enumerate(three_parts(mean * (SY * SX))):
        total_row = jnp.where(iota((1, 128), 1) == 96 + i, piece, total_row)

    def neighbour(ds, dg):
        got = recv[lax.rem(s + ds, S) * G + lax.rem(g + dg, G)].astype(F32)
        center = jnp.sum(jnp.where(iota((1, 128), 1) < 3, got[10:11], 0.0), axis=1, keepdims=True)
        return got[0:8] + (center - mean)

    for j, dg in enumerate((G - 1, 0, 1)):
        lanes = slice(128 * j, 128 * (j + 1))
        window[0:8, lanes] = neighbour(S - 1, dg)
        window[24:32, lanes] = neighbour(1, dg)
        if dg:
            side = neighbour(0, dg)
            window[8:16, lanes] = side
            window[16:24, lanes] = pltpu.roll(side, 64, 1)
        else:
            window[8:24, lanes] = keep[8:24, 0:128] - mean
    for b in range(16):
        table[b] = pltpu.roll(window[...], (b - 8) % 384, 1)[:, 128:256]

    row = iota((BX * 16, 128), 0)
    for t in range(8):
        sy = feet[t][0:1].astype(jnp.int32)
        sx = feet[t][1:2].astype(jnp.int32)
        code = ((sx >> 2) + 8) * 16 + (sx & 3) * 4 + (sy & 3)
        hot[:, 128 * t : 128 * (t + 1)] = (row == code).astype(F32).astype(BF16)

    for y in range(YS):
        for b in range(16):
            around[16 * b : 16 * (b + 1), 128 * y : 128 * (y + 1)] = table[b, y + 1 : y + 17, :].astype(BF16)
    for i in range(PARTS):
        part(i).wait()
        for y in range(i * YP, (i + 1) * YP):
            value = (held[y].astype(F32) - level[y] * keep[0:1, :]) * keep[1:2, :]
            v[y] = value.astype(BF16)
    corr[...] = lax.dot_general(
        v[...].reshape(YS * XS, BF), around[...], (((0,), (1,)), ((), ())), preferred_element_type=F32
    ).astype(BF16)
    core = lax.axis_index("core")
    for a in range(S // 2):
        for to, c in ((mine, core), (theirs, 1 - core)):
            to[64 * a : 64 * (a + 1), 384:640] = corr[pl.ds(pl.multiple_of(64 * (2 * a + c), 64), 64), :]

    for t in range(8):
        lanes = slice(128 * t, 128 * (t + 1))
        by = (feet[t][0:1].astype(jnp.int32) >> 2) + 8
        masks = [
            jnp.broadcast_to(((by >> b) & 1).astype(F32), (16, 128)).astype(BF16) > 0.5 for b in range(5)
        ]

        zero = jnp.zeros((16, 128), BF16)
        for x0 in range(0, XS, 16):
            rows_in = [v[y, x0 : x0 + 16, lanes] for y in range(YS)]
            for b in range(5):
                step = 1 << b
                size = min(len(rows_in) + step, 32)
                old = rows_in
                rows_in = [
                    jnp.where(
                        masks[b],
                        old[j - step] if 0 <= j - step < len(old) else zero,
                        old[j] if j < len(old) else zero,
                    )
                    for j in range(size)
                ]
            for j in range(32):
                moved[j, x0 : x0 + 16, lanes] = rows_in[j]

    lane = iota((16, 128), 1)

    for j in range(4):
        block = moved[8 * j : 8 * j + 8].reshape(8 * XS, BF)
        sums[j & 1] = lax.dot_general(hot[...], block, NT, preferred_element_type=F32)
        for h in range(8):
            lanes = slice(128 * h, 128 * (h + 1))
            acc_main = sums[j & 1, 0:16, lanes]
            acc_over = jnp.zeros((16, 128), F32)
            for b in range(1, BX):
                piece = pltpu.roll(sums[j & 1, 16 * b : 16 * (b + 1), lanes], b, 1)
                acc_main = acc_main + jnp.where(lane >= b, piece, 0.0)
                acc_over = acc_over + jnp.where(lane < b, piece, 0.0)
            main[8 * j + h] = acc_main
            over[8 * j + h] = acc_over

    sign_y = 1.0 - 2.0 * (iota((32, 16, 128), 0) & 1).astype(F32)
    sign_x = 1.0 - 2.0 * (iota((8, 128), 1) & 1).astype(F32)
    folded = jnp.sum((main[...] + over[...]) * sign_y, axis=0)
    folded = jnp.concatenate([jnp.zeros((64, 128), F32), folded, jnp.zeros((48, 128), F32)], axis=0)
    q_row = lax.dot_general(sign_x, folded, NT, precision=lax.Precision.HIGHEST, preferred_element_type=F32)[0:1]
    q_high = q_row.astype(BF16).astype(F32)
    q_row = q_high + pltpu.roll(q_row - q_high, 16, 1)

    col = iota((128, 512), 1)
    spread = ((iota((128, 512), 0) >> 2) == (col >> 4)) & ((iota((128, 512), 0) & 3) == (col & 3))
    left = jnp.dot(rows[...], spread.astype(F32).astype(BF16), preferred_element_type=F32)
    left = jnp.where(((iota((BF, 512), 0) >> 2) & 1) == ((iota((BF, 512), 1) >> 3) & 1), left, 0.0).astype(BF16)
    kind = (iota((512, 128), 0) >> 2) & 1
    u_main = main[...].reshape(512, 128)
    u_over = over[...].reshape(512, 128)
    first = jnp.where(kind == 0, u_over, 0.0)
    second = jnp.where(kind == 1, u_over, 0.0)
    right = jnp.concatenate(
        [
            jnp.where(kind == 0, u_main, 0.0),
            jnp.where(kind == 1, u_main, 0.0),
            first + pltpu.roll(second, 16, 1),
        ],
        axis=1,
    ).astype(BF16)
    z = jnp.dot(left, right, preferred_element_type=F32)
    z = jnp.concatenate([z[:, 0:256], z[:, 256:384] + (q_row + total_row)], axis=1).astype(BF16)
    for b in range(S):
        place = pl.multiple_of(64 * (lax.rem(s + b, S) >> 1), 64)
        to = theirs if b & 1 else mine
        to[pl.ds(place, 64), 0:384] = z[64 * b : 64 * (b + 1)]


def finish_kernel(recv, forward, inverse, phase, nyquist, out, corr_out, full):
    corr = jnp.zeros((8, 256), F32)
    sums = []
    for g in range(G):
        acc = jnp.zeros((8, 384), F32)
        for a in range(S // 2):
            got = recv[a * G + g].astype(F32)
            acc = acc + got[:, 0:384]
            corr = corr + got[:, 384:640]
        sums.append(acc)
    n = iota((256, 256), 0)
    m = iota((256, 256), 1)
    order = ((n >> 4) == (m & 15)) & ((15 - (n & 15)) == (m >> 4))
    corr_out[...] = jnp.dot(
        corr * (1.0 / math.sqrt(BF * SY * SX)),
        order.astype(F32),
        precision=lax.Precision.HIGHEST,
        preferred_element_type=F32,
    )
    lane = iota((8, 128), 1)
    foot = recv[0].astype(F32)[:, 256:384]
    total = jnp.sum(jnp.where((lane >= 96) & (lane < 99), foot, 0.0), axis=1, keepdims=True) * 0.5
    q_rows = jnp.zeros((8, 128), F32)
    for g in range(G):
        tail = sums[(g - 1) % G][:, 256:384]
        q_rows = q_rows + tail
        lanes = slice(128 * g, 128 * (g + 1))
        full[0:8, lanes] = sums[g][:, 0:128] + jnp.where(lane < 16, tail, 0.0)
        full[8:16, lanes] = sums[g][:, 128:256] + jnp.where(lane < 16, pltpu.roll(tail, 112, 1), 0.0)
    z0, z1, z2, z3 = (full[:, 256 * j : 256 * (j + 1)] for j in range(4))
    inputs = (
        (z0 + z1 + z2 + z3, None),
        (z0 - z2, z3 - z1),
        (z0 - z1 + z2 - z3, None),
        (z0 - z2, z1 - z3),
    )
    lane_e = iota((8, 128), 1)
    wave_cos = jnp.sum(q_rows * nyquist[0:8, :], axis=1, keepdims=True)
    wave_sin = jnp.sum(q_rows * nyquist[8:16, :], axis=1, keepdims=True)

    def both(value):
        return value + pltpu.roll(value, 4, 0)

    real_cos = jnp.zeros((8, 128), F32)
    real_sin = jnp.zeros((8, 128), F32)
    results = []
    for par, (real, imag) in enumerate(inputs):
        if imag is None:
            spec = jnp.dot(real.astype(BF16), forward[par], preferred_element_type=F32)
            cos_part, sin_part = spec[:, 0:128], spec[:, 128:256]
        else:
            stacked = jnp.concatenate([real, imag], axis=0).astype(BF16)
            spec = jnp.dot(stacked, forward[par], preferred_element_type=F32)
            cos_part = spec[0:16, 0:128] + spec[16:32, 128:256]
            sin_part = spec[0:16, 128:256] - spec[16:32, 0:128]
        re = jnp.zeros((8, 128), F32)
        im = jnp.zeros((8, 128), F32)
        for fxl in range(2):
            c = cos_part[8 * fxl : 8 * fxl + 8]
            s = sin_part[8 * fxl : 8 * fxl + 8]
            if par == 0:
                ny = s[:, 0:1]
                real_cos = real_cos + ny * nyquist[16 + 16 * fxl : 24 + 16 * fxl, :]
                real_sin = real_sin + ny * nyquist[24 + 16 * fxl : 32 + 16 * fxl, :]
                s = jnp.where(lane_e == 0, 0.0, s)
            pc = phase[32 * par + 8 * fxl : 32 * par + 8 * fxl + 8, :]
            ps = phase[32 * par + 16 + 8 * fxl : 32 * par + 24 + 8 * fxl, :]
            re = re + c * pc - s * ps
            im = im - (s * pc + c * ps)
        re = both(re)
        im = both(im)
        if par == 0:
            re = jnp.where(lane_e == 0, re - total * (1.0 / SY), re)
        coef = jnp.concatenate([re, im], axis=1)
        if imag is not None:
            coef = jnp.concatenate([coef, jnp.concatenate([im, -re], axis=1)], axis=0)
        results.append(jnp.dot(coef.astype(BF16), inverse[par], preferred_element_type=F32))
    wave_cos = wave_cos + both(real_cos)[:, 0:1]
    wave_sin = wave_sin + both(real_sin)[:, 0:1]
    turn = iota((8, 512), 1) & 3
    wave = wave_cos * jnp.where(turn == 0, 1.0, jnp.where(turn == 2, -1.0, 0.0))
    wave = wave + wave_sin * jnp.where(turn == 1, 1.0, jnp.where(turn == 3, -1.0, 0.0))
    scale = 1.0 / (SX * math.sqrt(BF))
    first = results[0] + wave
    e1, f1 = results[1][0:8], results[1][8:16]
    e3, f3 = results[3][0:8], results[3][8:16]
    quarters = (
        first + results[2] + e1 + e3,
        first - results[2] - f1 + f3,
        first + results[2] - e1 - e3,
        first - results[2] + f1 - f3,
    )
    for j, quarter in enumerate(quarters):
        out[:, 512 * j : 512 * (j + 1)] = (quarter * scale)[0:4]


def exchange(value, axes):
    return lax.all_to_all(value, axes, split_axis=0, concat_axis=0, tiled=True)


def limit(mib):
    return pltpu.CompilerParams(vmem_limit_bytes=mib * MIB)


def local(frames, dark_frame, gain_frame, bf_index, row_level, shift_num):
    smem = pl.BlockSpec(memory_space=pltpu.SMEM)
    vmem = pl.BlockSpec(memory_space=pltpu.VMEM)
    hbm = pl.BlockSpec(memory_space=pltpu.HBM)

    send, keep = pl.pallas_call(
        reference_kernel,
        in_specs=[smem, smem, hbm, vmem, vmem, vmem],
        out_specs=[vmem, vmem],
        out_shape=[
            jax.ShapeDtypeStruct((N, 16, 128), BF16),
            jax.ShapeDtypeStruct((24, BF), F32),
        ],
        scratch_shapes=[pltpu.VMEM((YS, XS, BF), BF16), pltpu.SemaphoreType.DMA((PARTS,))],
        compiler_params=limit(60),
        name="reference_image",
    )(
        row_level,
        shift_num,
        frames,
        dark_frame.reshape(ROWS, 128),
        gain_frame.reshape(ROWS, 128),
        bf_index.reshape(1, BF),
    )
    recv = exchange(send, AXES)
    mine, theirs = pl.pallas_call(
        strip_kernel,
        in_specs=[smem, vmem, vmem, hbm, vmem],
        out_specs=[vmem, vmem],
        out_shape=[jax.ShapeDtypeStruct((BF // 2, 640), BF16)] * 2,
        scratch_shapes=[
            pltpu.VMEM((BF, 256), BF16),
            pltpu.VMEM((YS, XS, BF), BF16),
            pltpu.VMEM((YS, XS, BF), BF16),
            pltpu.VMEM((32, XS, BF), BF16),
            pltpu.VMEM((BX * 16, BF), BF16),
            pltpu.VMEM((32, 16, 128), F32),
            pltpu.VMEM((32, 16, 128), F32),
            pltpu.VMEM((32, 384), F32),
            pltpu.VMEM((16, 32, 128), F32),
            pltpu.VMEM((256, YS * XS), BF16),
            pltpu.VMEM((2, BX * 16, BF), F32),
            pltpu.SemaphoreType.DMA((PARTS,)),
        ],
        compiler_params=limit(50),
        name="strip",
    )(row_level, recv, keep, frames, jnp.asarray(row_kernel()))
    swapped = lax.ppermute(theirs, "core", [(0, 1), (1, 0)])
    both = (mine.astype(F32) + swapped.astype(F32)).astype(BF16)
    parts = exchange(both.reshape(N // 2, 8, 640), ("pair", "grp"))
    tables = [jnp.asarray(t) for t in (*col_tables(), phase_tables(), nyquist_tables())]
    return pl.pallas_call(
        finish_kernel,
        in_specs=[vmem] * 5,
        out_specs=[vmem, vmem],
        out_shape=[
            jax.ShapeDtypeStruct((4, 2 * SX), F32),
            jax.ShapeDtypeStruct((8, 256), F32),
        ],
        scratch_shapes=[pltpu.VMEM((16, SX), F32)],
        compiler_params=limit(24),
        name="finish",
    )(parts, *tables)


def solution(mesh):
    scan = ("pair", "core")
    return jax.shard_map(
        local,
        mesh=Mesh(mesh.devices.reshape(S // 2, 2, G), AXES),
        in_specs=(P(scan, "grp", None), P(), P(), P(), P(scan), P(None, AXES)),
        out_specs=(P(AXES, None), P(AXES, None)),
        check_vma=False,
    )
```

```python
import math

import jax
import jax.numpy as jnp
import ml_dtypes
import numpy as np
from jax import lax
from jax.experimental import pallas as pl
from jax.experimental.pallas import tpu as pltpu
from jax.sharding import Mesh
from jax.sharding import PartitionSpec as P

SY = 256
SX = 1024
BF = 1024
DET = 36864
AXES = ("pair", "core", "grp")
S = 16
G = 8
N = S * G
YS = SY // S
XS = SX // G
ROWS = DET // 128
BX = 17
PARTS = 4
F32 = jnp.float32
BF16 = jnp.bfloat16
NT = (((1,), (1,)), ((), ()))
TN = (((0,), (0,)), ((), ()))
MIB = 1024 * 1024
YP = YS // PARTS
FOOT = 32
KEEP_ROWS = 1024


def iota(shape, dim):
    return lax.broadcasted_iota(jnp.int32, shape, dim)


def row_kernel():
    k = np.arange(-128, 128)
    q = np.arange(1024)
    d = np.cos(2 * np.pi * k[None, :] * q[:, None] / 1024).sum(1) / 256
    r = np.arange(1024)
    yp = 4 * (r // 8) + r % 4
    yy = np.repeat(np.arange(32), 4)
    fy = np.tile(np.arange(4), 32)
    return d[(2 * yp[:, None] - fy[None, :] - 4 * (yy[None, :] - 8)) % 1024].astype(ml_dtypes.bfloat16)


def col_tables():
    x = np.arange(256) - 8
    xp = np.arange(512)
    forward, inverse = [], []
    for par in range(4):
        k = 4 * np.arange(128) + par
        ang = 2 * np.pi * ((x[:, None] * k[None, :]) % 1024) / 1024
        c, s = np.cos(ang), np.sin(ang)
        if par == 0:
            s[:, 0] = np.where(x % 2 == 0, 1.0, -1.0)
        forward.append(np.concatenate([c, s], 1))
        w = np.where(k == 0, 1.0, 2.0)[:, None]
        ang = 2 * np.pi * ((k[:, None] * xp[None, :]) % 2048) / 2048
        inverse.append(np.concatenate([w * np.cos(ang), -w * np.sin(ang)], 0))
    return [np.stack(t).astype(ml_dtypes.bfloat16) for t in (forward, inverse)]


def phase_tables():
    out = np.zeros((4, 2, 2, 8, 128), np.float32)
    for par in range(4):
        k = 4 * np.arange(128) + par
        for fx in range(4):
            rows = slice(4 * (fx >> 1), 4 * (fx >> 1) + 4)
            out[par, 0, fx & 1, rows] = np.cos(2 * np.pi * k * fx / 4096)
            out[par, 1, fx & 1, rows] = np.sin(2 * np.pi * k * fx / 4096)
    return out.reshape(128, 128)


def nyquist_tables():
    w = np.zeros((2, 8, 128), np.float32)
    for i in range(8):
        for fx in range(4):
            for fy in range(4):
                sy = math.sin(math.pi * (2 * (i % 4) - fy) / 4) / 256
                for base in (64, 80):
                    w[0, i, base + fx * 4 + fy] = sy * math.sin(math.pi * fx / 4)
                    w[1, i, base + fx * 4 + fy] = -sy * math.cos(math.pi * fx / 4)
    v = np.zeros((2, 2, 8, 128), np.float32)
    for fx in range(4):
        rows = slice(4 * (fx >> 1), 4 * (fx >> 1) + 4)
        v[fx & 1, 0, rows] = math.cos(math.pi * fx / 4)
        v[fx & 1, 1, rows] = math.sin(math.pi * fx / 4)
    return np.concatenate([w.reshape(16, 128), v.reshape(32, 128)], 0)


def three_parts(value):
    high = value.astype(BF16).astype(F32)
    mid = (value - high).astype(BF16).astype(F32)
    return high, mid, value - high - mid


def reference_kernel(
    level, amounts, frames, dark, gain, index, send, foot_out, keep_out, held, keep, sems, keep_sems
):
    def stay(i):
        span = pl.ds(8 * i, 8 + 8 * i)
        return pltpu.make_async_copy(keep.at[span], keep_out.at[span], keep_sems.at[i])

    def part(i):
        span = pl.ds(i * (YS // PARTS), YS // PARTS)
        return pltpu.make_async_copy(frames.at[span], held.at[span], sems.at[i])

    for i in range(PARTS):
        part(i).start()
    g = gain[...]
    table = jnp.concatenate(
        [dark[...].astype(F32), (g >> 5).astype(F32), (g & 31).astype(F32)], axis=1
    ).astype(BF16)
    idx = index[...]
    hot = (iota((ROWS, BF), 0) == (idx >> 7)).astype(F32).astype(BF16)
    picked = lax.dot_general(table, hot, TN, preferred_element_type=F32)
    mine = iota((128, BF), 0) == (idx & 127)

    def pick(i):
        return jnp.sum(jnp.where(mine, picked[128 * i : 128 * (i + 1)], 0.0), axis=0, keepdims=True)

    dark_px = pick(0) * (1.0 / 256.0)
    gain_px = (pick(1) * 32.0 + pick(2)) * (1.0 / 4096.0)
    keep[0:1, :] = dark_px
    keep[1:2, :] = gain_px
    stay(0).start()
    offset = jnp.sum(dark_px * gain_px)
    for i in range(PARTS):
        part(i).wait()
        for y in range(i * (YS // PARTS), (i + 1) * (YS // PARTS)):
            acc = None
            for t in range(8):
                lanes = slice(128 * t, 128 * (t + 1))
                term = held[y, :, lanes].astype(F32) * gain_px[:, lanes]
                acc = term if acc is None else acc + term
            high = acc.astype(BF16)
            low = (acc - high.astype(F32)).astype(BF16)
            total = lax.dot_general(
                jnp.ones((8, 256), BF16), jnp.concatenate([high, low], 1), NT, preferred_element_type=F32
            )
            keep[8 + y : 9 + y, 0:128] = total[0:1] - level[y] * offset
    stay(1).start()
    s = lax.axis_index("pair") * 2 + lax.axis_index("core")
    g = lax.axis_index("grp")
    r = keep[8:24, 0:128]
    center = jnp.sum(r) * (1.0 / (YS * XS))
    rest = r - center
    lane = iota((8, 128), 1)
    top = iota((8, 128), 0) == 0
    foot = jnp.zeros((8, 128), F32)
    for i in range(8):
        foot = jnp.where(lane == FOOT + i, amounts[0, i].astype(F32), foot)
        foot = jnp.where(lane == FOOT + 8 + i, amounts[1, i].astype(F32), foot)
    for i, piece in enumerate(three_parts(jnp.full((8, 128), center))):
        foot = jnp.where(lane == FOOT + 16 + i, piece, foot)
    foot = jnp.where(top, foot, 0.0)
    foot_out[...] = foot.astype(BF16)
    plain = foot.astype(BF16)
    for d in range(N):
        send[d] = plain
    here = top & (lane >= FOOT) & (lane < FOOT + 24)
    first = rest[0:8]
    last = jnp.where(top, foot, rest[8:16])
    sides = jnp.where((lane >= 32) & (lane < 96), pltpu.roll(rest[8:16], 64, 1), first)
    for ds, block in ((S - 1, first), (0, sides), (1, last)):
        for dg in (G - 1, 0, 1):
            if ds or dg:
                whole = block if ds == S - 1 and dg == 0 else jnp.where(here, foot, block)
                send[lax.rem(s + ds, S) * G + lax.rem(g + dg, G)] = whole.astype(BF16)
    for i in range(2):
        stay(i).wait()


def strip_kernel(
    level, recv, below, keep_hbm, frames, rows, mine, theirs, corr, keep, feet, held, v, moved, hot, main, over, window, table, around, sums, sems, keep_sem
):
    s = lax.axis_index("pair") * 2 + lax.axis_index("core")
    g = lax.axis_index("grp")

    def part(i):
        return pltpu.make_async_copy(frames.at[pl.ds(i * YP, YP)], held.at[pl.ds(i * YP, YP)], sems.at[i])

    for i in range(PARTS):
        part(i).start()

    kept = pltpu.make_async_copy(keep_hbm.at[pl.ds(0, 24)], keep, keep_sem)
    kept.start()

    for d in range(N):
        feet[d : d + 1, :] = recv[d].astype(F32)[0:1, :]
    feet[pl.ds(lax.rem(s + 1, S) * G + g, 1), :] = below[...].astype(F32)[0:1, :]
    lane = iota((N, 128), 1)
    means = jnp.where((lane >= FOOT + 16) & (lane < FOOT + 19), feet[...], 0.0)
    mean = jnp.sum(jnp.sum(means, axis=0, keepdims=True), axis=1, keepdims=True) * (1.0 / N)
    total_row = jnp.zeros((1, 128), F32)
    for i, piece in enumerate(three_parts(mean * (SY * SX))):
        total_row = jnp.where(iota((1, 128), 1) == 96 + i, piece, total_row)
    wide = iota((128, 256), 1)
    pick = iota((128, 256), 0) == FOOT + 8 * (wide >> 7) + (wide & 7)
    shifts = jnp.dot(feet[...].astype(BF16), pick.astype(F32).astype(BF16), preferred_element_type=F32)
    shifts = jnp.where((iota((N, 256), 0) & 15) == ((wide & 127) >> 3), shifts, 0.0)
    shifts = jnp.sum(shifts.reshape(8, 16, 256), axis=1).astype(jnp.int32)
    kept.wait()

    def neighbour(ds, dg):
        src = lax.rem(s + ds, S) * G + lax.rem(g + dg, G)
        spot = iota((1, 128), 1)
        row = jnp.where((spot >= FOOT + 16) & (spot < FOOT + 19), feet[pl.ds(src, 1), :], 0.0)
        return recv[src].astype(F32) + (jnp.sum(row, axis=1, keepdims=True) - mean)

    for j, dg in enumerate((G - 1, 0, 1)):
        lanes = slice(128 * j, 128 * (j + 1))
        window[0:8, lanes] = neighbour(S - 1, dg)
        window[24:32, lanes] = neighbour(1, dg)
        if dg:
            side = neighbour(0, dg)
            window[8:16, lanes] = side
            window[16:24, lanes] = pltpu.roll(side, 64, 1)
        else:
            window[8:24, lanes] = keep[8:24, 0:128] - mean
    for b in range(16):
        table[b] = pltpu.roll(window[...], (b - 8) % 384, 1)[:, 128:256]

    row = iota((BX * 16, 128), 0)
    for t in range(8):
        sy = shifts[t : t + 1, 0:128]
        sx = shifts[t : t + 1, 128:256]
        code = ((sx >> 2) + 8) * 16 + (sx & 3) * 4 + (sy & 3)
        hot[:, 128 * t : 128 * (t + 1)] = (row == code).astype(F32).astype(BF16)

    for y in range(YS):
        for b in range(16):
            around[16 * b : 16 * (b + 1), 128 * y : 128 * (y + 1)] = table[b, y + 1 : y + 17, :].astype(BF16)
    for i in range(PARTS):
        part(i).wait()
        for y in range(i * YP, (i + 1) * YP):
            value = (held[y].astype(F32) - level[y] * keep[0:1, :]) * keep[1:2, :]
            v[y] = value.astype(BF16)
    corr[...] = lax.dot_general(
        v[...].reshape(YS * XS, BF), around[...], (((0,), (1,)), ((), ())), preferred_element_type=F32
    ).astype(BF16)
    core = lax.axis_index("core")
    for a in range(S // 2):
        for to, c in ((mine, core), (theirs, 1 - core)):
            to[64 * a : 64 * (a + 1), 384:640] = corr[pl.ds(pl.multiple_of(64 * (2 * a + c), 64), 64), :]

    for t in range(8):
        lanes = slice(128 * t, 128 * (t + 1))
        by = (shifts[t : t + 1, 0:128] >> 2) + 8
        masks = [
            jnp.broadcast_to(((by >> b) & 1).astype(F32), (16, 128)).astype(BF16) > 0.5 for b in range(5)
        ]

        zero = jnp.zeros((16, 128), BF16)
        for x0 in range(0, XS, 16):
            rows_in = [v[y, x0 : x0 + 16, lanes] for y in range(YS)]
            for b in range(5):
                step = 1 << b
                size = min(len(rows_in) + step, 32)
                old = rows_in
                rows_in = [
                    jnp.where(
                        masks[b],
                        old[j - step] if 0 <= j - step < len(old) else zero,
                        old[j] if j < len(old) else zero,
                    )
                    for j in range(size)
                ]
            for j in range(32):
                moved[j, x0 : x0 + 16, lanes] = rows_in[j]

    lane = iota((16, 128), 1)

    for j in range(4):
        block = moved[8 * j : 8 * j + 8].reshape(8 * XS, BF)
        sums[j & 1] = lax.dot_general(hot[...], block, NT, preferred_element_type=F32)
        for h in range(8):
            lanes = slice(128 * h, 128 * (h + 1))
            acc_main = sums[j & 1, 0:16, lanes]
            acc_over = jnp.zeros((16, 128), F32)
            for b in range(1, BX):
                piece = pltpu.roll(sums[j & 1, 16 * b : 16 * (b + 1), lanes], b, 1)
                acc_main = acc_main + jnp.where(lane >= b, piece, 0.0)
                acc_over = acc_over + jnp.where(lane < b, piece, 0.0)
            main[8 * j + h] = acc_main
            over[8 * j + h] = acc_over

    sign_y = 1.0 - 2.0 * (iota((32, 16, 128), 0) & 1).astype(F32)
    sign_x = 1.0 - 2.0 * (iota((8, 128), 1) & 1).astype(F32)
    folded = jnp.sum((main[...] + over[...]) * sign_y, axis=0)
    folded = jnp.concatenate([jnp.zeros((64, 128), F32), folded, jnp.zeros((48, 128), F32)], axis=0)
    q_row = lax.dot_general(sign_x, folded, NT, precision=lax.Precision.HIGHEST, preferred_element_type=F32)[0:1]
    q_high = q_row.astype(BF16).astype(F32)
    q_row = q_high + pltpu.roll(q_row - q_high, 16, 1)

    col = iota((128, 512), 1)
    spread = ((iota((128, 512), 0) >> 2) == (col >> 4)) & ((iota((128, 512), 0) & 3) == (col & 3))
    left = jnp.dot(rows[...], spread.astype(F32).astype(BF16), preferred_element_type=F32)
    left = jnp.where(((iota((BF, 512), 0) >> 2) & 1) == ((iota((BF, 512), 1) >> 3) & 1), left, 0.0).astype(BF16)
    kind = (iota((512, 128), 0) >> 2) & 1
    u_main = main[...].reshape(512, 128)
    u_over = over[...].reshape(512, 128)
    first = jnp.where(kind == 0, u_over, 0.0)
    second = jnp.where(kind == 1, u_over, 0.0)
    right = jnp.concatenate(
        [
            jnp.where(kind == 0, u_main, 0.0),
            jnp.where(kind == 1, u_main, 0.0),
            first + pltpu.roll(second, 16, 1),
        ],
        axis=1,
    ).astype(BF16)
    z = jnp.dot(left, right, preferred_element_type=F32)
    z = jnp.concatenate([z[:, 0:256], z[:, 256:384] + (q_row + total_row)], axis=1).astype(BF16)
    for b in range(S):
        place = pl.multiple_of(64 * (lax.rem(s + b, S) >> 1), 64)
        to = theirs if b & 1 else mine
        to[pl.ds(place, 64), 0:384] = z[64 * b : 64 * (b + 1)]


def finish_kernel(recv, forward, inverse, phase, nyquist, out, corr_out, full):
    corr = jnp.zeros((8, 256), F32)
    sums = []
    for g in range(G):
        acc = jnp.zeros((8, 384), F32)
        for a in range(S // 2):
            got = recv[a * G + g].astype(F32)
            acc = acc + got[:, 0:384]
            corr = corr + got[:, 384:640]
        sums.append(acc)
    n = iota((256, 256), 0)
    m = iota((256, 256), 1)
    order = ((n >> 4) == (m & 15)) & ((15 - (n & 15)) == (m >> 4))
    corr_out[...] = jnp.dot(
        corr * (1.0 / math.sqrt(BF * SY * SX)),
        order.astype(F32),
        precision=lax.Precision.HIGHEST,
        preferred_element_type=F32,
    )
    lane = iota((8, 128), 1)
    foot = recv[0].astype(F32)[:, 256:384]
    total = jnp.sum(jnp.where((lane >= 96) & (lane < 99), foot, 0.0), axis=1, keepdims=True) * 0.5
    q_rows = jnp.zeros((8, 128), F32)
    for g in range(G):
        tail = sums[(g - 1) % G][:, 256:384]
        q_rows = q_rows + tail
        lanes = slice(128 * g, 128 * (g + 1))
        full[0:8, lanes] = sums[g][:, 0:128] + jnp.where(lane < 16, tail, 0.0)
        full[8:16, lanes] = sums[g][:, 128:256] + jnp.where(lane < 16, pltpu.roll(tail, 112, 1), 0.0)
    z0, z1, z2, z3 = (full[:, 256 * j : 256 * (j + 1)] for j in range(4))
    inputs = (
        (z0 + z1 + z2 + z3, None),
        (z0 - z2, z3 - z1),
        (z0 - z1 + z2 - z3, None),
        (z0 - z2, z1 - z3),
    )
    lane_e = iota((8, 128), 1)
    wave_cos = jnp.sum(q_rows * nyquist[0:8, :], axis=1, keepdims=True)
    wave_sin = jnp.sum(q_rows * nyquist[8:16, :], axis=1, keepdims=True)

    def both(value):
        return value + pltpu.roll(value, 4, 0)

    real_cos = jnp.zeros((8, 128), F32)
    real_sin = jnp.zeros((8, 128), F32)
    results = []
    for par, (real, imag) in enumerate(inputs):
        if imag is None:
            spec = jnp.dot(real.astype(BF16), forward[par], preferred_element_type=F32)
            cos_part, sin_part = spec[:, 0:128], spec[:, 128:256]
        else:
            stacked = jnp.concatenate([real, imag], axis=0).astype(BF16)
            spec = jnp.dot(stacked, forward[par], preferred_element_type=F32)
            cos_part = spec[0:16, 0:128] + spec[16:32, 128:256]
            sin_part = spec[0:16, 128:256] - spec[16:32, 0:128]
        re = jnp.zeros((8, 128), F32)
        im = jnp.zeros((8, 128), F32)
        for fxl in range(2):
            c = cos_part[8 * fxl : 8 * fxl + 8]
            s = sin_part[8 * fxl : 8 * fxl + 8]
            if par == 0:
                ny = s[:, 0:1]
                real_cos = real_cos + ny * nyquist[16 + 16 * fxl : 24 + 16 * fxl, :]
                real_sin = real_sin + ny * nyquist[24 + 16 * fxl : 32 + 16 * fxl, :]
                s = jnp.where(lane_e == 0, 0.0, s)
            pc = phase[32 * par + 8 * fxl : 32 * par + 8 * fxl + 8, :]
            ps = phase[32 * par + 16 + 8 * fxl : 32 * par + 24 + 8 * fxl, :]
            re = re + c * pc - s * ps
            im = im - (s * pc + c * ps)
        re = both(re)
        im = both(im)
        if par == 0:
            re = jnp.where(lane_e == 0, re - total * (1.0 / SY), re)
        coef = jnp.concatenate([re, im], axis=1)
        if imag is not None:
            coef = jnp.concatenate([coef, jnp.concatenate([im, -re], axis=1)], axis=0)
        results.append(jnp.dot(coef.astype(BF16), inverse[par], preferred_element_type=F32))
    wave_cos = wave_cos + both(real_cos)[:, 0:1]
    wave_sin = wave_sin + both(real_sin)[:, 0:1]
    turn = iota((8, 512), 1) & 3
    wave = wave_cos * jnp.where(turn == 0, 1.0, jnp.where(turn == 2, -1.0, 0.0))
    wave = wave + wave_sin * jnp.where(turn == 1, 1.0, jnp.where(turn == 3, -1.0, 0.0))
    scale = 1.0 / (SX * math.sqrt(BF))
    first = results[0] + wave
    e1, f1 = results[1][0:8], results[1][8:16]
    e3, f3 = results[3][0:8], results[3][8:16]
    quarters = (
        first + results[2] + e1 + e3,
        first - results[2] - f1 + f3,
        first + results[2] - e1 - e3,
        first - results[2] + f1 - f3,
    )
    for j, quarter in enumerate(quarters):
        out[:, 512 * j : 512 * (j + 1)] = (quarter * scale)[0:4]


def permute(value, axes, pairs):
    return lax.ppermute(value, axes, pairs)


def exchange(value, axes):
    return lax.all_to_all(value, axes, split_axis=0, concat_axis=0, tiled=True)


def limit(mib):
    return pltpu.CompilerParams(vmem_limit_bytes=mib * MIB)


def local(frames, dark_frame, gain_frame, bf_index, row_level, shift_num):
    smem = pl.BlockSpec(memory_space=pltpu.SMEM)
    vmem = pl.BlockSpec(memory_space=pltpu.VMEM)
    hbm = pl.BlockSpec(memory_space=pltpu.HBM)

    send, foot, keep = pl.pallas_call(
        reference_kernel,
        in_specs=[smem, smem, hbm, vmem, vmem, vmem],
        out_specs=[vmem, vmem, hbm],
        out_shape=[
            jax.ShapeDtypeStruct((N, 8, 128), BF16),
            jax.ShapeDtypeStruct((8, 128), BF16),
            jax.ShapeDtypeStruct((KEEP_ROWS, BF), F32),
        ],
        scratch_shapes=[
            pltpu.VMEM((YS, XS, BF), BF16),
            pltpu.VMEM((24, BF), F32),
            pltpu.SemaphoreType.DMA((PARTS,)),
            pltpu.SemaphoreType.DMA((2,)),
        ],
        compiler_params=limit(60),
        name="reference_image",
    )(
        row_level,
        shift_num,
        frames,
        dark_frame.reshape(ROWS, 128),
        gain_frame.reshape(ROWS, 128),
        bf_index.reshape(1, BF),
    )
    below = permute(foot, ("pair", "core"), [(i, (i - 1) % S) for i in range(S)])
    recv = exchange(send, AXES)
    mine, theirs = pl.pallas_call(
        strip_kernel,
        in_specs=[smem, vmem, vmem, hbm, hbm, vmem],
        out_specs=[vmem, vmem],
        out_shape=[jax.ShapeDtypeStruct((BF // 2, 640), BF16)] * 2,
        scratch_shapes=[
            pltpu.VMEM((BF, 256), BF16),
            pltpu.VMEM((24, BF), F32),
            pltpu.VMEM((N, 128), F32),
            pltpu.VMEM((YS, XS, BF), BF16),
            pltpu.VMEM((YS, XS, BF), BF16),
            pltpu.VMEM((32, XS, BF), BF16),
            pltpu.VMEM((BX * 16, BF), BF16),
            pltpu.VMEM((32, 16, 128), F32),
            pltpu.VMEM((32, 16, 128), F32),
            pltpu.VMEM((32, 384), F32),
            pltpu.VMEM((16, 32, 128), F32),
            pltpu.VMEM((256, YS * XS), BF16),
            pltpu.VMEM((2, BX * 16, BF), F32),
            pltpu.SemaphoreType.DMA((PARTS,)),
            pltpu.SemaphoreType.DMA,
        ],
        compiler_params=limit(50),
        name="strip",
    )(row_level, recv, below, keep, frames, jnp.asarray(row_kernel()))
    swapped = permute(theirs, "core", [(0, 1), (1, 0)])
    both = (mine.astype(F32) + swapped.astype(F32)).astype(BF16)
    parts = exchange(both.reshape(N // 2, 8, 640), ("pair", "grp"))
    tables = [jnp.asarray(t) for t in (*col_tables(), phase_tables(), nyquist_tables())]
    return pl.pallas_call(
        finish_kernel,
        in_specs=[vmem] * 5,
        out_specs=[vmem, vmem],
        out_shape=[
            jax.ShapeDtypeStruct((4, 2 * SX), F32),
            jax.ShapeDtypeStruct((8, 256), F32),
        ],
        scratch_shapes=[pltpu.VMEM((16, SX), F32)],
        compiler_params=limit(24),
        name="finish",
    )(parts, *tables)


def solution(mesh):
    scan = ("pair", "core")
    return jax.shard_map(
        local,
        mesh=Mesh(mesh.devices.reshape(S // 2, 2, G), AXES),
        in_specs=(P(scan, "grp", None), P(), P(), P(), P(scan), P(None, AXES)),
        out_specs=(P(AXES, None), P(AXES, None)),
        check_vma=False,
    )
```

```python
import math

import jax
import jax.numpy as jnp
import ml_dtypes
import numpy as np
from jax import lax
from jax.experimental import pallas as pl
from jax.experimental.pallas import tpu as pltpu
from jax.sharding import Mesh
from jax.sharding import PartitionSpec as P

SY = 256
SX = 1024
BF = 1024
DET = 36864
AXES = ("pair", "core", "grp")
S = 16
G = 8
N = S * G
YS = SY // S
XS = SX // G
ROWS = DET // 128
BX = 17
PARTS = 4
F32 = jnp.float32
BF16 = jnp.bfloat16
NT = (((1,), (1,)), ((), ()))
TN = (((0,), (0,)), ((), ()))
MIB = 1024 * 1024
YP = YS // PARTS
FOOT = 32
KEEP_ROWS = 1024


def iota(shape, dim):
    return lax.broadcasted_iota(jnp.int32, shape, dim)


def row_kernel():
    k = np.arange(-128, 128)
    q = np.arange(1024)
    d = np.cos(2 * np.pi * k[None, :] * q[:, None] / 1024).sum(1) / 256
    r = np.arange(1024)
    yp = np.where(r < 512, r, (r - 512) ^ 4)
    yy = np.repeat(np.arange(32), 4)
    fy = np.tile(np.arange(4), 32)
    return d[(2 * yp[:, None] - fy[None, :] - 4 * (yy[None, :] - 8)) % 1024].astype(ml_dtypes.bfloat16)


def col_tables():
    x = np.arange(256) - 8
    xp = np.arange(512)
    forward, inverse = [], []
    for par in range(4):
        k = 4 * np.arange(128) + par
        ang = 2 * np.pi * ((x[:, None] * k[None, :]) % 1024) / 1024
        c, s = np.cos(ang), np.sin(ang)
        if par == 0:
            s[:, 0] = np.where(x % 2 == 0, 1.0, -1.0)
        forward.append(np.concatenate([c, s], 1))
        w = np.where(k == 0, 1.0, 2.0)[:, None]
        ang = 2 * np.pi * ((k[:, None] * xp[None, :]) % 2048) / 2048
        inverse.append(np.concatenate([w * np.cos(ang), -w * np.sin(ang)], 0))
    return [np.stack(t).astype(ml_dtypes.bfloat16) for t in (forward, inverse)]


def phase_tables():
    out = np.zeros((4, 2, 2, 8, 128), np.float32)
    for par in range(4):
        k = 4 * np.arange(128) + par
        for fx in range(4):
            rows = slice(4 * (fx >> 1), 4 * (fx >> 1) + 4)
            out[par, 0, fx & 1, rows] = np.cos(2 * np.pi * k * fx / 4096)
            out[par, 1, fx & 1, rows] = np.sin(2 * np.pi * k * fx / 4096)
    return out.reshape(128, 128)


def nyquist_tables():
    w = np.zeros((2, 8, 128), np.float32)
    for i in range(8):
        for fx in range(4):
            for fy in range(4):
                sy = math.sin(math.pi * (2 * (i % 4) - fy) / 4) / 256
                for base in (64, 80):
                    w[0, i, base + fx * 4 + fy] = sy * math.sin(math.pi * fx / 4)
                    w[1, i, base + fx * 4 + fy] = -sy * math.cos(math.pi * fx / 4)
    v = np.zeros((2, 2, 8, 128), np.float32)
    for fx in range(4):
        rows = slice(4 * (fx >> 1), 4 * (fx >> 1) + 4)
        v[fx & 1, 0, rows] = math.cos(math.pi * fx / 4)
        v[fx & 1, 1, rows] = math.sin(math.pi * fx / 4)
    return np.concatenate([w.reshape(16, 128), v.reshape(32, 128)], 0)


def three_parts(value):
    high = value.astype(BF16).astype(F32)
    mid = (value - high).astype(BF16).astype(F32)
    return high, mid, value - high - mid


def reference_kernel(
    level, amounts, frames, dark, gain, index, send, foot_out, keep_out, held, keep, sems, keep_sems
):
    def stay(i):
        span = pl.ds(8 * i, 8 + 8 * i)
        return pltpu.make_async_copy(keep.at[span], keep_out.at[span], keep_sems.at[i])

    def part(i):
        span = pl.ds(i * (YS // PARTS), YS // PARTS)
        return pltpu.make_async_copy(frames.at[span], held.at[span], sems.at[i])

    for i in range(PARTS):
        part(i).start()
    g = gain[...]
    table = jnp.concatenate(
        [dark[...].astype(F32), (g >> 5).astype(F32), (g & 31).astype(F32)], axis=1
    ).astype(BF16)
    idx = index[...]
    hot = (iota((ROWS, BF), 0) == (idx >> 7)).astype(F32).astype(BF16)
    picked = lax.dot_general(table, hot, TN, preferred_element_type=F32)
    mine = iota((128, BF), 0) == (idx & 127)

    def pick(i):
        return jnp.sum(jnp.where(mine, picked[128 * i : 128 * (i + 1)], 0.0), axis=0, keepdims=True)

    dark_px = pick(0) * (1.0 / 256.0)
    gain_px = (pick(1) * 32.0 + pick(2)) * (1.0 / 4096.0)
    keep[0:1, :] = dark_px
    keep[1:2, :] = gain_px
    stay(0).start()
    offset = jnp.sum(dark_px * gain_px)
    for i in range(PARTS):
        part(i).wait()
        for y in range(i * (YS // PARTS), (i + 1) * (YS // PARTS)):
            acc = None
            for t in range(8):
                lanes = slice(128 * t, 128 * (t + 1))
                term = held[y, :, lanes].astype(F32) * gain_px[:, lanes]
                acc = term if acc is None else acc + term
            high = acc.astype(BF16)
            low = (acc - high.astype(F32)).astype(BF16)
            total = lax.dot_general(
                jnp.ones((8, 256), BF16), jnp.concatenate([high, low], 1), NT, preferred_element_type=F32
            )
            keep[8 + y : 9 + y, 0:128] = total[0:1] - level[y] * offset
    stay(1).start()
    s = lax.axis_index("pair") * 2 + lax.axis_index("core")
    g = lax.axis_index("grp")
    r = keep[8:24, 0:128]
    center = jnp.sum(r) * (1.0 / (YS * XS))
    rest = r - center
    lane = iota((8, 128), 1)
    top = iota((8, 128), 0) == 0
    foot = jnp.zeros((8, 128), F32)
    for i in range(8):
        foot = jnp.where(lane == FOOT + i, amounts[0, i].astype(F32), foot)
        foot = jnp.where(lane == FOOT + 8 + i, amounts[1, i].astype(F32), foot)
    for i, piece in enumerate(three_parts(jnp.full((8, 128), center))):
        foot = jnp.where(lane == FOOT + 16 + i, piece, foot)
    foot = jnp.where(top, foot, 0.0)
    foot_out[...] = foot.astype(BF16)
    plain = foot.astype(BF16)
    for d in range(N):
        send[d] = plain
    here = top & (lane >= FOOT) & (lane < FOOT + 24)
    first = rest[0:8]
    last = jnp.where(top, foot, rest[8:16])
    sides = jnp.where((lane >= 32) & (lane < 96), pltpu.roll(rest[8:16], 64, 1), first)
    for ds, block in ((S - 1, first), (0, sides), (1, last)):
        for dg in (G - 1, 0, 1):
            if ds or dg:
                whole = block if ds == S - 1 and dg == 0 else jnp.where(here, foot, block)
                send[lax.rem(s + ds, S) * G + lax.rem(g + dg, G)] = whole.astype(BF16)
    for i in range(2):
        stay(i).wait()


def strip_kernel(
    level, recv, below, keep_hbm, frames, rows, mine, theirs, corr, keep, feet, held, v, moved, hot, main, over, window, table, around, sums, left, sems, keep_sem
):
    s = lax.axis_index("pair") * 2 + lax.axis_index("core")
    g = lax.axis_index("grp")

    def part(i):
        return pltpu.make_async_copy(frames.at[pl.ds(i * YP, YP)], held.at[pl.ds(i * YP, YP)], sems.at[i])

    kept = pltpu.make_async_copy(keep_hbm.at[pl.ds(0, 24)], keep, keep_sem)
    kept.start()
    for i in range(PARTS):
        part(i).start()

    col = iota((128, 256), 1)
    spread = ((iota((128, 256), 0) >> 2) == (col >> 3)) & ((iota((128, 256), 0) & 3) == (col & 3))
    left[...] = jnp.dot(
        rows[...], spread.astype(F32).astype(BF16), preferred_element_type=F32
    ).astype(BF16)

    for d in range(N):
        feet[d : d + 1, :] = recv[d].astype(F32)[0:1, :]
    feet[pl.ds(lax.rem(s + 1, S) * G + g, 1), :] = below[...].astype(F32)[0:1, :]
    lane = iota((N, 128), 1)
    means = jnp.where((lane >= FOOT + 16) & (lane < FOOT + 19), feet[...], 0.0)
    mean = jnp.sum(jnp.sum(means, axis=0, keepdims=True), axis=1, keepdims=True) * (1.0 / N)
    total_row = jnp.zeros((1, 128), F32)
    for i, piece in enumerate(three_parts(mean * (SY * SX))):
        total_row = jnp.where(iota((1, 128), 1) == 96 + i, piece, total_row)
    wide = iota((128, 256), 1)
    pick = iota((128, 256), 0) == FOOT + 8 * (wide >> 7) + (wide & 7)
    shifts = jnp.dot(feet[...].astype(BF16), pick.astype(F32).astype(BF16), preferred_element_type=F32)
    shifts = jnp.where((iota((N, 256), 0) & 15) == ((wide & 127) >> 3), shifts, 0.0)
    shifts = jnp.sum(shifts.reshape(8, 16, 256), axis=1).astype(jnp.int32)
    kept.wait()

    def neighbour(ds, dg):
        src = lax.rem(s + ds, S) * G + lax.rem(g + dg, G)
        spot = iota((1, 128), 1)
        row = jnp.where((spot >= FOOT + 16) & (spot < FOOT + 19), feet[pl.ds(src, 1), :], 0.0)
        return recv[src].astype(F32) + (jnp.sum(row, axis=1, keepdims=True) - mean)

    for j, dg in enumerate((G - 1, 0, 1)):
        lanes = slice(128 * j, 128 * (j + 1))
        window[0:8, lanes] = neighbour(S - 1, dg)
        window[24:32, lanes] = neighbour(1, dg)
        if dg:
            side = neighbour(0, dg)
            window[8:16, lanes] = side
            window[16:24, lanes] = pltpu.roll(side, 64, 1)
        else:
            window[8:24, lanes] = keep[8:24, 0:128] - mean
    for b in range(16):
        table[b] = pltpu.roll(window[...], (b - 8) % 384, 1)[:, 128:256]

    row = iota((BX * 16, 128), 0)
    for t in range(8):
        sy = shifts[t : t + 1, 0:128]
        sx = shifts[t : t + 1, 128:256]
        code = ((sx >> 2) + 8) * 16 + (sx & 3) * 4 + (sy & 3)
        hot[:, 128 * t : 128 * (t + 1)] = (row == code).astype(F32).astype(BF16)

    for y in range(YS):
        for b in range(16):
            around[16 * b : 16 * (b + 1), 128 * y : 128 * (y + 1)] = table[b, y + 1 : y + 17, :].astype(BF16)
    for i in range(PARTS):
        part(i).wait()
        for y in range(i * YP, (i + 1) * YP):
            value = (held[y].astype(F32) - level[y] * keep[0:1, :]) * keep[1:2, :]
            v[y] = value.astype(BF16)
    corr[...] = lax.dot_general(
        v[...].reshape(YS * XS, BF), around[...], (((0,), (1,)), ((), ())), preferred_element_type=F32
    ).astype(BF16)
    core = lax.axis_index("core")
    for a in range(S // 2):
        for to, c in ((mine, core), (theirs, 1 - core)):
            to[64 * a : 64 * (a + 1), 384:640] = corr[pl.ds(pl.multiple_of(64 * (2 * a + c), 64), 64), :]

    for t in range(8):
        lanes = slice(128 * t, 128 * (t + 1))
        by = (shifts[t : t + 1, 0:128] >> 2) + 8
        masks = [
            jnp.broadcast_to(((by >> b) & 1).astype(F32), (16, 128)).astype(BF16) > 0.5 for b in range(5)
        ]

        zero = jnp.zeros((16, 128), BF16)
        for x0 in range(0, XS, 16):
            rows_in = [v[y, x0 : x0 + 16, lanes] for y in range(YS)]
            for b in range(5):
                step = 1 << b
                size = min(len(rows_in) + step, 32)
                old = rows_in
                rows_in = [
                    jnp.where(
                        masks[b],
                        old[j - step] if 0 <= j - step < len(old) else zero,
                        old[j] if j < len(old) else zero,
                    )
                    for j in range(size)
                ]
            for j in range(32):
                moved[j, x0 : x0 + 16, lanes] = rows_in[j]

    lane = iota((16, 128), 1)

    for j in range(4):
        block = moved[8 * j : 8 * j + 8].reshape(8 * XS, BF)
        sums[j & 1] = lax.dot_general(hot[...], block, NT, preferred_element_type=F32)
        for h in range(8):
            lanes = slice(128 * h, 128 * (h + 1))
            acc_main = sums[j & 1, 0:16, lanes]
            acc_over = jnp.zeros((16, 128), F32)
            for b in range(1, BX):
                piece = pltpu.roll(sums[j & 1, 16 * b : 16 * (b + 1), lanes], b, 1)
                acc_main = acc_main + piece
                acc_over = acc_over + jnp.where(lane < b, piece, 0.0)
            main[8 * j + h] = acc_main - acc_over
            over[8 * j + h] = acc_over

    sign_y = 1.0 - 2.0 * (iota((32, 16, 128), 0) & 1).astype(F32)
    sign_x = 1.0 - 2.0 * (iota((8, 128), 1) & 1).astype(F32)
    folded = jnp.sum((main[...] + over[...]) * sign_y, axis=0)
    folded = jnp.concatenate([jnp.zeros((64, 128), F32), folded, jnp.zeros((48, 128), F32)], axis=0)
    q_row = lax.dot_general(sign_x, folded, NT, precision=lax.Precision.HIGHEST, preferred_element_type=F32)[0:1]
    q_high = q_row.astype(BF16).astype(F32)
    q_row = q_high + pltpu.roll(q_row - q_high, 16, 1)

    kind = (iota((256, 128), 0) >> 2) & 1
    z = []
    for h in range(2):
        u_main = main[:, 8 * h : 8 * h + 8, :].reshape(256, 128)
        u_over = over[:, 8 * h : 8 * h + 8, :].reshape(256, 128)
        right = jnp.concatenate(
            [
                jnp.where(kind == 0, u_main, 0.0),
                jnp.where(kind == 1, u_main, 0.0),
                jnp.where(kind == 0, u_over, 0.0) + pltpu.roll(jnp.where(kind == 1, u_over, 0.0), 16, 1),
            ],
            axis=1,
        ).astype(BF16)
        z.append(jnp.dot(left[512 * h : 512 * (h + 1), :], right, preferred_element_type=F32))
    extra = jnp.concatenate([jnp.zeros((1, 256), F32), q_row + total_row], axis=1)
    lower = iota((8, 384), 0) < 4
    for b in range(S):
        pieces = []
        for j in range(4 * b, 4 * b + 4):
            z0 = z[0][8 * j : 8 * j + 8]
            z1 = z[1][8 * j : 8 * j + 8]
            pieces += [jnp.where(lower, z0, z1) + extra, jnp.where(lower, z1, z0) + extra]
        place = pl.multiple_of(64 * (lax.rem(s + b, S) >> 1), 64)
        to = theirs if b & 1 else mine
        to[pl.ds(place, 64), 0:384] = jnp.concatenate(pieces, axis=0).astype(BF16)


def finish_kernel(recv, forward, inverse, phase, nyquist, out, corr_out, full):
    swap = (jnp.zeros((8, 384), jnp.int32) + lax.axis_index("grp")) & 1 == 1
    corr = jnp.zeros((8, 256), F32)
    sums = []
    for g in range(G):
        acc = jnp.zeros((8, 384), F32)
        for a in range(S // 2):
            got = recv[a * G + g].astype(F32)
            acc = acc + got[:, 0:384]
            corr = corr + got[:, 384:640]
        sums.append(jnp.where(swap, pltpu.roll(acc, 4, 0), acc))
    n = iota((256, 256), 0)
    m = iota((256, 256), 1)
    order = ((n >> 4) == (m & 15)) & ((15 - (n & 15)) == (m >> 4))
    corr_out[...] = jnp.dot(
        corr * (1.0 / math.sqrt(BF * SY * SX)),
        order.astype(F32),
        precision=lax.Precision.HIGHEST,
        preferred_element_type=F32,
    )
    lane = iota((8, 128), 1)
    foot = recv[0].astype(F32)[:, 256:384]
    total = jnp.sum(jnp.where((lane >= 96) & (lane < 99), foot, 0.0), axis=1, keepdims=True) * 0.5
    q_rows = jnp.zeros((8, 128), F32)
    for g in range(G):
        tail = sums[(g - 1) % G][:, 256:384]
        q_rows = q_rows + tail
        lanes = slice(128 * g, 128 * (g + 1))
        full[0:8, lanes] = sums[g][:, 0:128] + jnp.where(lane < 16, tail, 0.0)
        full[8:16, lanes] = sums[g][:, 128:256] + jnp.where(lane < 16, pltpu.roll(tail, 112, 1), 0.0)
    z0, z1, z2, z3 = (full[:, 256 * j : 256 * (j + 1)] for j in range(4))
    inputs = (
        (z0 + z1 + z2 + z3, None),
        (z0 - z2, z3 - z1),
        (z0 - z1 + z2 - z3, None),
        (z0 - z2, z1 - z3),
    )
    lane_e = iota((8, 128), 1)
    wave_cos = jnp.sum(q_rows * nyquist[0:8, :], axis=1, keepdims=True)
    wave_sin = jnp.sum(q_rows * nyquist[8:16, :], axis=1, keepdims=True)

    def both(value):
        return value + pltpu.roll(value, 4, 0)

    real_cos = jnp.zeros((8, 128), F32)
    real_sin = jnp.zeros((8, 128), F32)
    results = []
    for par, (real, imag) in enumerate(inputs):
        if imag is None:
            spec = jnp.dot(real.astype(BF16), forward[par], preferred_element_type=F32)
            cos_part, sin_part = spec[:, 0:128], spec[:, 128:256]
        else:
            stacked = jnp.concatenate([real, imag], axis=0).astype(BF16)
            spec = jnp.dot(stacked, forward[par], preferred_element_type=F32)
            cos_part = spec[0:16, 0:128] + spec[16:32, 128:256]
            sin_part = spec[0:16, 128:256] - spec[16:32, 0:128]
        re = jnp.zeros((8, 128), F32)
        im = jnp.zeros((8, 128), F32)
        for fxl in range(2):
            c = cos_part[8 * fxl : 8 * fxl + 8]
            s = sin_part[8 * fxl : 8 * fxl + 8]
            if par == 0:
                ny = s[:, 0:1]
                real_cos = real_cos + ny * nyquist[16 + 16 * fxl : 24 + 16 * fxl, :]
                real_sin = real_sin + ny * nyquist[24 + 16 * fxl : 32 + 16 * fxl, :]
                s = jnp.where(lane_e == 0, 0.0, s)
            pc = phase[32 * par + 8 * fxl : 32 * par + 8 * fxl + 8, :]
            ps = phase[32 * par + 16 + 8 * fxl : 32 * par + 24 + 8 * fxl, :]
            re = re + c * pc - s * ps
            im = im - (s * pc + c * ps)
        re = both(re)
        im = both(im)
        if par == 0:
            re = jnp.where(lane_e == 0, re - total * (1.0 / SY), re)
        coef = jnp.concatenate([re, im], axis=1)
        if imag is not None:
            coef = jnp.concatenate([coef, jnp.concatenate([im, -re], axis=1)], axis=0)
        results.append(jnp.dot(coef.astype(BF16), inverse[par], preferred_element_type=F32))
    wave_cos = wave_cos + both(real_cos)[:, 0:1]
    wave_sin = wave_sin + both(real_sin)[:, 0:1]
    turn = iota((8, 512), 1) & 3
    wave = wave_cos * jnp.where(turn == 0, 1.0, jnp.where(turn == 2, -1.0, 0.0))
    wave = wave + wave_sin * jnp.where(turn == 1, 1.0, jnp.where(turn == 3, -1.0, 0.0))
    scale = 1.0 / (SX * math.sqrt(BF))
    first = results[0] + wave
    e1, f1 = results[1][0:8], results[1][8:16]
    e3, f3 = results[3][0:8], results[3][8:16]
    quarters = (
        first + results[2] + e1 + e3,
        first - results[2] - f1 + f3,
        first + results[2] - e1 - e3,
        first - results[2] + f1 - f3,
    )
    for j, quarter in enumerate(quarters):
        out[:, 512 * j : 512 * (j + 1)] = (quarter * scale)[0:4]


def permute(value, axes, pairs):
    return lax.ppermute(value, axes, pairs)


def exchange(value, axes):
    return lax.all_to_all(value, axes, split_axis=0, concat_axis=0, tiled=True)


def limit(mib):
    return pltpu.CompilerParams(vmem_limit_bytes=mib * MIB)


def local(frames, dark_frame, gain_frame, bf_index, row_level, shift_num):
    smem = pl.BlockSpec(memory_space=pltpu.SMEM)
    vmem = pl.BlockSpec(memory_space=pltpu.VMEM)
    hbm = pl.BlockSpec(memory_space=pltpu.HBM)

    send, foot, keep = pl.pallas_call(
        reference_kernel,
        in_specs=[smem, smem, hbm, vmem, vmem, vmem],
        out_specs=[vmem, vmem, hbm],
        out_shape=[
            jax.ShapeDtypeStruct((N, 8, 128), BF16),
            jax.ShapeDtypeStruct((8, 128), BF16),
            jax.ShapeDtypeStruct((KEEP_ROWS, BF), F32),
        ],
        scratch_shapes=[
            pltpu.VMEM((YS, XS, BF), BF16),
            pltpu.VMEM((24, BF), F32),
            pltpu.SemaphoreType.DMA((PARTS,)),
            pltpu.SemaphoreType.DMA((2,)),
        ],
        compiler_params=limit(60),
        name="reference_image",
    )(
        row_level,
        shift_num,
        frames,
        dark_frame.reshape(ROWS, 128),
        gain_frame.reshape(ROWS, 128),
        bf_index.reshape(1, BF),
    )
    below = permute(foot, ("pair", "core"), [(i, (i - 1) % S) for i in range(S)])
    recv = exchange(send, AXES)
    mine, theirs = pl.pallas_call(
        strip_kernel,
        in_specs=[smem, vmem, vmem, hbm, hbm, vmem],
        out_specs=[vmem, vmem],
        out_shape=[jax.ShapeDtypeStruct((BF // 2, 640), BF16)] * 2,
        scratch_shapes=[
            pltpu.VMEM((BF, 256), BF16),
            pltpu.VMEM((24, BF), F32),
            pltpu.VMEM((N, 128), F32),
            pltpu.VMEM((YS, XS, BF), BF16),
            pltpu.VMEM((YS, XS, BF), BF16),
            pltpu.VMEM((32, XS, BF), BF16),
            pltpu.VMEM((BX * 16, BF), BF16),
            pltpu.VMEM((32, 16, 128), F32),
            pltpu.VMEM((32, 16, 128), F32),
            pltpu.VMEM((32, 384), F32),
            pltpu.VMEM((16, 32, 128), F32),
            pltpu.VMEM((256, YS * XS), BF16),
            pltpu.VMEM((2, BX * 16, BF), F32),
            pltpu.VMEM((BF, 256), BF16),
            pltpu.SemaphoreType.DMA((PARTS,)),
            pltpu.SemaphoreType.DMA,
        ],
        compiler_params=limit(50),
        name="strip",
    )(row_level, recv, below, keep, frames, jnp.asarray(row_kernel()))
    swapped = permute(theirs, "core", [(0, 1), (1, 0)])
    both = (mine.astype(F32) + swapped.astype(F32)).astype(BF16)
    parts = exchange(both.reshape(N // 2, 8, 640), ("pair", "grp"))
    tables = [jnp.asarray(t) for t in (*col_tables(), phase_tables(), nyquist_tables())]
    return pl.pallas_call(
        finish_kernel,
        in_specs=[vmem] * 5,
        out_specs=[vmem, vmem],
        out_shape=[
            jax.ShapeDtypeStruct((4, 2 * SX), F32),
            jax.ShapeDtypeStruct((8, 256), F32),
        ],
        scratch_shapes=[pltpu.VMEM((16, SX), F32)],
        compiler_params=limit(24),
        name="finish",
    )(parts, *tables)


def solution(mesh):
    scan = ("pair", "core")
    return jax.shard_map(
        local,
        mesh=Mesh(mesh.devices.reshape(S // 2, 2, G), AXES),
        in_specs=(P(scan, "grp", None), P(), P(), P(), P(scan), P(None, AXES)),
        out_specs=(P(AXES, None), P(AXES, None)),
        check_vma=False,
    )
```

```python
import math

import jax
import jax.numpy as jnp
import ml_dtypes
import numpy as np
from jax import lax
from jax.experimental import pallas as pl
from jax.experimental.pallas import tpu as pltpu
from jax.sharding import Mesh
from jax.sharding import PartitionSpec as P

SY = 256
SX = 1024
BF = 1024
DET = 36864
AXES = ("pair", "core", "grp")
S = 16
G = 8
N = S * G
YS = SY // S
XS = SX // G
ROWS = DET // 128
BX = 17
PARTS = 4
F32 = jnp.float32
BF16 = jnp.bfloat16
NT = (((1,), (1,)), ((), ()))
TN = (((0,), (0,)), ((), ()))
MIB = 1024 * 1024
YP = YS // PARTS
FOOT = 32
KEEP_ROWS = 1024


def iota(shape, dim):
    return lax.broadcasted_iota(jnp.int32, shape, dim)


def row_kernel():
    k = np.arange(-128, 128)
    q = np.arange(1024)
    d = np.cos(2 * np.pi * k[None, :] * q[:, None] / 1024).sum(1) / 256
    r = np.arange(1024)
    yp = np.where(r < 512, r, (r - 512) ^ 4)
    yy = np.repeat(np.arange(32), 4)
    fy = np.tile(np.arange(4), 32)
    return d[(2 * yp[:, None] - fy[None, :] - 4 * (yy[None, :] - 8)) % 1024].astype(ml_dtypes.bfloat16)


def col_tables():
    x = np.arange(256) - 8
    xp = np.arange(512)
    forward, inverse = [], []
    for par in range(4):
        k = 4 * np.arange(128) + par
        ang = 2 * np.pi * ((x[:, None] * k[None, :]) % 1024) / 1024
        c, s = np.cos(ang), np.sin(ang)
        if par == 0:
            s[:, 0] = np.where(x % 2 == 0, 1.0, -1.0)
        forward.append(np.concatenate([c, s], 1))
        w = np.where(k == 0, 1.0, 2.0)[:, None]
        ang = 2 * np.pi * ((k[:, None] * xp[None, :]) % 2048) / 2048
        inverse.append(np.concatenate([w * np.cos(ang), -w * np.sin(ang)], 0))
    return [np.stack(t).astype(ml_dtypes.bfloat16) for t in (forward, inverse)]


def phase_tables():
    out = np.zeros((4, 2, 2, 8, 128), np.float32)
    for par in range(4):
        k = 4 * np.arange(128) + par
        for fx in range(4):
            rows = slice(4 * (fx >> 1), 4 * (fx >> 1) + 4)
            out[par, 0, fx & 1, rows] = np.cos(2 * np.pi * k * fx / 4096)
            out[par, 1, fx & 1, rows] = np.sin(2 * np.pi * k * fx / 4096)
    return out.reshape(128, 128)


def nyquist_tables():
    w = np.zeros((2, 8, 128), np.float32)
    for i in range(8):
        for fx in range(4):
            for fy in range(4):
                sy = math.sin(math.pi * (2 * (i % 4) - fy) / 4) / 256
                for base in (64, 80):
                    w[0, i, base + fx * 4 + fy] = sy * math.sin(math.pi * fx / 4)
                    w[1, i, base + fx * 4 + fy] = -sy * math.cos(math.pi * fx / 4)
    v = np.zeros((2, 2, 8, 128), np.float32)
    for fx in range(4):
        rows = slice(4 * (fx >> 1), 4 * (fx >> 1) + 4)
        v[fx & 1, 0, rows] = math.cos(math.pi * fx / 4)
        v[fx & 1, 1, rows] = math.sin(math.pi * fx / 4)
    return np.concatenate([w.reshape(16, 128), v.reshape(32, 128)], 0)


def three_parts(value):
    high = value.astype(BF16).astype(F32)
    mid = (value - high).astype(BF16).astype(F32)
    return high, mid, value - high - mid


def reference_kernel(
    level, amounts, frames, dark, gain, index, send, foot_out, keep_out, held, keep, sems, keep_sems
):
    def stay(i):
        span = pl.ds(8 * i, 8 + 8 * i)
        return pltpu.make_async_copy(keep.at[span], keep_out.at[span], keep_sems.at[i])

    def part(i):
        span = pl.ds(i * (YS // PARTS), YS // PARTS)
        return pltpu.make_async_copy(frames.at[span], held.at[span], sems.at[i])

    for i in range(PARTS):
        part(i).start()
    g = gain[...]
    table = jnp.concatenate(
        [dark[...].astype(F32), (g >> 5).astype(F32), (g & 31).astype(F32)], axis=1
    ).astype(BF16)
    idx = index[...]
    hot = (iota((ROWS, BF), 0) == (idx >> 7)).astype(F32).astype(BF16)
    picked = lax.dot_general(table, hot, TN, preferred_element_type=F32)
    mine = iota((128, BF), 0) == (idx & 127)

    def pick(i):
        return jnp.sum(jnp.where(mine, picked[128 * i : 128 * (i + 1)], 0.0), axis=0, keepdims=True)

    dark_px = pick(0) * (1.0 / 256.0)
    gain_px = (pick(1) * 32.0 + pick(2)) * (1.0 / 4096.0)
    keep[0:1, :] = dark_px
    keep[1:2, :] = gain_px
    stay(0).start()
    offset = jnp.sum(dark_px * gain_px)
    for i in range(PARTS):
        part(i).wait()
        for y in range(i * (YS // PARTS), (i + 1) * (YS // PARTS)):
            acc = None
            for t in range(8):
                lanes = slice(128 * t, 128 * (t + 1))
                term = held[y, :, lanes].astype(F32) * gain_px[:, lanes]
                acc = term if acc is None else acc + term
            high = acc.astype(BF16)
            low = (acc - high.astype(F32)).astype(BF16)
            total = lax.dot_general(
                jnp.ones((8, 256), BF16), jnp.concatenate([high, low], 1), NT, preferred_element_type=F32
            )
            keep[8 + y : 9 + y, 0:128] = total[0:1] - level[y] * offset
    stay(1).start()
    s = lax.axis_index("pair") * 2 + lax.axis_index("core")
    g = lax.axis_index("grp")
    r = keep[8:24, 0:128]
    center = jnp.sum(r) * (1.0 / (YS * XS))
    rest = r - center
    lane = iota((8, 128), 1)
    top = iota((8, 128), 0) == 0
    foot = jnp.zeros((8, 128), F32)
    for i in range(8):
        foot = jnp.where(lane == FOOT + i, amounts[0, i].astype(F32), foot)
        foot = jnp.where(lane == FOOT + 8 + i, amounts[1, i].astype(F32), foot)
    for i, piece in enumerate(three_parts(jnp.full((8, 128), center))):
        foot = jnp.where(lane == FOOT + 16 + i, piece, foot)
    foot = jnp.where(top, foot, 0.0)
    foot_out[...] = foot.astype(BF16)
    plain = foot.astype(BF16)
    for d in range(N):
        send[d] = plain
    here = top & (lane >= FOOT) & (lane < FOOT + 24)
    first = rest[0:8]
    last = jnp.where(top, foot, rest[8:16])
    sides = jnp.where((lane >= 32) & (lane < 96), pltpu.roll(rest[8:16], 64, 1), first)
    for ds, block in ((S - 1, first), (0, sides), (1, last)):
        for dg in (G - 1, 0, 1):
            if ds or dg:
                whole = block if ds == S - 1 and dg == 0 else jnp.where(here, foot, block)
                send[lax.rem(s + ds, S) * G + lax.rem(g + dg, G)] = whole.astype(BF16)
    for i in range(2):
        stay(i).wait()


def early_kernel(level, keep_hbm, frames, v_out, held, keep, sems):
    copies = [
        pltpu.make_async_copy(keep_hbm.at[pl.ds(0, 8)], keep, sems.at[2]),
        pltpu.make_async_copy(frames.at[pl.ds(0, 4)], held.at[pl.ds(0, 4)], sems.at[0]),
        pltpu.make_async_copy(frames.at[pl.ds(4, 4)], held.at[pl.ds(4, 4)], sems.at[1]),
    ]
    for copy in copies:
        copy.start()
    copies[0].wait()
    for i in range(2):
        copies[1 + i].wait()
        for y in range(4 * i, 4 * i + 4):
            value = (held[y].astype(F32) - level[y] * keep[0:1, :]) * keep[1:2, :]
            v_out[y] = value.astype(BF16)


def strip_kernel(
    level, recv, below, keep_hbm, frames, early, rows, mine, theirs, corr, keep, feet, held, v, moved, hot, main, over, window, table, around, sums, left, sems, keep_sem
):
    s = lax.axis_index("pair") * 2 + lax.axis_index("core")
    g = lax.axis_index("grp")

    def part(i):
        return pltpu.make_async_copy(frames.at[pl.ds(8 + 4 * i, 4)], held.at[pl.ds(4 * i, 4)], sems.at[i])

    kept = pltpu.make_async_copy(keep_hbm.at[pl.ds(0, 24)], keep, keep_sem)
    kept.start()
    for i in range(2):
        part(i).start()

    col = iota((128, 256), 1)
    spread = ((iota((128, 256), 0) >> 2) == (col >> 3)) & ((iota((128, 256), 0) & 3) == (col & 3))
    left[...] = jnp.dot(
        rows[...], spread.astype(F32).astype(BF16), preferred_element_type=F32
    ).astype(BF16)

    for d in range(N):
        feet[d : d + 1, :] = recv[d].astype(F32)[0:1, :]
    feet[pl.ds(lax.rem(s + 1, S) * G + g, 1), :] = below[...].astype(F32)[0:1, :]
    lane = iota((N, 128), 1)
    means = jnp.where((lane >= FOOT + 16) & (lane < FOOT + 19), feet[...], 0.0)
    mean = jnp.sum(jnp.sum(means, axis=0, keepdims=True), axis=1, keepdims=True) * (1.0 / N)
    total_row = jnp.zeros((1, 128), F32)
    for i, piece in enumerate(three_parts(mean * (SY * SX))):
        total_row = jnp.where(iota((1, 128), 1) == 96 + i, piece, total_row)
    wide = iota((128, 256), 1)
    pick = iota((128, 256), 0) == FOOT + 8 * (wide >> 7) + (wide & 7)
    shifts = jnp.dot(feet[...].astype(BF16), pick.astype(F32).astype(BF16), preferred_element_type=F32)
    shifts = jnp.where((iota((N, 256), 0) & 15) == ((wide & 127) >> 3), shifts, 0.0)
    shifts = jnp.sum(shifts.reshape(8, 16, 256), axis=1).astype(jnp.int32)
    kept.wait()

    def neighbour(ds, dg):
        src = lax.rem(s + ds, S) * G + lax.rem(g + dg, G)
        spot = iota((1, 128), 1)
        row = jnp.where((spot >= FOOT + 16) & (spot < FOOT + 19), feet[pl.ds(src, 1), :], 0.0)
        return recv[src].astype(F32) + (jnp.sum(row, axis=1, keepdims=True) - mean)

    for j, dg in enumerate((G - 1, 0, 1)):
        lanes = slice(128 * j, 128 * (j + 1))
        window[0:8, lanes] = neighbour(S - 1, dg)
        window[24:32, lanes] = neighbour(1, dg)
        if dg:
            side = neighbour(0, dg)
            window[8:16, lanes] = side
            window[16:24, lanes] = pltpu.roll(side, 64, 1)
        else:
            window[8:24, lanes] = keep[8:24, 0:128] - mean
    for b in range(16):
        table[b] = pltpu.roll(window[...], (b - 8) % 384, 1)[:, 128:256]

    row = iota((BX * 16, 128), 0)
    for t in range(8):
        sy = shifts[t : t + 1, 0:128]
        sx = shifts[t : t + 1, 128:256]
        code = ((sx >> 2) + 8) * 16 + (sx & 3) * 4 + (sy & 3)
        hot[:, 128 * t : 128 * (t + 1)] = (row == code).astype(F32).astype(BF16)

    for y in range(YS):
        for b in range(16):
            around[16 * b : 16 * (b + 1), 128 * y : 128 * (y + 1)] = table[b, y + 1 : y + 17, :].astype(BF16)
    for i in range(2):
        part(i).wait()
        for y in range(4 * i, 4 * i + 4):
            value = (held[y].astype(F32) - level[8 + y] * keep[0:1, :]) * keep[1:2, :]
            v[y] = value.astype(BF16)
    half = YS * XS // 2
    corr[...] = (
        lax.dot_general(
            early[...].reshape(half, BF), around[:, 0:half], (((0,), (1,)), ((), ())), preferred_element_type=F32
        )
        + lax.dot_general(
            v[...].reshape(half, BF), around[:, half:], (((0,), (1,)), ((), ())), preferred_element_type=F32
        )
    ).astype(BF16)
    core = lax.axis_index("core")
    for a in range(S // 2):
        for to, c in ((mine, core), (theirs, 1 - core)):
            to[64 * a : 64 * (a + 1), 384:640] = corr[pl.ds(pl.multiple_of(64 * (2 * a + c), 64), 64), :]

    for t in range(8):
        lanes = slice(128 * t, 128 * (t + 1))
        by = (shifts[t : t + 1, 0:128] >> 2) + 8
        masks = [
            jnp.broadcast_to(((by >> b) & 1).astype(F32), (16, 128)).astype(BF16) > 0.5 for b in range(5)
        ]

        zero = jnp.zeros((16, 128), BF16)
        for x0 in range(0, XS, 16):
            rows_in = [early[y, x0 : x0 + 16, lanes] for y in range(8)]
            rows_in += [v[y, x0 : x0 + 16, lanes] for y in range(8)]
            for b in range(5):
                step = 1 << b
                size = min(len(rows_in) + step, 32)
                old = rows_in
                rows_in = [
                    jnp.where(
                        masks[b],
                        old[j - step] if 0 <= j - step < len(old) else zero,
                        old[j] if j < len(old) else zero,
                    )
                    for j in range(size)
                ]
            for j in range(32):
                moved[j, x0 : x0 + 16, lanes] = rows_in[j]

    lane = iota((16, 128), 1)

    for j in range(4):
        block = moved[8 * j : 8 * j + 8].reshape(8 * XS, BF)
        sums[j & 1] = lax.dot_general(hot[...], block, NT, preferred_element_type=F32)
        for h in range(8):
            lanes = slice(128 * h, 128 * (h + 1))
            acc_main = sums[j & 1, 0:16, lanes]
            acc_over = jnp.zeros((16, 128), F32)
            for b in range(1, BX):
                piece = pltpu.roll(sums[j & 1, 16 * b : 16 * (b + 1), lanes], b, 1)
                acc_main = acc_main + piece
                acc_over = acc_over + jnp.where(lane < b, piece, 0.0)
            main[8 * j + h] = acc_main - acc_over
            over[8 * j + h] = acc_over

    sign_y = 1.0 - 2.0 * (iota((32, 16, 128), 0) & 1).astype(F32)
    sign_x = 1.0 - 2.0 * (iota((8, 128), 1) & 1).astype(F32)
    folded = jnp.sum((main[...] + over[...]) * sign_y, axis=0)
    folded = jnp.concatenate([jnp.zeros((64, 128), F32), folded, jnp.zeros((48, 128), F32)], axis=0)
    q_row = lax.dot_general(sign_x, folded, NT, precision=lax.Precision.HIGHEST, preferred_element_type=F32)[0:1]
    q_high = q_row.astype(BF16).astype(F32)
    q_row = q_high + pltpu.roll(q_row - q_high, 16, 1)

    kind = (iota((256, 128), 0) >> 2) & 1
    z = []
    for h in range(2):
        u_main = main[:, 8 * h : 8 * h + 8, :].reshape(256, 128)
        u_over = over[:, 8 * h : 8 * h + 8, :].reshape(256, 128)
        right = jnp.concatenate(
            [
                jnp.where(kind == 0, u_main, 0.0),
                jnp.where(kind == 1, u_main, 0.0),
                jnp.where(kind == 0, u_over, 0.0) + pltpu.roll(jnp.where(kind == 1, u_over, 0.0), 16, 1),
            ],
            axis=1,
        ).astype(BF16)
        z.append(jnp.dot(left[512 * h : 512 * (h + 1), :], right, preferred_element_type=F32))
    extra = jnp.concatenate([jnp.zeros((1, 256), F32), q_row + total_row], axis=1)
    lower = iota((8, 384), 0) < 4
    for b in range(S):
        pieces = []
        for j in range(4 * b, 4 * b + 4):
            z0 = z[0][8 * j : 8 * j + 8]
            z1 = z[1][8 * j : 8 * j + 8]
            pieces += [jnp.where(lower, z0, z1) + extra, jnp.where(lower, z1, z0) + extra]
        place = pl.multiple_of(64 * (lax.rem(s + b, S) >> 1), 64)
        to = theirs if b & 1 else mine
        to[pl.ds(place, 64), 0:384] = jnp.concatenate(pieces, axis=0).astype(BF16)


def finish_kernel(recv, forward, inverse, phase, nyquist, out, corr_out, full):
    swap = (jnp.zeros((8, 384), jnp.int32) + lax.axis_index("grp")) & 1 == 1
    corr = jnp.zeros((8, 256), F32)
    sums = []
    for g in range(G):
        acc = jnp.zeros((8, 384), F32)
        for a in range(S // 2):
            got = recv[a * G + g].astype(F32)
            acc = acc + got[:, 0:384]
            corr = corr + got[:, 384:640]
        sums.append(jnp.where(swap, pltpu.roll(acc, 4, 0), acc))
    n = iota((256, 256), 0)
    m = iota((256, 256), 1)
    order = ((n >> 4) == (m & 15)) & ((15 - (n & 15)) == (m >> 4))
    corr_out[...] = jnp.dot(
        corr * (1.0 / math.sqrt(BF * SY * SX)),
        order.astype(F32),
        precision=lax.Precision.HIGHEST,
        preferred_element_type=F32,
    )
    lane = iota((8, 128), 1)
    foot = recv[0].astype(F32)[:, 256:384]
    total = jnp.sum(jnp.where((lane >= 96) & (lane < 99), foot, 0.0), axis=1, keepdims=True) * 0.5
    q_rows = jnp.zeros((8, 128), F32)
    for g in range(G):
        tail = sums[(g - 1) % G][:, 256:384]
        q_rows = q_rows + tail
        lanes = slice(128 * g, 128 * (g + 1))
        full[0:8, lanes] = sums[g][:, 0:128] + jnp.where(lane < 16, tail, 0.0)
        full[8:16, lanes] = sums[g][:, 128:256] + jnp.where(lane < 16, pltpu.roll(tail, 112, 1), 0.0)
    z0, z1, z2, z3 = (full[:, 256 * j : 256 * (j + 1)] for j in range(4))
    inputs = (
        (z0 + z1 + z2 + z3, None),
        (z0 - z2, z3 - z1),
        (z0 - z1 + z2 - z3, None),
        (z0 - z2, z1 - z3),
    )
    lane_e = iota((8, 128), 1)
    wave_cos = jnp.sum(q_rows * nyquist[0:8, :], axis=1, keepdims=True)
    wave_sin = jnp.sum(q_rows * nyquist[8:16, :], axis=1, keepdims=True)

    def both(value):
        return value + pltpu.roll(value, 4, 0)

    real_cos = jnp.zeros((8, 128), F32)
    real_sin = jnp.zeros((8, 128), F32)
    results = []
    for par, (real, imag) in enumerate(inputs):
        if imag is None:
            spec = jnp.dot(real.astype(BF16), forward[par], preferred_element_type=F32)
            cos_part, sin_part = spec[:, 0:128], spec[:, 128:256]
        else:
            stacked = jnp.concatenate([real, imag], axis=0).astype(BF16)
            spec = jnp.dot(stacked, forward[par], preferred_element_type=F32)
            cos_part = spec[0:16, 0:128] + spec[16:32, 128:256]
            sin_part = spec[0:16, 128:256] - spec[16:32, 0:128]
        re = jnp.zeros((8, 128), F32)
        im = jnp.zeros((8, 128), F32)
        for fxl in range(2):
            c = cos_part[8 * fxl : 8 * fxl + 8]
            s = sin_part[8 * fxl : 8 * fxl + 8]
            if par == 0:
                ny = s[:, 0:1]
                real_cos = real_cos + ny * nyquist[16 + 16 * fxl : 24 + 16 * fxl, :]
                real_sin = real_sin + ny * nyquist[24 + 16 * fxl : 32 + 16 * fxl, :]
                s = jnp.where(lane_e == 0, 0.0, s)
            pc = phase[32 * par + 8 * fxl : 32 * par + 8 * fxl + 8, :]
            ps = phase[32 * par + 16 + 8 * fxl : 32 * par + 24 + 8 * fxl, :]
            re = re + c * pc - s * ps
            im = im - (s * pc + c * ps)
        re = both(re)
        im = both(im)
        if par == 0:
            re = jnp.where(lane_e == 0, re - total * (1.0 / SY), re)
        coef = jnp.concatenate([re, im], axis=1)
        if imag is not None:
            coef = jnp.concatenate([coef, jnp.concatenate([im, -re], axis=1)], axis=0)
        results.append(jnp.dot(coef.astype(BF16), inverse[par], preferred_element_type=F32))
    wave_cos = wave_cos + both(real_cos)[:, 0:1]
    wave_sin = wave_sin + both(real_sin)[:, 0:1]
    turn = iota((8, 512), 1) & 3
    wave = wave_cos * jnp.where(turn == 0, 1.0, jnp.where(turn == 2, -1.0, 0.0))
    wave = wave + wave_sin * jnp.where(turn == 1, 1.0, jnp.where(turn == 3, -1.0, 0.0))
    scale = 1.0 / (SX * math.sqrt(BF))
    first = results[0] + wave
    e1, f1 = results[1][0:8], results[1][8:16]
    e3, f3 = results[3][0:8], results[3][8:16]
    quarters = (
        first + results[2] + e1 + e3,
        first - results[2] - f1 + f3,
        first + results[2] - e1 - e3,
        first - results[2] + f1 - f3,
    )
    for j, quarter in enumerate(quarters):
        out[:, 512 * j : 512 * (j + 1)] = (quarter * scale)[0:4]


def permute(value, axes, pairs):
    return lax.ppermute(value, axes, pairs)


def exchange(value, axes):
    return lax.all_to_all(value, axes, split_axis=0, concat_axis=0, tiled=True)


def limit(mib):
    return pltpu.CompilerParams(vmem_limit_bytes=mib * MIB)


def local(frames, dark_frame, gain_frame, bf_index, row_level, shift_num):
    smem = pl.BlockSpec(memory_space=pltpu.SMEM)
    vmem = pl.BlockSpec(memory_space=pltpu.VMEM)
    hbm = pl.BlockSpec(memory_space=pltpu.HBM)

    send, foot, keep = pl.pallas_call(
        reference_kernel,
        in_specs=[smem, smem, hbm, vmem, vmem, vmem],
        out_specs=[vmem, vmem, hbm],
        out_shape=[
            jax.ShapeDtypeStruct((N, 8, 128), BF16),
            jax.ShapeDtypeStruct((8, 128), BF16),
            jax.ShapeDtypeStruct((KEEP_ROWS, BF), F32),
        ],
        scratch_shapes=[
            pltpu.VMEM((YS, XS, BF), BF16),
            pltpu.VMEM((24, BF), F32),
            pltpu.SemaphoreType.DMA((PARTS,)),
            pltpu.SemaphoreType.DMA((2,)),
        ],
        compiler_params=limit(60),
        name="reference_image",
    )(
        row_level,
        shift_num,
        frames,
        dark_frame.reshape(ROWS, 128),
        gain_frame.reshape(ROWS, 128),
        bf_index.reshape(1, BF),
    )
    below = permute(foot, ("pair", "core"), [(i, (i - 1) % S) for i in range(S)])
    recv = exchange(send, AXES)
    early = pl.pallas_call(
        early_kernel,
        in_specs=[smem, hbm, hbm],
        out_specs=vmem,
        out_shape=jax.ShapeDtypeStruct((8, XS, BF), BF16),
        scratch_shapes=[
            pltpu.VMEM((8, XS, BF), BF16),
            pltpu.VMEM((8, BF), F32),
            pltpu.SemaphoreType.DMA((3,)),
        ],
        compiler_params=limit(50),
        cost_estimate=pl.CostEstimate(flops=4 * YS * XS * BF, bytes_accessed=2 * YS * XS * BF, transcendentals=0),
        name="early",
    )(row_level, keep, frames)
    mine, theirs = pl.pallas_call(
        strip_kernel,
        in_specs=[smem, vmem, vmem, hbm, hbm, vmem, vmem],
        out_specs=[vmem, vmem],
        out_shape=[jax.ShapeDtypeStruct((BF // 2, 640), BF16)] * 2,
        scratch_shapes=[
            pltpu.VMEM((BF, 256), BF16),
            pltpu.VMEM((24, BF), F32),
            pltpu.VMEM((N, 128), F32),
            pltpu.VMEM((8, XS, BF), BF16),
            pltpu.VMEM((8, XS, BF), BF16),
            pltpu.VMEM((32, XS, BF), BF16),
            pltpu.VMEM((BX * 16, BF), BF16),
            pltpu.VMEM((32, 16, 128), F32),
            pltpu.VMEM((32, 16, 128), F32),
            pltpu.VMEM((32, 384), F32),
            pltpu.VMEM((16, 32, 128), F32),
            pltpu.VMEM((256, YS * XS), BF16),
            pltpu.VMEM((2, BX * 16, BF), F32),
            pltpu.VMEM((BF, 256), BF16),
            pltpu.SemaphoreType.DMA((2,)),
            pltpu.SemaphoreType.DMA,
        ],
        compiler_params=limit(50),
        name="strip",
    )(row_level, recv, below, keep, frames, early, jnp.asarray(row_kernel()))
    swapped = permute(theirs, "core", [(0, 1), (1, 0)])
    both = (mine.astype(F32) + swapped.astype(F32)).astype(BF16)
    parts = exchange(both.reshape(N // 2, 8, 640), ("pair", "grp"))
    tables = [jnp.asarray(t) for t in (*col_tables(), phase_tables(), nyquist_tables())]
    return pl.pallas_call(
        finish_kernel,
        in_specs=[vmem] * 5,
        out_specs=[vmem, vmem],
        out_shape=[
            jax.ShapeDtypeStruct((4, 2 * SX), F32),
            jax.ShapeDtypeStruct((8, 256), F32),
        ],
        scratch_shapes=[pltpu.VMEM((16, SX), F32)],
        compiler_params=limit(24),
        name="finish",
    )(parts, *tables)


def solution(mesh):
    scan = ("pair", "core")
    return jax.shard_map(
        local,
        mesh=Mesh(mesh.devices.reshape(S // 2, 2, G), AXES),
        in_specs=(P(scan, "grp", None), P(), P(), P(), P(scan), P(None, AXES)),
        out_specs=(P(AXES, None), P(AXES, None)),
        check_vma=False,
    )
```
